32 devices in a mesh: grp: 2 (over x), row: 16 (over z, y, core).
Axes of the slice: x: 2, y: 2, z: 4, core: 2. Of those that a mesh axis runs over, the one named last changes fastest.
Arguments:
- features: bfloat16 [64, 128, 384], P(('grp', 'row')), parts along dimension 0, may hold values from -6 to 6
- decay_rate: float32 [4, 6, 64, 128], P(None, None, ('grp', 'row')), parts along dimension 2, may hold values from 0 to 2
- input_proj: float32 [4, 16, 64, 128], P(None, None, ('grp', 'row')), parts along dimension 2, may hold values from -1 to 1
- read_proj: float32 [4, 16, 64, 128], P(None, None, ('grp', 'row')), parts along dimension 2, may hold values from -1 to 1
- skip_gain: float32 [384], replicated, may hold values from 0.5 to 1.5
- out_weight: bfloat16 [384, 384], replicated, may hold values from -0.3125 to 0.3125
- out_cotangent: bfloat16 [64, 128, 384], P(('grp', 'row')), parts along dimension 0, may hold values from -6 to 6
Outputs:
- grad_features: bfloat16 [64, 128, 384], P(('grp', 'row')), parts along dimension 0
- grad_rate: float32 [4, 6, 64, 128], P(None, None, ('grp', 'row')), parts along dimension 2
- grad_input: float32 [4, 16, 64, 128], P(None, None, ('grp', 'row')), parts along dimension 2
- grad_read: float32 [4, 16, 64, 128], P(None, None, ('grp', 'row')), parts along dimension 2
- grad_skip: float32 [768], P('grp'), parts along dimension 0
- grad_out_weight: float32 [768, 384], P('grp'), parts along dimension 0
The draws below stay inside these ranges and needn't reach their ends.
There are 2 independent parts, one for each index of `grp`. The reference program is written for one: setup_inputs(seed, part) draws one part's arguments, and reference() takes and returns one part's arrays. A program takes and returns all parts, laid end to end along the dimension named above; an argument that names none is the same for every part. Nothing has to cross between parts.
All inputs are finite; a program needn't handle non-finite values.
Results may differ from the reference program's by a relative error of at most 0.0065.
Values may be sent and summed in bfloat16 or wider, within the bound.
No kernel may reach another device: no remote copies, remote signals or barrier semaphores. Data moves between devices by JAX's collectives and lax.ppermute only.
A program may use at most 64 MiB of HBM per device.

```python
import jax
import jax.numpy as jnp
from jax import lax

D = 384
E = 384
P_SIZE = 64
N = 16
HEAD_TOTAL = 6
NC = 128
NR = 32


def draw_decay_rate(key, part):
    split_random_keys = jax.random.split(key, 8)
    line_length = jnp.array([NC, NC, NR, NR], jnp.float32)[:, None, None, None]
    order = jax.vmap(lambda sub: jax.random.permutation(sub, HEAD_TOTAL))(jax.random.split(split_random_keys[0], 4))
    slow_count = HEAD_TOTAL // 2
    row_spread = 0.7
    slow_heads = (order < slow_count)[:, :, None, None]
    fast_rate = jax.random.uniform(split_random_keys[1], (4, HEAD_TOTAL, 1, 1), jnp.float32, 0.03, 0.08)
    slow_rate = jax.random.uniform(split_random_keys[2], (4, HEAD_TOTAL, 1, 1), jnp.float32, 0.3, 0.6) / line_length
    base_rate = jnp.where(slow_heads, slow_rate, fast_rate)
    row_factor = jnp.exp(jax.random.uniform(split_random_keys[3], (4, HEAD_TOTAL, NR, 1), jnp.float32, -row_spread, row_spread))
    cell_factor = jax.random.uniform(split_random_keys[4], (4, HEAD_TOTAL, NR, NC), jnp.float32, 0.6, 1.4)
    decay_rates = base_rate * row_factor * cell_factor
    spots_col = jax.random.randint(split_random_keys[5], (4, HEAD_TOTAL, 2), 0, NC)
    spots_row = jax.random.randint(split_random_keys[6], (4, HEAD_TOTAL, 2), 0, NR)
    chosen_column = jnp.any(jnp.arange(NC)[None, None, None, :] == spots_col[..., None], axis=2)
    chosen_row = jnp.any(jnp.arange(NR)[None, None, None, :] == spots_row[..., None], axis=2)
    group_length = jax.random.uniform(split_random_keys[7], (4, HEAD_TOTAL, 1, 1), jnp.float32, 0.25, 0.7)
    sideways_scan = (jnp.arange(4) < 2)[:, None, None, None]
    line_groups = jnp.where(sideways_scan, chosen_column[:, :, None, :], chosen_row[:, :, :, None])
    return (decay_rates + group_length * line_groups.astype(jnp.float32)).astype(jnp.float32)


def level_of(stream_key, dims, cuts, smallest, high):
    def one(axis_at, blocks):
        steps = jax.random.uniform(jax.random.fold_in(jax.random.fold_in(stream_key, 6), axis_at), (blocks,), jnp.float32, smallest / len(cuts), high / len(cuts))
        return jnp.repeat(jnp.exp(steps), dims[axis_at] // blocks).reshape((-1,) + (1,) * (len(dims) - axis_at - 1))

    loudness = one(*cuts[0])
    for cut in cuts[1:]:
        loudness = loudness * one(*cut)
    return loudness


def normal_values(rng, extent, width, most, cuts=(), held_as=jnp.bfloat16):
    drawn = width * jax.random.normal(rng, extent, jnp.float32)
    if cuts:
        drawn = drawn * level_of(rng, extent, cuts, -0.22, 0.18)
    return jnp.clip(drawn, -most, most).astype(held_as)


def setup_inputs(seed: int = 0, part: int = 0) -> dict:
    keys = jax.random.split(jax.random.key(seed), 8)
    part_keys = jax.random.split(jax.random.fold_in(keys[7], part), 8)
    features = normal_values(part_keys[0], (NR, NC, E), 1.0, 6.0, ((0, 16),))
    decay_rate = draw_decay_rate(jax.random.fold_in(jax.random.fold_in(keys[7], part), 71), part)
    input_proj = normal_values(part_keys[2], (4, N, NR, NC), 0.15, 1.0, ((2, 16),), jnp.float32)
    read_proj = normal_values(part_keys[3], (4, N, NR, NC), 0.15, 1.0, ((2, 16),), jnp.float32)
    skip_gain = jnp.clip(jax.random.uniform(keys[4], (E,), jnp.float32, 0.5, 1.5), 0.5, 1.5)
    out_weight = normal_values(keys[5], (E, D), E ** -0.5, 0.3125)
    out_cotangent = normal_values(part_keys[6], (NR, NC, D), 1.0, 6.0, ((0, 16),))
    return dict(features=features, decay_rate=decay_rate, input_proj=input_proj, read_proj=read_proj, skip_gain=skip_gain, out_weight=out_weight, out_cotangent=out_cotangent)


masked_log = -1e+30

def line_scan(decay_log, line_values, line_inputs, line_reads):
    length = decay_log.shape[-1]
    prefix = jnp.cumsum(decay_log, axis=-1)
    spread = prefix[:, :, None] - prefix[:, None, :]
    places = jnp.arange(length)
    keep_mask = places[:, None] >= places[None, :]
    kernel = jnp.exp(jnp.where(keep_mask[None], spread, masked_log))
    scores = jnp.dot(line_reads.T, line_inputs, precision=lax.Precision.HIGHEST)
    return jnp.einsum('htu,uhp->thp', kernel * scores[None], line_values, precision=lax.Precision.HIGHEST)

def all_lines(decay_log, line_values, line_inputs, line_reads, flipped):
    if flipped:
        decay_log = decay_log[..., ::-1]
        line_values = line_values[:, ::-1]
        line_inputs = line_inputs[..., ::-1]
        line_reads = line_reads[..., ::-1]

    def single_line(packed):
        return line_scan(packed[0], packed[1], packed[2], packed[3])
    result = lax.map(jax.checkpoint(single_line), (decay_log, line_values, line_inputs, line_reads))
    if flipped:
        result = result[:, ::-1]
    return result

def block_core(feat_f32, decay_rate, input_proj, read_proj, skip_gain):
    across = skip_gain * feat_f32
    row_values = feat_f32.reshape(NR, NC, HEAD_TOTAL, P_SIZE)
    for direction in (0, 1):
        decay_log = -decay_rate[direction].transpose(1, 0, 2)
        line_inputs = input_proj[direction].transpose(1, 0, 2)
        line_reads = read_proj[direction].transpose(1, 0, 2)
        result = all_lines(decay_log, row_values, line_inputs, line_reads, direction == 1)
        across = across + result.reshape(NR, NC, E)
    col_values = feat_f32.transpose(1, 0, 2).reshape(NC, NR, HEAD_TOTAL, P_SIZE)
    down = jnp.zeros((NR, NC, E), jnp.float32)
    for direction in (2, 3):
        decay_log = -decay_rate[direction].transpose(2, 0, 1)
        line_inputs = input_proj[direction].transpose(2, 0, 1)
        line_reads = read_proj[direction].transpose(2, 0, 1)
        result = all_lines(decay_log, col_values, line_inputs, line_reads, direction == 3)
        down = down + result.reshape(NC, NR, E).transpose(1, 0, 2)
    return (across, down)

def reference(features, decay_rate, input_proj, read_proj, skip_gain, out_weight, out_cotangent):
    feat_f32 = features.astype(jnp.float32)
    outputs, pullback = jax.vjp(block_core, feat_f32, decay_rate, input_proj, read_proj, skip_gain)
    across_round = outputs[0].astype(jnp.bfloat16).reshape(NR * NC, E)
    down_round = outputs[1].astype(jnp.bfloat16).reshape(NR * NC, E)
    flat_cot = out_cotangent.reshape(NR * NC, D)
    grad_out_weight = jnp.dot(across_round.T, flat_cot, preferred_element_type=jnp.float32) + jnp.dot(down_round.T, flat_cot, preferred_element_type=jnp.float32)
    grad_y = jnp.dot(flat_cot, out_weight.T, preferred_element_type=jnp.float32).astype(jnp.bfloat16)
    grad_y = grad_y.reshape(NR, NC, E).astype(jnp.float32)
    grad_x_full, grad_rate, grad_input, grad_read, grad_skip = pullback((grad_y, grad_y))
    return (grad_x_full.astype(jnp.bfloat16), grad_rate, grad_input, grad_read, grad_skip, grad_out_weight)
```

```python
import functools

import jax
import jax.numpy as jnp
from jax import lax
from jax.experimental import pallas as pl
from jax.experimental.pallas import tpu as pltpu
from jax.sharding import PartitionSpec as P

F32 = jnp.float32
BF16 = jnp.bfloat16
HI = lax.Precision.HIGHEST
LANES = 128
FAR = -1e30


def iota(shape, dim):
    return lax.broadcasted_iota(jnp.int32, shape, dim)


def nt(a, b):
    return lax.dot_general(a, b, (((1,), (1,)), ((), ())), preferred_element_type=F32)


def nn(a, b):
    return jnp.dot(a, b, preferred_element_type=F32)


def tn(a, b):
    return lax.dot_general(a, b, (((0,), (0,)), ((), ())), preferred_element_type=F32)


def split_index(index, sizes):
    parts = []
    for size in reversed(sizes):
        if size & (size - 1) == 0:
            parts.append(index & (size - 1))
            index = index >> (size.bit_length() - 1)
        else:
            parts.append(lax.rem(index, size))
            index = lax.div(index, size)
    return parts[::-1]


def one_hot_rows(count, source_of):
    wanted = source_of(iota((count, 1), 0))
    return (wanted == iota((count, count), 1)).astype(F32).astype(BF16)


class Slots:
    def __init__(self, heads, states):
        self.heads = heads
        self.states = states
        self.inputs = (0, states)
        self.reads = (2 * states, 3 * states)
        pad = -(-heads // 8) * 8
        self.pad = pad
        self.rates = (4 * states, 4 * states + pad)
        self.lows = (4 * states + 2 * pad, 4 * states + 3 * pad)
        self.used = 4 * states + 2 * pad


def scan_block(feats, grads, rows, rates, slots, line, small_ref, row_slice):
    block = feats.shape[0]
    heads = slots.heads
    head_size = feats.shape[1] // heads
    per_group = LANES // head_size
    at_t, at_u = iota((block, block), 0), iota((block, block), 1)
    below, above = at_t > at_u, at_t < at_u
    same = None
    if line < block:
        (line_t, _), (line_u, _) = (
            split_index(at_t, (block // line, line)),
            split_index(at_u, (block // line, line)),
        )
        same = line_t == line_u

    def within(mask):
        return mask if same is None else mask & same

    ends = within(at_t <= at_u).astype(F32)
    starts = within(at_t >= at_u).astype(F32)
    sums = (
        -jnp.dot(rates[0], ends, precision=HI, preferred_element_type=F32),
        -jnp.dot(rates[1], starts, precision=HI, preferred_element_type=F32),
    )
    columns = jnp.transpose(jnp.concatenate(sums, axis=0))
    in_b = [rows[at : at + slots.states].astype(BF16) for at in slots.inputs]
    out_c = [rows[at : at + slots.states].astype(BF16) for at in slots.reads]
    score_down, score_up = tn(out_c[0], in_b[0]), tn(out_c[1], in_b[1])
    scores = jnp.where(
        below, score_down, jnp.where(above, score_up, score_down + score_up)
    )
    lane = iota((block, LANES), 1)
    grad_scores = jnp.zeros((block, block), F32)
    out_parts, grad_parts = [], []
    lane_pad = iota((block, LANES), 1)
    row_sums = jnp.zeros((block, LANES), F32)
    row_at = iota((2 * slots.pad, block), 0)
    col_sums = jnp.zeros((2 * slots.pad, block), F32)
    for group in range(heads // per_group):
        span = slice(group * LANES, (group + 1) * LANES)
        feat_group, grad_group = feats[:, span], grads[:, span]
        mixes, feat_own, grad_own = [], [], []
        for member in range(per_group):
            head = group * per_group + member
            mine = (lane >= member * head_size) & (lane < (member + 1) * head_size)
            feat_head = jnp.where(mine, feat_group, jnp.zeros_like(feat_group))
            grad_head = jnp.where(mine, grad_group, jnp.zeros_like(grad_group))
            up = slots.pad + head
            spread = jnp.where(
                below,
                columns[:, head : head + 1] - sums[0][head : head + 1],
                columns[:, up : up + 1] - sums[1][head : head + 1],
            )
            if same is not None:
                spread = jnp.where(same, spread, FAR)
            kernel = jnp.exp(spread)
            mix = kernel * scores
            grad_mix = nt(grad_group, feat_head)
            grad_scores = grad_scores + kernel * grad_mix
            flow = mix * grad_mix
            flow_down = jnp.where(below, flow, 0.0)
            row_down = jnp.sum(flow_down, axis=1, keepdims=True)
            row_all = jnp.sum(flow, axis=1, keepdims=True)
            col_down = jnp.sum(flow_down, axis=0, keepdims=True)
            col_all = jnp.sum(flow, axis=0, keepdims=True)
            row_sums = jnp.where(lane_pad == head, row_down, row_sums)
            row_sums = jnp.where(lane_pad == up, row_all - row_down, row_sums)
            col_sums = jnp.where(row_at == head, col_down, col_sums)
            col_sums = jnp.where(row_at == up, col_all - col_down, col_sums)
            mixes.append(mix.astype(BF16))
            feat_own.append(feat_head)
            grad_own.append(grad_head)
        out_parts.append(
            nn(jnp.concatenate(mixes, axis=1), jnp.concatenate(feat_own, axis=0))
        )
        grad_parts.append(
            tn(jnp.concatenate(mixes, axis=0), jnp.concatenate(grad_own, axis=0))
        )
    change = col_sums - jnp.transpose(row_sums)[: 2 * slots.pad]
    grad_down = within(at_t >= at_u)
    grad_up = within(at_t <= at_u)
    score_grads = (
        jnp.where(grad_down, grad_scores, 0.0).astype(BF16),
        jnp.where(grad_up, grad_scores, 0.0).astype(BF16),
    )
    for way in (0, 1):
        small_ref[slots.inputs[way] : slots.inputs[way] + slots.states, row_slice] = nn(
            out_c[way], score_grads[way]
        )
        small_ref[slots.reads[way] : slots.reads[way] + slots.states, row_slice] = nt(
            in_b[way], score_grads[way]
        )
        part = change[way * slots.pad : (way + 1) * slots.pad]
        reach = starts if way == 0 else ends
        small_ref[slots.rates[way] : slots.rates[way] + slots.pad, row_slice] = jnp.dot(
            part, reach, precision=HI, preferred_element_type=F32
        )
    return jnp.concatenate(out_parts, axis=1), jnp.concatenate(grad_parts, axis=1)


def pack_kernel(slots, ranks, feat_ref, cot_ref, rate_ref, input_ref, read_ref, out_ref, rows_ref):
    tile_rows, columns, width = feat_ref.shape
    model = cot_ref.shape[2]
    tokens = tile_rows * columns
    narrow = columns // ranks

    def source(at):
        rank, row, column = split_index(at, (ranks, tile_rows, narrow))
        return row * columns + rank * narrow + column

    order = one_hot_rows(tokens, source)
    out_ref[:, :width] = nn(order, feat_ref[...].reshape(tokens, width)).astype(BF16)
    out_ref[:, width : width + model] = nn(order, cot_ref[...].reshape(tokens, model)).astype(BF16)
    rows_ref[...] = jnp.zeros_like(rows_ref)
    for way in (0, 1):
        for row in range(tile_rows):
            span = slice(row * columns, (row + 1) * columns)
            at = slots.inputs[way]
            rows_ref[at : at + slots.states, span] = input_ref[2 + way, :, row, :]
            at = slots.reads[way]
            rows_ref[at : at + slots.states, span] = read_ref[2 + way, :, row, :]
            at = slots.rates[way]
            rate = rate_ref[2 + way, :, row, :]
            rows_ref[at : at + slots.heads, span] = rate
            at = slots.lows[way]
            rows_ref[at : at + slots.heads, span] = rate - rate.astype(BF16).astype(F32)
    out_ref[:, width + model :] = nt(order, rows_ref[...].astype(BF16)).astype(BF16)


def rows_kernel(
    slots, chunk, feat_ref, cot_ref, weight_ref, skip_ref, rate_ref, input_ref, read_ref,
    gx_ref, small_ref, part_ref, skip_out_ref, rows_ref,
):
    tile_rows, columns, width = feat_ref.shape
    tokens = tile_rows * columns
    skip = skip_ref[...]
    rows_ref[...] = jnp.zeros_like(rows_ref)
    partial = jnp.zeros(part_ref.shape, F32)
    skip_part = jnp.zeros((1, width), F32)
    for row in range(tile_rows):
        feats, cots = feat_ref[row], cot_ref[row]
        grads = nt(cots, weight_ref[...]).astype(BF16)
        for way in (0, 1):
            at = slots.inputs[way]
            rows_ref[at : at + slots.states, :] = input_ref[way, :, row, :]
            at = slots.reads[way]
            rows_ref[at : at + slots.states, :] = read_ref[way, :, row, :]
            at = slots.rates[way]
            rows_ref[at : at + slots.heads, :] = rate_ref[way, :, row, :]
        rates = [rows_ref[at : at + slots.pad, :] for at in slots.rates]
        outs, gx = scan_block(
            feats, grads, rows_ref, rates, slots, columns, small_ref,
            slice(row * columns, (row + 1) * columns),
        )
        feat_f32, grad_f32 = feats.astype(F32), grads.astype(F32)
        across = (outs + skip * feat_f32).astype(BF16)
        partial = partial + tn(across, cots)
        gx_ref[row * columns : (row + 1) * columns, :] = gx + skip * grad_f32
        skip_part = skip_part + jnp.sum(feat_f32 * grad_f32, axis=0, keepdims=True)
    part_ref[...] = partial
    if chunk is None:
        skip_out_ref[...] = skip_part
    else:
        high = skip_part.astype(BF16).astype(F32)
        piece = width // chunk
        lane_of = iota((chunk, width), 1)
        start = iota((chunk, width), 0) * piece
        owned = (lane_of >= start) & (lane_of < start + piece)
        spread = jnp.concatenate(
            [jnp.where(owned, high, 0.0), jnp.where(owned, skip_part - high, 0.0)], axis=1
        ).astype(BF16)
        skip_out_ref[...] = nn(spread, skip_places(slots, width, piece))


def skip_places(slots, width, piece):
    place = lax.rem(iota((width, 1), 0), piece) + slots.used
    lane = iota((width, LANES), 1)
    high, low = place == lane, place + piece == lane
    return jnp.concatenate([high.astype(F32), low.astype(F32)], axis=0).astype(BF16)


def cols_kernel(
    slots, ranks, tile_rows, chunk, recv_ref, weight_ref, part_ref, skip_ref,
    back_ref, sum_ref, small_ref,
):
    tokens = recv_ref.shape[0]
    width, model = weight_ref.shape
    line = ranks * tile_rows
    narrow = tokens // line
    block = max(line, min(LANES, tokens))

    def source(at):
        column, rank, row = split_index(at, (narrow, ranks, tile_rows))
        return rank * (tile_rows * narrow) + row * narrow + column

    def source_back(at):
        rank, row, column = split_index(at, (ranks, tile_rows, narrow))
        return column * line + rank * tile_rows + row

    order = one_hot_rows(tokens, source)
    feats = nn(order, recv_ref[:, :width]).astype(BF16)
    cots = nn(order, recv_ref[:, width : width + model]).astype(BF16)
    params = nn(order, recv_ref[:, width + model :])
    grads = nt(cots, weight_ref[...]).astype(BF16)
    small_ref[...] = jnp.zeros_like(small_ref)
    outs, gxs = [], []
    for at in range(0, tokens, block):
        span = slice(at, at + block)
        rows = jnp.transpose(params[span])
        rates = [
            rows[hi : hi + slots.pad] + rows[lo : lo + slots.pad]
            for hi, lo in zip(slots.rates, slots.lows)
        ]
        out, gx = scan_block(
            feats[span], grads[span], rows, rates, slots, line, small_ref, span
        )
        outs.append(out.astype(BF16))
        gxs.append(gx.astype(BF16))
    sum_ref[...] = (part_ref[...] + tn(jnp.concatenate(outs, axis=0), cots)).astype(BF16)
    order_back = one_hot_rows(tokens, source_back)
    back_ref[:, :width] = nn(order_back, jnp.concatenate(gxs, axis=0)).astype(BF16)
    smalls = nt(order_back, small_ref[...].astype(BF16))
    if chunk is not None:
        skip = skip_ref[...]
        smalls = smalls + jnp.concatenate([skip] * ranks, axis=0)
    back_ref[:, width:] = smalls.astype(BF16)


def sum_kernel(ranks, parts_ref, out_ref):
    rows = parts_ref.shape[0] // ranks
    total = parts_ref[:rows, :].astype(F32)
    for rank in range(1, ranks):
        total = total + parts_ref[rank * rows : (rank + 1) * rows, :].astype(F32)
    out_ref[...] = total.astype(BF16)


def finish_kernel(
    slots, ranks, chunk, back_ref, gx_ref, small_ref,
    feat_out, rate_out, input_out, read_out, *skip_out,
):
    tile_rows, columns, width = feat_out.shape
    tokens = tile_rows * columns
    narrow = columns // ranks

    def source(at):
        row, rank, column = split_index(at, (tile_rows, ranks, narrow))
        return rank * (tile_rows * narrow) + row * narrow + column

    order = one_hot_rows(tokens, source)
    total = gx_ref[...] + nn(order, back_ref[:, :width])
    feat_out[...] = total.astype(BF16).reshape(tile_rows, columns, width)
    smalls = nn(order, back_ref[:, width:])
    for row in range(tile_rows):
        span = slice(row * columns, (row + 1) * columns)
        rows = jnp.transpose(smalls[span])
        for way in (0, 1):
            at = slots.inputs[way]
            input_out[way, :, row, :] = small_ref[at : at + slots.states, span]
            input_out[2 + way, :, row, :] = rows[at : at + slots.states]
            at = slots.reads[way]
            read_out[way, :, row, :] = small_ref[at : at + slots.states, span]
            read_out[2 + way, :, row, :] = rows[at : at + slots.states]
            at = slots.rates[way]
            rate_out[way, :, row, :] = small_ref[at : at + slots.heads, span]
            rate_out[2 + way, :, row, :] = rows[at : at + slots.heads]
    if chunk is not None:
        piece = width // chunk
        gathered = back_ref[:chunk, width:].astype(F32)
        for rank in range(1, ranks):
            gathered = gathered + back_ref[rank * chunk : (rank + 1) * chunk, width:].astype(F32)
        places = skip_places(slots, width, piece).astype(F32)
        places = places[:width] + places[width:]
        spread = lax.dot_general(
            gathered, places, (((1,), (1,)), ((), ())), precision=HI, preferred_element_type=F32
        )
        lane_of = iota((chunk, width), 1)
        start = iota((chunk, width), 0) * piece
        owned = (lane_of >= start) & (lane_of < start + piece)
        skip_out[0][...] = jnp.sum(jnp.where(owned, spread, 0.0), axis=0, keepdims=True)


def widen_kernel(in_ref, out_ref):
    out_ref[...] = in_ref[...].astype(F32)


def call(kernel, name, out_shape, operands, scratch=(), flops=0, moved=0):
    return pl.pallas_call(
        kernel,
        name=name,
        out_shape=out_shape,
        scratch_shapes=list(scratch),
        cost_estimate=pl.CostEstimate(flops=flops, bytes_accessed=moved, transcendentals=0),
    )(*operands)


def local(ranks, features, decay_rate, input_proj, read_proj, skip_gain, out_weight, out_cotangent):
    tile_rows, columns, width = features.shape
    model = out_cotangent.shape[2]
    heads, states = decay_rate.shape[1], input_proj.shape[1]
    slots = Slots(heads, states)
    tokens = tile_rows * columns
    chunk = tokens // ranks
    room = chunk * (LANES - slots.used)
    if chunk % 8 or width % chunk or 2 * width > room:
        chunk = None
    shape = jax.ShapeDtypeStruct

    def exchange(array):
        return lax.all_to_all(array, "row", split_axis=0, concat_axis=0, tiled=True)

    packed = call(
        functools.partial(pack_kernel, slots, ranks), "pack",
        shape((tokens, width + model + LANES), BF16),
        (features, out_cotangent, decay_rate, input_proj, read_proj),
        [pltpu.VMEM((LANES, tokens), F32)],
        flops=2 * tokens * tokens * (width + model), moved=4 * tokens * (width + model),
    )
    received = exchange(packed)
    skip_shape = (1, width) if chunk is None else (chunk, LANES)
    gx_rows, small_rows, partial, skip_part = call(
        functools.partial(rows_kernel, slots, chunk), "rows",
        (
            shape((tokens, width), F32),
            shape((LANES, tokens), F32),
            shape((width, model), F32),
            shape(skip_shape, F32),
        ),
        (
            features, out_cotangent, out_weight, skip_gain.reshape(1, width),
            decay_rate, input_proj, read_proj,
        ),
        [pltpu.VMEM((LANES, columns), F32)],
        flops=2 * tokens * width * (2 * model + 3 * columns), moved=8 * tokens * width,
    )
    back, weight_sum = call(
        functools.partial(cols_kernel, slots, ranks, tile_rows, chunk), "cols",
        (shape((tokens, width + LANES), BF16), shape((width, model), BF16)),
        (received, out_weight, partial, skip_part),
        [pltpu.VMEM((LANES, tokens), F32)],
        flops=2 * tokens * width * (2 * model + 3 * columns), moved=8 * tokens * width,
    )
    weight_parts = exchange(weight_sum)
    returned = exchange(back)
    own = call(
        functools.partial(sum_kernel, ranks), "sum",
        shape((width // ranks, model), BF16), (weight_parts,),
        flops=width * model, moved=2 * width * model,
    )
    gathered = exchange(jnp.tile(own, (ranks, 1)))
    outs = [
        shape(features.shape, BF16),
        shape(decay_rate.shape, F32),
        shape(input_proj.shape, F32),
        shape(read_proj.shape, F32),
    ]
    if chunk is not None:
        outs.append(shape((1, width), F32))
    done = call(
        functools.partial(finish_kernel, slots, ranks, chunk), "finish",
        tuple(outs), (returned, gx_rows, small_rows),
        flops=2 * tokens * tokens * width, moved=8 * tokens * width,
    )
    grad_weight = call(
        widen_kernel, "widen", shape((width, model), F32), (gathered,),
        flops=width * model, moved=6 * width * model,
    )
    if chunk is None:
        grad_skip = lax.psum(skip_part, "row").reshape(width)
    else:
        grad_skip = done[4].reshape(width)
    return (*done[:4], grad_skip, grad_weight)


def solution(mesh):
    in_specs = (
        P(("grp", "row"), None, None),
        P(None, None, ("grp", "row"), None),
        P(None, None, ("grp", "row"), None),
        P(None, None, ("grp", "row"), None),
        P(),
        P(),
        P(("grp", "row"), None, None),
    )
    out_specs = (
        P(("grp", "row"), None, None),
        P(None, None, ("grp", "row"), None),
        P(None, None, ("grp", "row"), None),
        P(None, None, ("grp", "row"), None),
        P("grp"),
        P("grp", None),
    )
    body = functools.partial(local, mesh.shape["row"])
    return jax.shard_map(body, mesh=mesh, in_specs=in_specs, out_specs=out_specs, check_vma=False)
```

```python
import functools

import jax
import jax.numpy as jnp
from jax import lax
from jax.experimental import pallas as pl
from jax.experimental.pallas import tpu as pltpu
from jax.sharding import PartitionSpec as P

F32 = jnp.float32
BF16 = jnp.bfloat16
HI = lax.Precision.HIGHEST
LANES = 128
FAR = -1e30
VMEM_GRANT = 16 << 20


def iota(shape, dim):
    return lax.broadcasted_iota(jnp.int32, shape, dim)


def nt(a, b):
    return lax.dot_general(a, b, (((1,), (1,)), ((), ())), preferred_element_type=F32)


def nn(a, b):
    return jnp.dot(a, b, preferred_element_type=F32)


def tn(a, b):
    return lax.dot_general(a, b, (((0,), (0,)), ((), ())), preferred_element_type=F32)


def split_index(index, sizes):
    parts = []
    for size in reversed(sizes):
        if size & (size - 1) == 0:
            parts.append(index & (size - 1))
            index = index >> (size.bit_length() - 1)
        else:
            parts.append(lax.rem(index, size))
            index = lax.div(index, size)
    return parts[::-1]


def one_hot_rows(count, source_of):
    wanted = source_of(iota((count, 1), 0))
    return (wanted == iota((count, count), 1)).astype(F32).astype(BF16)


class Slots:
    def __init__(self, heads, states):
        self.heads = heads
        self.states = states
        self.inputs = (0, states)
        self.reads = (2 * states, 3 * states)
        pad = -(-heads // 8) * 8
        self.pad = pad
        self.rates = (4 * states, 4 * states + pad)
        self.lows = (4 * states + 2 * pad, 4 * states + 3 * pad)
        self.used = 4 * states + 2 * pad


class Lines:
    def __init__(self, rows, rates, slots, line, block):
        at_t, at_u = iota((block, block), 0), iota((block, block), 1)
        self.below, self.above = at_t > at_u, at_t < at_u
        self.same = None
        if line < block:
            line_t = split_index(at_t, (block // line, line))[0]
            line_u = split_index(at_u, (block // line, line))[0]
            self.same = line_t == line_u
        self.till = self.within(at_t <= at_u)
        self.since = self.within(at_t >= at_u)
        self.sums = (
            -jnp.dot(rates[0], self.till.astype(F32), precision=HI, preferred_element_type=F32),
            -jnp.dot(rates[1], self.since.astype(F32), precision=HI, preferred_element_type=F32),
        )
        self.columns = jnp.transpose(jnp.concatenate(self.sums, axis=0))
        self.inputs = [rows[at : at + slots.states].astype(BF16) for at in slots.inputs]
        self.reads = [rows[at : at + slots.states].astype(BF16) for at in slots.reads]
        down, up = (tn(self.reads[way], self.inputs[way]) for way in (0, 1))
        self.scores = jnp.where(self.below, down, jnp.where(self.above, up, down + up))
        self.pad = slots.pad

    def within(self, mask):
        return mask if self.same is None else mask & self.same

    def kernel(self, head):
        up = self.pad + head
        spread = jnp.where(
            self.below,
            self.columns[:, head : head + 1] - self.sums[0][head : head + 1],
            self.columns[:, up : up + 1] - self.sums[1][head : head + 1],
        )
        if self.same is not None:
            spread = jnp.where(self.same, spread, FAR)
        return jnp.exp(spread)


def head_mask(block, head_size, member):
    lane = iota((block, LANES), 1)
    return (lane >= member * head_size) & (lane < (member + 1) * head_size)


def scan_block(feats, grads, lines, slots, small_ref, row_slice, forward, backward):
    block = feats.shape[0]
    heads = slots.heads
    head_size = feats.shape[1] // heads
    per_group = LANES // head_size
    below = lines.below
    grad_scores = jnp.zeros((block, block), F32)
    out_parts, grad_parts = [], []
    lane_pad = iota((block, LANES), 1)
    row_sums = jnp.zeros((block, LANES), F32)
    row_at = iota((2 * slots.pad, block), 0)
    col_sums = jnp.zeros((2 * slots.pad, block), F32)
    for group in range(heads // per_group):
        span = slice(group * LANES, (group + 1) * LANES)
        feat_group = feats[:, span]
        grad_group = grads[:, span] if backward else None
        mixes, feat_own, grad_own = [], [], []
        for member in range(per_group):
            head = group * per_group + member
            up = slots.pad + head
            mine = head_mask(block, head_size, member)
            feat_head = jnp.where(mine, feat_group, jnp.zeros_like(feat_group))
            kernel = lines.kernel(head)
            mix = kernel * lines.scores
            mixes.append(mix.astype(BF16))
            feat_own.append(feat_head)
            if not backward:
                continue
            grad_own.append(jnp.where(mine, grad_group, jnp.zeros_like(grad_group)))
            grad_mix = nt(grad_group, feat_head)
            grad_scores = grad_scores + kernel * grad_mix
            flow = mix * grad_mix
            flow_down = jnp.where(below, flow, 0.0)
            row_down = jnp.sum(flow_down, axis=1, keepdims=True)
            row_all = jnp.sum(flow, axis=1, keepdims=True)
            col_down = jnp.sum(flow_down, axis=0, keepdims=True)
            col_all = jnp.sum(flow, axis=0, keepdims=True)
            row_sums = jnp.where(lane_pad == head, row_down, row_sums)
            row_sums = jnp.where(lane_pad == up, row_all - row_down, row_sums)
            col_sums = jnp.where(row_at == head, col_down, col_sums)
            col_sums = jnp.where(row_at == up, col_all - col_down, col_sums)
        if forward:
            out_parts.append(
                nn(jnp.concatenate(mixes, axis=1), jnp.concatenate(feat_own, axis=0))
            )
        if backward:
            grad_parts.append(
                tn(jnp.concatenate(mixes, axis=0), jnp.concatenate(grad_own, axis=0))
            )
    out = jnp.concatenate(out_parts, axis=1) if forward else None
    if not backward:
        return out, None
    change = col_sums - jnp.transpose(row_sums)[: 2 * slots.pad]
    reach = (lines.since, lines.till)
    for way in (0, 1):
        score_grad = jnp.where(reach[way], grad_scores, 0.0).astype(BF16)
        at = slots.inputs[way]
        small_ref[at : at + slots.states, row_slice] = nn(lines.reads[way], score_grad)
        at = slots.reads[way]
        small_ref[at : at + slots.states, row_slice] = nt(lines.inputs[way], score_grad)
        at = slots.rates[way]
        part = change[way * slots.pad : (way + 1) * slots.pad]
        small_ref[at : at + slots.pad, row_slice] = jnp.dot(
            part, reach[way].astype(F32), precision=HI, preferred_element_type=F32
        )
    return out, jnp.concatenate(grad_parts, axis=1)


def pack_kernel(slots, ranks, feat_ref, cot_ref, rate_ref, input_ref, read_ref, out_ref, rows_ref):
    tile_rows, columns, width = feat_ref.shape
    model = cot_ref.shape[2]
    tokens = tile_rows * columns
    narrow = columns // ranks

    def source(at):
        rank, row, column = split_index(at, (ranks, tile_rows, narrow))
        return row * columns + rank * narrow + column

    order = one_hot_rows(tokens, source)
    out_ref[:, :width] = nn(order, feat_ref[...].reshape(tokens, width)).astype(BF16)
    out_ref[:, width : width + model] = nn(order, cot_ref[...].reshape(tokens, model)).astype(BF16)
    rows_ref[...] = jnp.zeros_like(rows_ref)
    for way in (0, 1):
        for row in range(tile_rows):
            span = slice(row * columns, (row + 1) * columns)
            at = slots.inputs[way]
            rows_ref[at : at + slots.states, span] = input_ref[2 + way, :, row, :]
            at = slots.reads[way]
            rows_ref[at : at + slots.states, span] = read_ref[2 + way, :, row, :]
            at = slots.rates[way]
            rate = rate_ref[2 + way, :, row, :]
            rows_ref[at : at + slots.heads, span] = rate
            at = slots.lows[way]
            rows_ref[at : at + slots.heads, span] = rate - rate.astype(BF16).astype(F32)
    out_ref[:, width + model :] = nt(order, rows_ref[...].astype(BF16)).astype(BF16)


def rows_kernel(
    slots, chunk, feat_ref, cot_ref, weight_ref, skip_ref, rate_ref, input_ref, read_ref,
    gx_ref, small_ref, part_ref, skip_out_ref, rows_ref,
):
    tile_rows, columns, width = feat_ref.shape
    tokens = tile_rows * columns
    skip = skip_ref[...]
    rows_ref[...] = jnp.zeros_like(rows_ref)
    partial = jnp.zeros(part_ref.shape, F32)
    skip_part = jnp.zeros((1, width), F32)
    for row in range(tile_rows):
        feats, cots = feat_ref[row], cot_ref[row]
        grads = nt(cots, weight_ref[...]).astype(BF16)
        for way in (0, 1):
            at = slots.inputs[way]
            rows_ref[at : at + slots.states, :] = input_ref[way, :, row, :]
            at = slots.reads[way]
            rows_ref[at : at + slots.states, :] = read_ref[way, :, row, :]
            at = slots.rates[way]
            rows_ref[at : at + slots.heads, :] = rate_ref[way, :, row, :]
        rates = [rows_ref[at : at + slots.pad, :] for at in slots.rates]
        lines = Lines(rows_ref, rates, slots, columns, columns)
        outs, gx = scan_block(
            feats, grads, lines, slots, small_ref,
            slice(row * columns, (row + 1) * columns), True, True,
        )
        feat_f32, grad_f32 = feats.astype(F32), grads.astype(F32)
        across = (outs + skip * feat_f32).astype(BF16)
        partial = partial + tn(across, cots)
        gx_ref[row * columns : (row + 1) * columns, :] = gx + skip * grad_f32
        skip_part = skip_part + jnp.sum(feat_f32 * grad_f32, axis=0, keepdims=True)
    part_ref[...] = partial
    if chunk is None:
        skip_out_ref[...] = skip_part
    else:
        high = skip_part.astype(BF16).astype(F32)
        piece = width // chunk
        lane_of = iota((chunk, width), 1)
        start = iota((chunk, width), 0) * piece
        owned = (lane_of >= start) & (lane_of < start + piece)
        spread = jnp.concatenate(
            [jnp.where(owned, high, 0.0), jnp.where(owned, skip_part - high, 0.0)], axis=1
        ).astype(BF16)
        skip_out_ref[...] = nn(spread, skip_places(slots, width, piece))


def skip_places(slots, width, piece):
    place = lax.rem(iota((width, 1), 0), piece) + slots.used
    lane = iota((width, LANES), 1)
    high, low = place == lane, place + piece == lane
    return jnp.concatenate([high.astype(F32), low.astype(F32)], axis=0).astype(BF16)


class Columns:
    def __init__(self, slots, ranks, tile_rows, width, model, recv_ref):
        tokens = recv_ref.shape[0]
        self.line = ranks * tile_rows
        narrow = tokens // self.line
        self.block = max(self.line, min(LANES, tokens))
        self.slots = slots

        def source(at):
            column, rank, row = split_index(at, (narrow, ranks, tile_rows))
            return rank * (tile_rows * narrow) + row * narrow + column

        def source_back(at):
            rank, row, column = split_index(at, (ranks, tile_rows, narrow))
            return column * self.line + rank * tile_rows + row

        order = one_hot_rows(tokens, source)
        self.source_back = source_back
        self.feats = nn(order, recv_ref[:, :width]).astype(BF16)
        self.cots = nn(order, recv_ref[:, width : width + model]).astype(BF16)
        self.params = nn(order, recv_ref[:, width + model :])
        self.spans = [slice(at, at + self.block) for at in range(0, tokens, self.block)]

    def lines(self, span):
        slots = self.slots
        rows = jnp.transpose(self.params[span])
        rates = [
            rows[hi : hi + slots.pad] + rows[lo : lo + slots.pad]
            for hi, lo in zip(slots.rates, slots.lows)
        ]
        return Lines(rows, rates, slots, self.line, self.block)


def forward_kernel(slots, ranks, tile_rows, recv_ref, part_ref, sum_ref):
    width, model = part_ref.shape
    cols = Columns(slots, ranks, tile_rows, width, model, recv_ref)
    outs = [
        scan_block(cols.feats[span], None, cols.lines(span), slots, None, None, True, False)[0]
        for span in cols.spans
    ]
    down = jnp.concatenate(outs, axis=0).astype(BF16)
    sum_ref[...] = (part_ref[...] + tn(down, cols.cots)).astype(BF16)


def backward_kernel(
    slots, ranks, tile_rows, chunk, recv_ref, weight_ref, skip_ref, back_ref, small_ref
):
    width, model = weight_ref.shape
    cols = Columns(slots, ranks, tile_rows, width, model, recv_ref)
    grads = nt(cols.cots, weight_ref[...]).astype(BF16)
    small_ref[...] = jnp.zeros_like(small_ref)
    gxs = [
        scan_block(
            cols.feats[span], grads[span], cols.lines(span), slots, small_ref, span, False, True
        )[1].astype(BF16)
        for span in cols.spans
    ]
    order_back = one_hot_rows(recv_ref.shape[0], cols.source_back)
    back_ref[:, :width] = nn(order_back, jnp.concatenate(gxs, axis=0)).astype(BF16)
    smalls = nt(order_back, small_ref[...].astype(BF16))
    if chunk is not None:
        smalls = smalls + jnp.concatenate([skip_ref[...]] * ranks, axis=0)
    back_ref[:, width:] = smalls.astype(BF16)


def strip(array):
    return [array[:, at : at + LANES] for at in range(0, array.shape[1], LANES)]


def sum_kernel(ranks, parts_ref, back_ref, out_ref):
    rows = parts_ref.shape[0] // ranks
    total = parts_ref[:rows, :].astype(F32)
    for rank in range(1, ranks):
        total = total + parts_ref[rank * rows : (rank + 1) * rows, :].astype(F32)
    own = total.astype(BF16)
    tokens = back_ref.shape[0] // ranks
    for rank in range(ranks):
        at = 0
        pieces = strip(back_ref[rank * tokens : (rank + 1) * tokens, :]) + strip(own)
        for piece in pieces:
            out_ref[rank, at : at + piece.shape[0], :] = piece
            at += piece.shape[0]


def finish_kernel(
    slots, ranks, chunk, recv_ref, gx_ref, small_ref,
    feat_out, rate_out, input_out, read_out, weight_out, *skip_out,
):
    tile_rows, columns, width = feat_out.shape
    tokens = tile_rows * columns
    narrow = columns // ranks
    group = tokens // ranks
    model = weight_out.shape[1]
    rows = weight_out.shape[0] // ranks
    backs = width // LANES + 1

    for rank in range(ranks):
        at = backs * group
        for lane in range(0, model, LANES):
            weight_out[rank * rows : (rank + 1) * rows, lane : lane + LANES] = recv_ref[
                rank, at : at + rows, :
            ].astype(F32)
            at += rows

    def source(at):
        row, rank, column = split_index(at, (tile_rows, ranks, narrow))
        return rank * group + row * narrow + column

    order = one_hot_rows(tokens, source)
    back = [
        jnp.concatenate(
            [recv_ref[rank, part * group : (part + 1) * group, :] for rank in range(ranks)], axis=0
        )
        for part in range(backs)
    ]
    for part in range(backs - 1):
        lane = slice(part * LANES, (part + 1) * LANES)
        total = gx_ref[:, lane] + nn(order, back[part])
        feat_out[:, :, lane] = total.astype(BF16).reshape(tile_rows, columns, LANES)
    smalls = nn(order, back[-1])
    for row in range(tile_rows):
        span = slice(row * columns, (row + 1) * columns)
        held = jnp.transpose(smalls[span])
        for way in (0, 1):
            at = slots.inputs[way]
            input_out[way, :, row, :] = small_ref[at : at + slots.states, span]
            input_out[2 + way, :, row, :] = held[at : at + slots.states]
            at = slots.reads[way]
            read_out[way, :, row, :] = small_ref[at : at + slots.states, span]
            read_out[2 + way, :, row, :] = held[at : at + slots.states]
            at = slots.rates[way]
            rate_out[way, :, row, :] = small_ref[at : at + slots.heads, span]
            rate_out[2 + way, :, row, :] = held[at : at + slots.heads]
    if chunk is not None:
        piece = width // chunk
        gathered = back[-1][:chunk].astype(F32)
        for rank in range(1, ranks):
            gathered = gathered + back[-1][rank * chunk : (rank + 1) * chunk].astype(F32)
        places = skip_places(slots, width, piece).astype(F32)
        places = places[:width] + places[width:]
        spread = lax.dot_general(
            gathered, places, (((1,), (1,)), ((), ())), precision=HI, preferred_element_type=F32
        )
        lane_of = iota((chunk, width), 1)
        start = iota((chunk, width), 0) * piece
        owned = (lane_of >= start) & (lane_of < start + piece)
        skip_out[0][...] = jnp.sum(jnp.where(owned, spread, 0.0), axis=0)


def call(kernel, name, out_shape, operands, scratch=(), flops=0, moved=0, grant=VMEM_GRANT):
    return pl.pallas_call(
        kernel,
        name=name,
        out_shape=out_shape,
        in_specs=[pl.BlockSpec(memory_space=pltpu.VMEM)] * len(operands),
        out_specs=jax.tree.map(lambda leaf: pl.BlockSpec(memory_space=pltpu.VMEM), out_shape),
        scratch_shapes=list(scratch),
        compiler_params=pltpu.CompilerParams(vmem_limit_bytes=grant),
        cost_estimate=pl.CostEstimate(flops=flops, bytes_accessed=moved, transcendentals=0),
    )(*operands)


def local(ranks, features, decay_rate, input_proj, read_proj, skip_gain, out_weight, out_cotangent):
    tile_rows, columns, width = features.shape
    model = out_cotangent.shape[2]
    heads, states = decay_rate.shape[1], input_proj.shape[1]
    slots = Slots(heads, states)
    tokens = tile_rows * columns
    chunk = tokens // ranks
    room = chunk * (LANES - slots.used)
    if chunk % 8 or width % chunk or 2 * width > room:
        chunk = None
    shape = jax.ShapeDtypeStruct

    def exchange(array):
        return lax.all_to_all(array, "row", split_axis=0, concat_axis=0, tiled=True)

    packed = call(
        functools.partial(pack_kernel, slots, ranks), "pack",
        shape((tokens, width + model + LANES), BF16),
        (features, out_cotangent, decay_rate, input_proj, read_proj),
        [pltpu.VMEM((LANES, tokens), F32)],
        flops=2 * tokens * tokens * (width + model), moved=4 * tokens * (width + model), grant=None,
    )
    received = exchange(packed)
    skip_shape = (1, width) if chunk is None else (chunk, LANES)
    gx_rows, small_rows, partial, skip_part = call(
        functools.partial(rows_kernel, slots, chunk), "rows",
        (
            shape((tokens, width), F32),
            shape((LANES, tokens), F32),
            shape((width, model), F32),
            shape(skip_shape, F32),
        ),
        (
            features, out_cotangent, out_weight, skip_gain.reshape(1, width),
            decay_rate, input_proj, read_proj,
        ),
        [pltpu.VMEM((LANES, columns), F32)],
        flops=2 * tokens * width * (2 * model + 3 * columns), moved=8 * tokens * width,
    )
    weight_sum = call(
        functools.partial(forward_kernel, slots, ranks, tile_rows), "forward",
        shape((width, model), BF16), (received, partial),
        flops=2 * tokens * width * (2 * model + columns), moved=8 * tokens * width,
    )
    weight_parts = exchange(weight_sum)
    back = call(
        functools.partial(backward_kernel, slots, ranks, tile_rows, chunk), "backward",
        shape((tokens, width + LANES), BF16), (received, out_weight, skip_part),
        [pltpu.VMEM((LANES, tokens), F32)],
        flops=2 * tokens * width * (2 * model + 3 * columns), moved=8 * tokens * width,
    )
    group = tokens // ranks
    chunk_rows = (width // LANES + 1) * group + (model // LANES) * (width // ranks)
    last = call(
        functools.partial(sum_kernel, ranks), "sum",
        shape((ranks, chunk_rows, LANES), BF16), (weight_parts, back),
        flops=width * model, moved=2 * width * model,
    )
    returned = exchange(last)
    outs = [
        shape(features.shape, BF16),
        shape(decay_rate.shape, F32),
        shape(input_proj.shape, F32),
        shape(read_proj.shape, F32),
        shape((width, model), F32),
    ]
    if chunk is not None:
        outs.append(shape((width,), F32))
    done = call(
        functools.partial(finish_kernel, slots, ranks, chunk), "finish",
        tuple(outs), (returned, gx_rows, small_rows),
        flops=2 * tokens * tokens * width, moved=8 * tokens * width,
    )
    if chunk is None:
        grad_skip = lax.psum(skip_part, "row").reshape(width)
    else:
        grad_skip = done[5]
    return (*done[:4], grad_skip, done[4])


def solution(mesh):
    in_specs = (
        P(("grp", "row"), None, None),
        P(None, None, ("grp", "row"), None),
        P(None, None, ("grp", "row"), None),
        P(None, None, ("grp", "row"), None),
        P(),
        P(),
        P(("grp", "row"), None, None),
    )
    out_specs = (
        P(("grp", "row"), None, None),
        P(None, None, ("grp", "row"), None),
        P(None, None, ("grp", "row"), None),
        P(None, None, ("grp", "row"), None),
        P("grp"),
        P("grp", None),
    )
    body = functools.partial(local, mesh.shape["row"])
    return jax.shard_map(body, mesh=mesh, in_specs=in_specs, out_specs=out_specs, check_vma=False)
```

```python
import functools

import jax
import jax.numpy as jnp
from jax import lax
from jax.experimental import pallas as pl
from jax.experimental.pallas import tpu as pltpu
from jax.sharding import PartitionSpec as P

F32 = jnp.float32
BF16 = jnp.bfloat16
HI = lax.Precision.HIGHEST
LANES = 128
FAR = -1e30
VMEM_GRANT = 16 << 20


def iota(shape, dim):
    return lax.broadcasted_iota(jnp.int32, shape, dim)


def nt(a, b):
    return lax.dot_general(a, b, (((1,), (1,)), ((), ())), preferred_element_type=F32)


def nn(a, b):
    return jnp.dot(a, b, preferred_element_type=F32)


def tn(a, b):
    return lax.dot_general(a, b, (((0,), (0,)), ((), ())), preferred_element_type=F32)


def split_index(index, sizes):
    parts = []
    for size in reversed(sizes):
        if size & (size - 1) == 0:
            parts.append(index & (size - 1))
            index = index >> (size.bit_length() - 1)
        else:
            parts.append(lax.rem(index, size))
            index = lax.div(index, size)
    return parts[::-1]


def one_hot_rows(count, source_of):
    wanted = source_of(iota((count, 1), 0))
    return (wanted == iota((count, count), 1)).astype(F32).astype(BF16)


class Slots:
    def __init__(self, heads, states):
        self.heads = heads
        self.states = states
        self.inputs = (0, states)
        self.reads = (2 * states, 3 * states)
        pad = -(-heads // 8) * 8
        self.pad = pad
        self.rates = (4 * states, 4 * states + pad)
        self.lows = (4 * states + 2 * pad, 4 * states + 3 * pad)
        self.used = 4 * states + 2 * pad


class Lines:
    def __init__(self, rows, rates, slots, line, block):
        at_t, at_u = iota((block, block), 0), iota((block, block), 1)
        self.below, self.above = at_t > at_u, at_t < at_u
        self.same = None
        if line < block:
            line_t = split_index(at_t, (block // line, line))[0]
            line_u = split_index(at_u, (block // line, line))[0]
            self.same = line_t == line_u
        self.till = self.within(at_t <= at_u)
        self.since = self.within(at_t >= at_u)
        self.sums = (
            -jnp.dot(rates[0], self.till.astype(F32), precision=HI, preferred_element_type=F32),
            -jnp.dot(rates[1], self.since.astype(F32), precision=HI, preferred_element_type=F32),
        )
        self.columns = jnp.transpose(jnp.concatenate(self.sums, axis=0))
        self.inputs = [rows[at : at + slots.states].astype(BF16) for at in slots.inputs]
        self.reads = [rows[at : at + slots.states].astype(BF16) for at in slots.reads]
        down, up = (tn(self.reads[way], self.inputs[way]) for way in (0, 1))
        self.scores = jnp.where(self.below, down, jnp.where(self.above, up, down + up))
        self.pad = slots.pad

    def within(self, mask):
        return mask if self.same is None else mask & self.same

    def kernel(self, head):
        up = self.pad + head
        spread = jnp.where(
            self.below,
            self.columns[:, head : head + 1] - self.sums[0][head : head + 1],
            self.columns[:, up : up + 1] - self.sums[1][head : head + 1],
        )
        if self.same is not None:
            spread = jnp.where(self.same, spread, FAR)
        return jnp.exp(spread)


def head_mask(block, head_size, member):
    lane = iota((block, LANES), 1)
    return (lane >= member * head_size) & (lane < (member + 1) * head_size)


def scan_block(feats, grads, lines, slots, small_ref, row_slice, forward, backward):
    block = feats.shape[0]
    heads = slots.heads
    head_size = feats.shape[1] // heads
    per_group = LANES // head_size
    below = lines.below
    grad_scores = jnp.zeros((block, block), F32)
    out_parts, grad_parts = [], []
    lane_pad = iota((block, LANES), 1)
    row_sums = jnp.zeros((block, LANES), F32)
    row_at = iota((2 * slots.pad, block), 0)
    col_sums = jnp.zeros((2 * slots.pad, block), F32)
    for group in range(heads // per_group):
        span = slice(group * LANES, (group + 1) * LANES)
        feat_group = feats[:, span]
        grad_group = grads[:, span] if backward else None
        mixes, feat_own, grad_own = [], [], []
        for member in range(per_group):
            head = group * per_group + member
            up = slots.pad + head
            mine = head_mask(block, head_size, member)
            feat_head = jnp.where(mine, feat_group, jnp.zeros_like(feat_group))
            kernel = lines.kernel(head)
            mix = kernel * lines.scores
            mixes.append(mix.astype(BF16))
            feat_own.append(feat_head)
            if not backward:
                continue
            grad_own.append(jnp.where(mine, grad_group, jnp.zeros_like(grad_group)))
            grad_mix = nt(grad_group, feat_head)
            grad_scores = grad_scores + kernel * grad_mix
            flow = mix * grad_mix
            flow_down = jnp.where(below, flow, 0.0)
            row_down = jnp.sum(flow_down, axis=1, keepdims=True)
            row_all = jnp.sum(flow, axis=1, keepdims=True)
            col_down = jnp.sum(flow_down, axis=0, keepdims=True)
            col_all = jnp.sum(flow, axis=0, keepdims=True)
            row_sums = jnp.where(lane_pad == head, row_down, row_sums)
            row_sums = jnp.where(lane_pad == up, row_all - row_down, row_sums)
            col_sums = jnp.where(row_at == head, col_down, col_sums)
            col_sums = jnp.where(row_at == up, col_all - col_down, col_sums)
        if forward:
            out_parts.append(
                nn(jnp.concatenate(mixes, axis=1), jnp.concatenate(feat_own, axis=0))
            )
        if backward:
            grad_parts.append(
                tn(jnp.concatenate(mixes, axis=0), jnp.concatenate(grad_own, axis=0))
            )
    out = jnp.concatenate(out_parts, axis=1) if forward else None
    if not backward:
        return out, None
    change = col_sums - jnp.transpose(row_sums)[: 2 * slots.pad]
    reach = (lines.since, lines.till)
    for way in (0, 1):
        score_grad = jnp.where(reach[way], grad_scores, 0.0).astype(BF16)
        at = slots.inputs[way]
        small_ref[at : at + slots.states, row_slice] = nn(lines.reads[way], score_grad)
        at = slots.reads[way]
        small_ref[at : at + slots.states, row_slice] = nt(lines.inputs[way], score_grad)
        at = slots.rates[way]
        part = change[way * slots.pad : (way + 1) * slots.pad]
        small_ref[at : at + slots.pad, row_slice] = jnp.dot(
            part, reach[way].astype(F32), precision=HI, preferred_element_type=F32
        )
    return out, jnp.concatenate(grad_parts, axis=1)


def by_rank(array, ranks):
    narrow = array[0].shape[0] // ranks
    return [
        jnp.concatenate([row[rank * narrow : (rank + 1) * narrow] for row in array], axis=0)
        for rank in range(ranks)
    ]


def pack_kernel(slots, ranks, feat_ref, cot_ref, rate_ref, input_ref, read_ref, out_ref, rows_ref):
    tile_rows, columns, width = feat_ref.shape
    model = cot_ref.shape[2]
    group = tile_rows * columns // ranks
    rows_ref[...] = jnp.zeros_like(rows_ref)
    for way in (0, 1):
        for row in range(tile_rows):
            span = slice(row * columns, (row + 1) * columns)
            at = slots.inputs[way]
            rows_ref[at : at + slots.states, span] = input_ref[2 + way, :, row, :]
            at = slots.reads[way]
            rows_ref[at : at + slots.states, span] = read_ref[2 + way, :, row, :]
            at = slots.rates[way]
            rate = rate_ref[2 + way, :, row, :]
            rows_ref[at : at + slots.heads, span] = rate
            at = slots.lows[way]
            rows_ref[at : at + slots.heads, span] = rate - rate.astype(BF16).astype(F32)
    values = [
        (0, [feat_ref[row].astype(F32) for row in range(tile_rows)]),
        (width, [cot_ref[row].astype(F32) for row in range(tile_rows)]),
        (
            width + model,
            [
                jnp.transpose(rows_ref[:, row * columns : (row + 1) * columns])
                for row in range(tile_rows)
            ],
        ),
    ]
    for lane, array in values:
        for rank, piece in enumerate(by_rank(array, ranks)):
            out_ref[rank * group : (rank + 1) * group, lane : lane + piece.shape[1]] = (
                piece.astype(BF16)
            )


def rows_kernel(
    slots, chunk, feat_ref, cot_ref, weight_ref, skip_ref, rate_ref, input_ref, read_ref,
    gx_ref, small_ref, part_ref, skip_out_ref, rows_ref,
):
    tile_rows, columns, width = feat_ref.shape
    tokens = tile_rows * columns
    skip = skip_ref[...]
    rows_ref[...] = jnp.zeros_like(rows_ref)
    partial = jnp.zeros(part_ref.shape, F32)
    skip_part = jnp.zeros((1, width), F32)
    for row in range(tile_rows):
        feats, cots = feat_ref[row], cot_ref[row]
        grads = nt(cots, weight_ref[...]).astype(BF16)
        for way in (0, 1):
            at = slots.inputs[way]
            rows_ref[at : at + slots.states, :] = input_ref[way, :, row, :]
            at = slots.reads[way]
            rows_ref[at : at + slots.states, :] = read_ref[way, :, row, :]
            at = slots.rates[way]
            rows_ref[at : at + slots.heads, :] = rate_ref[way, :, row, :]
        rates = [rows_ref[at : at + slots.pad, :] for at in slots.rates]
        lines = Lines(rows_ref, rates, slots, columns, columns)
        outs, gx = scan_block(
            feats, grads, lines, slots, small_ref,
            slice(row * columns, (row + 1) * columns), True, True,
        )
        feat_f32, grad_f32 = feats.astype(F32), grads.astype(F32)
        across = (outs + skip * feat_f32).astype(BF16)
        partial = partial + tn(across, cots)
        gx_ref[row * columns : (row + 1) * columns, :] = gx + skip * grad_f32
        skip_part = skip_part + jnp.sum(feat_f32 * grad_f32, axis=0, keepdims=True)
    part_ref[...] = partial
    if chunk is None:
        skip_out_ref[...] = skip_part
    else:
        high = skip_part.astype(BF16).astype(F32)
        piece = width // chunk
        lane_of = iota((chunk, width), 1)
        start = iota((chunk, width), 0) * piece
        owned = (lane_of >= start) & (lane_of < start + piece)
        spread = jnp.concatenate(
            [jnp.where(owned, high, 0.0), jnp.where(owned, skip_part - high, 0.0)], axis=1
        ).astype(BF16)
        skip_out_ref[...] = nn(spread, skip_places(slots, width, piece))


def skip_places(slots, width, piece):
    place = lax.rem(iota((width, 1), 0), piece) + slots.used
    lane = iota((width, LANES), 1)
    high, low = place == lane, place + piece == lane
    return jnp.concatenate([high.astype(F32), low.astype(F32)], axis=0).astype(BF16)


class Columns:
    def __init__(self, slots, ranks, tile_rows, width, model, recv_ref):
        tokens = recv_ref.shape[0]
        self.line = ranks * tile_rows
        narrow = tokens // self.line
        self.block = max(self.line, min(LANES, tokens))
        self.slots = slots

        def source(at):
            column, rank, row = split_index(at, (narrow, ranks, tile_rows))
            return rank * (tile_rows * narrow) + row * narrow + column

        def source_back(at):
            rank, row, column = split_index(at, (ranks, tile_rows, narrow))
            return column * self.line + rank * tile_rows + row

        order = one_hot_rows(tokens, source)
        self.source_back = source_back
        self.feats = nn(order, recv_ref[:, :width]).astype(BF16)
        self.cots = nn(order, recv_ref[:, width : width + model]).astype(BF16)
        self.params = nn(order, recv_ref[:, width + model :])
        self.spans = [slice(at, at + self.block) for at in range(0, tokens, self.block)]

    def lines(self, span):
        slots = self.slots
        rows = jnp.transpose(self.params[span])
        rates = [
            rows[hi : hi + slots.pad] + rows[lo : lo + slots.pad]
            for hi, lo in zip(slots.rates, slots.lows)
        ]
        return Lines(rows, rates, slots, self.line, self.block)


def forward_kernel(slots, ranks, tile_rows, recv_ref, part_ref, sum_ref):
    width, model = part_ref.shape
    cols = Columns(slots, ranks, tile_rows, width, model, recv_ref)
    outs = [
        scan_block(cols.feats[span], None, cols.lines(span), slots, None, None, True, False)[0]
        for span in cols.spans
    ]
    down = jnp.concatenate(outs, axis=0).astype(BF16)
    sum_ref[...] = (part_ref[...] + tn(down, cols.cots)).astype(BF16)


def backward_kernel(
    slots, ranks, tile_rows, chunk, recv_ref, weight_ref, skip_ref, back_ref, small_ref
):
    width, model = weight_ref.shape
    cols = Columns(slots, ranks, tile_rows, width, model, recv_ref)
    grads = nt(cols.cots, weight_ref[...]).astype(BF16)
    small_ref[...] = jnp.zeros_like(small_ref)
    gxs = [
        scan_block(
            cols.feats[span], grads[span], cols.lines(span), slots, small_ref, span, False, True
        )[1].astype(BF16)
        for span in cols.spans
    ]
    order_back = one_hot_rows(recv_ref.shape[0], cols.source_back)
    back_ref[:, :width] = nn(order_back, jnp.concatenate(gxs, axis=0)).astype(BF16)
    smalls = nt(order_back, small_ref[...].astype(BF16))
    if chunk is not None:
        smalls = smalls + jnp.concatenate([skip_ref[...]] * ranks, axis=0)
    back_ref[:, width:] = smalls.astype(BF16)


def strip(array):
    return [array[:, at : at + LANES] for at in range(0, array.shape[1], LANES)]


class Halves:
    def __init__(self, rows, model):
        self.unit = 8 if rows % 8 == 0 else rows
        steps = rows // self.unit
        self.places = [
            (at * self.unit, lane) for lane in range(0, model, LANES) for at in range(steps)
        ]
        self.count = -(-len(self.places) // 2)
        self.size = self.count * self.unit

    def of(self, index):
        return divmod(index, self.count)


def sum_kernel(ranks, parts_ref, back_ref, out_ref):
    rows, model = parts_ref.shape[0] // ranks, parts_ref.shape[1]
    total = parts_ref[:rows, :].astype(F32)
    for rank in range(1, ranks):
        total = total + parts_ref[rank * rows : (rank + 1) * rows, :].astype(F32)
    tokens = back_ref.shape[0] // ranks
    halves = Halves(rows, model)
    unit = halves.unit
    blocks = [
        total[at : at + unit, lane : lane + LANES].astype(BF16) for at, lane in halves.places
    ]
    blocks += [jnp.zeros_like(blocks[0])] * (2 * halves.count - len(blocks))
    for rank in range(ranks):
        at = 0
        for piece in strip(back_ref[rank * tokens : (rank + 1) * tokens, :]):
            out_ref[rank, at : at + tokens, :] = piece
            at += tokens
        half = rank % 2
        for piece in blocks[half * halves.count : (half + 1) * halves.count]:
            out_ref[rank, at : at + unit, :] = piece
            at += unit


def half_kernel(recv_ref, out_ref):
    size = out_ref.shape[1]
    out_ref[...] = recv_ref[:, recv_ref.shape[1] - size :, :]


def weight_kernel(mine_ref, theirs_ref, out_ref):
    ranks = mine_ref.shape[0]
    width, model = out_ref.shape
    rows = width // ranks
    halves = Halves(rows, model)
    unit = halves.unit
    even = lax.rem(lax.axis_index("row"), 2) == 0
    mine, theirs = mine_ref[...].astype(F32), theirs_ref[...].astype(F32)
    pair = (jnp.where(even, mine, theirs), jnp.where(even, theirs, mine))
    for rank in range(ranks):
        for index, (at, lane) in enumerate(halves.places):
            half, step = halves.of(index)
            out_ref[rank * rows + at : rank * rows + at + unit, lane : lane + LANES] = pair[half][
                rank, step * unit : (step + 1) * unit, :
            ]


def finish_kernel(
    slots, ranks, chunk, recv_ref, gx_ref, small_ref,
    feat_out, rate_out, input_out, read_out, *skip_out,
):
    tile_rows, columns, width = feat_out.shape
    narrow = columns // ranks
    group = tile_rows * narrow
    lanes = width // LANES

    def part_of(part):
        return recv_ref[:, part * group : (part + 1) * group, :].astype(F32)

    def row_of(array, row):
        return jnp.concatenate(
            [array[rank, row * narrow : (row + 1) * narrow] for rank in range(ranks)], axis=0
        )

    for part in range(lanes):
        lane = slice(part * LANES, (part + 1) * LANES)
        back = part_of(part)
        for row in range(tile_rows):
            span = slice(row * columns, (row + 1) * columns)
            feat_out[row, :, lane] = (gx_ref[span, lane] + row_of(back, row)).astype(BF16)
    back = part_of(lanes)
    for row in range(tile_rows):
        span = slice(row * columns, (row + 1) * columns)
        held = jnp.transpose(row_of(back, row))
        for way in (0, 1):
            at = slots.inputs[way]
            input_out[way, :, row, :] = small_ref[at : at + slots.states, span]
            input_out[2 + way, :, row, :] = held[at : at + slots.states]
            at = slots.reads[way]
            read_out[way, :, row, :] = small_ref[at : at + slots.states, span]
            read_out[2 + way, :, row, :] = held[at : at + slots.states]
            at = slots.rates[way]
            rate_out[way, :, row, :] = small_ref[at : at + slots.heads, span]
            rate_out[2 + way, :, row, :] = held[at : at + slots.heads]
    if chunk is not None:
        piece = width // chunk
        gathered = jnp.sum(back, axis=0)
        places = skip_places(slots, width, piece).astype(F32)
        places = places[:width] + places[width:]
        spread = lax.dot_general(
            gathered, places, (((1,), (1,)), ((), ())), precision=HI, preferred_element_type=F32
        )
        lane_of = iota((chunk, width), 1)
        start = iota((chunk, width), 0) * piece
        owned = (lane_of >= start) & (lane_of < start + piece)
        skip_out[0][...] = jnp.sum(jnp.where(owned, spread, 0.0), axis=0)


def call(kernel, name, out_shape, operands, scratch=(), flops=0, moved=0, grant=VMEM_GRANT):
    return pl.pallas_call(
        kernel,
        name=name,
        out_shape=out_shape,
        in_specs=[pl.BlockSpec(memory_space=pltpu.VMEM)] * len(operands),
        out_specs=jax.tree.map(lambda leaf: pl.BlockSpec(memory_space=pltpu.VMEM), out_shape),
        scratch_shapes=list(scratch),
        compiler_params=pltpu.CompilerParams(vmem_limit_bytes=grant),
        cost_estimate=pl.CostEstimate(flops=flops, bytes_accessed=moved, transcendentals=0),
    )(*operands)


def local(ranks, features, decay_rate, input_proj, read_proj, skip_gain, out_weight, out_cotangent):
    tile_rows, columns, width = features.shape
    model = out_cotangent.shape[2]
    heads, states = decay_rate.shape[1], input_proj.shape[1]
    slots = Slots(heads, states)
    tokens = tile_rows * columns
    chunk = tokens // ranks
    room = chunk * (LANES - slots.used)
    if chunk % 8 or width % chunk or 2 * width > room:
        chunk = None
    shape = jax.ShapeDtypeStruct

    def exchange(array):
        return lax.all_to_all(array, "row", split_axis=0, concat_axis=0, tiled=True)

    packed = call(
        functools.partial(pack_kernel, slots, ranks), "pack",
        shape((tokens, width + model + LANES), BF16),
        (features, out_cotangent, decay_rate, input_proj, read_proj),
        [pltpu.VMEM((LANES, tokens), F32)],
        flops=2 * tokens * tokens * (width + model), moved=4 * tokens * (width + model), grant=None,
    )
    received = exchange(packed)
    skip_shape = (1, width) if chunk is None else (chunk, LANES)
    gx_rows, small_rows, partial, skip_part = call(
        functools.partial(rows_kernel, slots, chunk), "rows",
        (
            shape((tokens, width), F32),
            shape((LANES, tokens), F32),
            shape((width, model), F32),
            shape(skip_shape, F32),
        ),
        (
            features, out_cotangent, out_weight, skip_gain.reshape(1, width),
            decay_rate, input_proj, read_proj,
        ),
        [pltpu.VMEM((LANES, columns), F32)],
        flops=2 * tokens * width * (2 * model + 3 * columns), moved=8 * tokens * width,
    )
    weight_sum = call(
        functools.partial(forward_kernel, slots, ranks, tile_rows), "forward",
        shape((width, model), BF16), (received, partial),
        flops=2 * tokens * width * (2 * model + columns), moved=8 * tokens * width,
    )
    weight_parts = exchange(weight_sum)
    back = call(
        functools.partial(backward_kernel, slots, ranks, tile_rows, chunk), "backward",
        shape((tokens, width + LANES), BF16), (received, out_weight, skip_part),
        [pltpu.VMEM((LANES, tokens), F32)],
        flops=2 * tokens * width * (2 * model + 3 * columns), moved=8 * tokens * width,
    )
    group = tokens // ranks
    size = Halves(width // ranks, model).size
    last = call(
        functools.partial(sum_kernel, ranks), "sum",
        shape((ranks, (width // LANES + 1) * group + size, LANES), BF16), (weight_parts, back),
        flops=width * model, moved=2 * width * model,
    )
    returned = exchange(last)
    mine = call(
        half_kernel, "half", shape((ranks, size, LANES), BF16), (returned,),
        flops=width * model, moved=2 * width * model,
    )
    theirs = lax.ppermute(mine, "row", [(rank, rank ^ 1) for rank in range(ranks)])
    outs = [
        shape(features.shape, BF16),
        shape(decay_rate.shape, F32),
        shape(input_proj.shape, F32),
        shape(read_proj.shape, F32),
    ]
    if chunk is not None:
        outs.append(shape((width,), F32))
    done = call(
        functools.partial(finish_kernel, slots, ranks, chunk), "finish",
        tuple(outs), (returned, gx_rows, small_rows),
        flops=2 * tokens * tokens * width, moved=8 * tokens * width,
    )
    grad_weight = call(
        weight_kernel, "weight", shape((width, model), F32), (mine, theirs),
        flops=width * model, moved=6 * width * model,
    )
    if chunk is None:
        grad_skip = lax.psum(skip_part, "row").reshape(width)
    else:
        grad_skip = done[4]
    return (*done[:4], grad_skip, grad_weight)


def solution(mesh):
    in_specs = (
        P(("grp", "row"), None, None),
        P(None, None, ("grp", "row"), None),
        P(None, None, ("grp", "row"), None),
        P(None, None, ("grp", "row"), None),
        P(),
        P(),
        P(("grp", "row"), None, None),
    )
    out_specs = (
        P(("grp", "row"), None, None),
        P(None, None, ("grp", "row"), None),
        P(None, None, ("grp", "row"), None),
        P(None, None, ("grp", "row"), None),
        P("grp"),
        P("grp", None),
    )
    body = functools.partial(local, mesh.shape["row"])
    return jax.shard_map(body, mesh=mesh, in_specs=in_specs, out_specs=out_specs, check_vma=False)
```

```python
import functools

import jax
import jax.numpy as jnp
from jax import lax
from jax.experimental import pallas as pl
from jax.experimental.pallas import tpu as pltpu
from jax.sharding import PartitionSpec as P

F32 = jnp.float32
BF16 = jnp.bfloat16
HI = lax.Precision.HIGHEST
LANES = 128
FAR = -1e30
VMEM_GRANT = 16 << 20


def iota(shape, dim):
    return lax.broadcasted_iota(jnp.int32, shape, dim)


def nt(a, b):
    return lax.dot_general(a, b, (((1,), (1,)), ((), ())), preferred_element_type=F32)


def nn(a, b):
    return jnp.dot(a, b, preferred_element_type=F32)


def tn(a, b):
    return lax.dot_general(a, b, (((0,), (0,)), ((), ())), preferred_element_type=F32)


def split_index(index, sizes):
    parts = []
    for size in reversed(sizes):
        if size & (size - 1) == 0:
            parts.append(index & (size - 1))
            index = index >> (size.bit_length() - 1)
        else:
            parts.append(lax.rem(index, size))
            index = lax.div(index, size)
    return parts[::-1]


def one_hot_rows(count, source_of):
    wanted = source_of(iota((count, 1), 0))
    return (wanted == iota((count, count), 1)).astype(F32).astype(BF16)


class Slots:
    def __init__(self, heads, states):
        self.heads = heads
        self.states = states
        self.inputs = (0, states)
        self.reads = (2 * states, 3 * states)
        pad = -(-heads // 8) * 8
        self.pad = pad
        self.rates = (4 * states, 4 * states + pad)
        self.lows = (4 * states + 2 * pad, 4 * states + 3 * pad)
        self.used = 4 * states + 2 * pad


class Lines:
    def __init__(self, rows, rates, slots, line, block):
        at_t, at_u = iota((block, block), 0), iota((block, block), 1)
        self.below, self.above = at_t > at_u, at_t < at_u
        self.same = None
        if line < block:
            line_t = split_index(at_t, (block // line, line))[0]
            line_u = split_index(at_u, (block // line, line))[0]
            self.same = line_t == line_u
        self.till = self.within(at_t <= at_u)
        self.since = self.within(at_t >= at_u)
        self.sums = (
            -jnp.dot(rates[0], self.till.astype(F32), precision=HI, preferred_element_type=F32),
            -jnp.dot(rates[1], self.since.astype(F32), precision=HI, preferred_element_type=F32),
        )
        self.columns = jnp.transpose(jnp.concatenate(self.sums, axis=0))
        self.inputs = [rows[at : at + slots.states].astype(BF16) for at in slots.inputs]
        self.reads = [rows[at : at + slots.states].astype(BF16) for at in slots.reads]
        down, up = (tn(self.reads[way], self.inputs[way]) for way in (0, 1))
        self.scores = jnp.where(self.below, down, jnp.where(self.above, up, down + up))
        self.pad = slots.pad

    def within(self, mask):
        return mask if self.same is None else mask & self.same

    def kernel(self, head):
        up = self.pad + head
        spread = jnp.where(
            self.below,
            self.columns[:, head : head + 1] - self.sums[0][head : head + 1],
            self.columns[:, up : up + 1] - self.sums[1][head : head + 1],
        )
        if self.same is not None:
            spread = jnp.where(self.same, spread, FAR)
        return jnp.exp(spread)


def head_mask(block, head_size, member):
    lane = iota((block, LANES), 1)
    return (lane >= member * head_size) & (lane < (member + 1) * head_size)


def scan_block(feats, grads, lines, slots, small_ref, row_slice, forward, backward):
    block = feats.shape[0]
    heads = slots.heads
    head_size = feats.shape[1] // heads
    per_group = LANES // head_size
    below = lines.below
    grad_scores = jnp.zeros((block, block), F32)
    out_parts, grad_parts = [], []
    lane_pad = iota((block, LANES), 1)
    row_sums = jnp.zeros((block, LANES), F32)
    row_at = iota((2 * slots.pad, block), 0)
    col_sums = jnp.zeros((2 * slots.pad, block), F32)
    for group in range(heads // per_group):
        span = slice(group * LANES, (group + 1) * LANES)
        feat_group = feats[:, span]
        grad_group = grads[:, span] if backward else None
        mixes, feat_own, grad_own = [], [], []
        for member in range(per_group):
            head = group * per_group + member
            up = slots.pad + head
            mine = head_mask(block, head_size, member)
            feat_head = jnp.where(mine, feat_group, jnp.zeros_like(feat_group))
            kernel = lines.kernel(head)
            mix = kernel * lines.scores
            mixes.append(mix.astype(BF16))
            feat_own.append(feat_head)
            if not backward:
                continue
            grad_own.append(jnp.where(mine, grad_group, jnp.zeros_like(grad_group)))
            grad_mix = nt(grad_group, feat_head)
            grad_scores = grad_scores + kernel * grad_mix
            flow = mix * grad_mix
            flow_down = jnp.where(below, flow, 0.0)
            row_down = jnp.sum(flow_down, axis=1, keepdims=True)
            row_all = jnp.sum(flow, axis=1, keepdims=True)
            col_down = jnp.sum(flow_down, axis=0, keepdims=True)
            col_all = jnp.sum(flow, axis=0, keepdims=True)
            row_sums = jnp.where(lane_pad == head, row_down, row_sums)
            row_sums = jnp.where(lane_pad == up, row_all - row_down, row_sums)
            col_sums = jnp.where(row_at == head, col_down, col_sums)
            col_sums = jnp.where(row_at == up, col_all - col_down, col_sums)
        if forward:
            out_parts.append(
                nn(jnp.concatenate(mixes, axis=1), jnp.concatenate(feat_own, axis=0))
            )
        if backward:
            grad_parts.append(
                tn(jnp.concatenate(mixes, axis=0), jnp.concatenate(grad_own, axis=0))
            )
    out = jnp.concatenate(out_parts, axis=1) if forward else None
    if not backward:
        return out, None
    change = col_sums - jnp.transpose(row_sums)[: 2 * slots.pad]
    reach = (lines.since, lines.till)
    for way in (0, 1):
        score_grad = jnp.where(reach[way], grad_scores, 0.0).astype(BF16)
        at = slots.inputs[way]
        small_ref[at : at + slots.states, row_slice] = nn(lines.reads[way], score_grad)
        at = slots.reads[way]
        small_ref[at : at + slots.states, row_slice] = nt(lines.inputs[way], score_grad)
        at = slots.rates[way]
        part = change[way * slots.pad : (way + 1) * slots.pad]
        small_ref[at : at + slots.pad, row_slice] = jnp.dot(
            part, reach[way].astype(F32), precision=HI, preferred_element_type=F32
        )
    return out, jnp.concatenate(grad_parts, axis=1)


def by_rank(array, ranks):
    narrow = array[0].shape[0] // ranks
    return [
        jnp.concatenate([row[rank * narrow : (rank + 1) * narrow] for row in array], axis=0)
        for rank in range(ranks)
    ]


def pack_kernel(slots, ranks, feat_ref, cot_ref, rate_ref, input_ref, read_ref, out_ref, rows_ref):
    tile_rows, columns, width = feat_ref.shape
    model = cot_ref.shape[2]
    group = tile_rows * columns // ranks
    rows_ref[...] = jnp.zeros_like(rows_ref)
    for way in (0, 1):
        for row in range(tile_rows):
            span = slice(row * columns, (row + 1) * columns)
            at = slots.inputs[way]
            rows_ref[at : at + slots.states, span] = input_ref[2 + way, :, row, :]
            at = slots.reads[way]
            rows_ref[at : at + slots.states, span] = read_ref[2 + way, :, row, :]
            at = slots.rates[way]
            rate = rate_ref[2 + way, :, row, :]
            rows_ref[at : at + slots.heads, span] = rate
            at = slots.lows[way]
            rows_ref[at : at + slots.heads, span] = rate - rate.astype(BF16).astype(F32)
    values = [
        (0, [feat_ref[row].astype(F32) for row in range(tile_rows)]),
        (width, [cot_ref[row].astype(F32) for row in range(tile_rows)]),
        (
            width + model,
            [
                jnp.transpose(rows_ref[:, row * columns : (row + 1) * columns])
                for row in range(tile_rows)
            ],
        ),
    ]
    for lane, array in values:
        for rank, piece in enumerate(by_rank(array, ranks)):
            out_ref[rank * group : (rank + 1) * group, lane : lane + piece.shape[1]] = (
                piece.astype(BF16)
            )


def rows_kernel(
    slots, chunk, tables, feat_ref, cot_ref, weight_ref, skip_ref, rate_ref, input_ref, read_ref,
    gx_ref, small_ref, part_ref, skip_out_ref, *refs,
):
    *table_refs, rows_ref = refs
    tables.fill(table_refs)
    tile_rows, columns, width = feat_ref.shape
    tokens = tile_rows * columns
    skip = skip_ref[...]
    rows_ref[...] = jnp.zeros_like(rows_ref)
    partial = jnp.zeros(part_ref.shape, F32)
    skip_part = jnp.zeros((1, width), F32)
    for row in range(tile_rows):
        feats, cots = feat_ref[row], cot_ref[row]
        grads = nt(cots, weight_ref[...]).astype(BF16)
        for way in (0, 1):
            at = slots.inputs[way]
            rows_ref[at : at + slots.states, :] = input_ref[way, :, row, :]
            at = slots.reads[way]
            rows_ref[at : at + slots.states, :] = read_ref[way, :, row, :]
            at = slots.rates[way]
            rows_ref[at : at + slots.heads, :] = rate_ref[way, :, row, :]
        rates = [rows_ref[at : at + slots.pad, :] for at in slots.rates]
        lines = Lines(rows_ref, rates, slots, columns, columns)
        outs, gx = scan_block(
            feats, grads, lines, slots, small_ref,
            slice(row * columns, (row + 1) * columns), True, True,
        )
        feat_f32, grad_f32 = feats.astype(F32), grads.astype(F32)
        across = (outs + skip * feat_f32).astype(BF16)
        partial = partial + tn(across, cots)
        gx_ref[row * columns : (row + 1) * columns, :] = gx + skip * grad_f32
        skip_part = skip_part + jnp.sum(feat_f32 * grad_f32, axis=0, keepdims=True)
    part_ref[...] = partial
    if chunk is None:
        skip_out_ref[...] = skip_part
    else:
        high = skip_part.astype(BF16).astype(F32)
        piece = width // chunk
        lane_of = iota((chunk, width), 1)
        start = iota((chunk, width), 0) * piece
        owned = (lane_of >= start) & (lane_of < start + piece)
        spread = jnp.concatenate(
            [jnp.where(owned, high, 0.0), jnp.where(owned, skip_part - high, 0.0)], axis=1
        ).astype(BF16)
        skip_out_ref[...] = nn(spread, skip_places(slots, width, piece))


def skip_places(slots, width, piece):
    at = iota((width, 1), 0)
    whole = ((at.astype(F32) + 0.5) * (1.0 / piece)).astype(jnp.int32)
    place = at - whole * piece + slots.used
    lane = iota((width, LANES), 1)
    high, low = place == lane, place + piece == lane
    return jnp.concatenate([high.astype(F32), low.astype(F32)], axis=0).astype(BF16)


def ordered_by_column(ranks, tile_rows, tokens):
    line = ranks * tile_rows
    narrow = tokens // line

    def source(at):
        column, rank, row = split_index(at, (narrow, ranks, tile_rows))
        return rank * (tile_rows * narrow) + row * narrow + column

    return one_hot_rows(tokens, source)


def ordered_by_rank(ranks, tile_rows, tokens):
    line = ranks * tile_rows
    narrow = tokens // line

    def source(at):
        rank, row, column = split_index(at, (ranks, tile_rows, narrow))
        return column * line + rank * tile_rows + row

    return one_hot_rows(tokens, source)


def blocks_of(line, tokens):
    block = max(line, min(LANES, tokens))
    return block, [slice(at, at + block) for at in range(0, tokens, block)]


def long_lines(params, span, slots, line, block):
    rows = jnp.transpose(params[span].astype(F32))
    rates = [
        rows[hi : hi + slots.pad] + rows[lo : lo + slots.pad]
        for hi, lo in zip(slots.rates, slots.lows)
    ]
    return Lines(rows, rates, slots, line, block)


def halves_of(array):
    high = array.astype(BF16)
    return high, (array - high.astype(F32)).astype(BF16)


def reach_of(line, block):
    at_t, at_u = iota((block, block), 0), iota((block, block), 1)
    same = split_index(at_t, (block // line, line))[0] == (
        split_index(at_u, (block // line, line))[0]
    )
    return same, (same & (at_t >= at_u), same & (at_t <= at_u))


class Tables:
    def __init__(self, slots, ranks, tile_rows, tokens, width):
        line = ranks * tile_rows
        block = blocks_of(line, tokens)[0]
        self.slots, self.ranks, self.tile_rows = slots, ranks, tile_rows
        self.tokens, self.width, self.line, self.block = tokens, width, line, block
        self.shapes = [(tokens, tokens)] * 2
        if line <= LONGEST_SHORT:
            self.shapes += [(2 * block, block), (2 * LANES, 2 * width), (4 * width, LANES)]

    def fill(self, refs):
        slots, width, block = self.slots, self.width, self.block
        size = width // slots.heads
        refs[0][...] = ordered_by_column(self.ranks, self.tile_rows, self.tokens)
        refs[1][...] = ordered_by_rank(self.ranks, self.tile_rows, self.tokens)
        if self.line > LONGEST_SHORT:
            return
        same, reach = reach_of(self.line, block)
        half = jnp.where(same, 0.5, 0.0)
        for way in (0, 1):
            refs[2][way * block : (way + 1) * block, :] = (
                reach[way].astype(F32) - half
            ).astype(BF16)
            at = iota((LANES, width), 0)
            head = split_index(iota((LANES, width), 1), (slots.heads, size))[0]
            spread = (at == head + slots.rates[way]).astype(F32).astype(BF16)
            lanes = slice(way * width, (way + 1) * width)
            refs[3][:LANES, lanes] = spread
            refs[3][LANES:, lanes] = spread
            at = iota((width, LANES), 1)
            head = split_index(iota((width, LANES), 0), (slots.heads, size))[0]
            gather = (at == head + slots.rates[way]).astype(F32).astype(BF16)
            refs[4][way * width : (way + 1) * width, :] = gather
            refs[4][(2 + way) * width : (3 + way) * width, :] = gather


class ShortLines:
    def __init__(self, params, slots, line, block, spans, width, tables):
        self.slots, self.spans, self.block = slots, spans, block
        self.tables = tables
        self.reach = reach_of(line, block)[1]
        tokens = params.shape[0]
        lane = iota((tokens, LANES), 1)
        states = slots.states
        ways = tables[2][...]
        sums = [nn(ways, params[span]) for span in spans]
        low_up = lane >= slots.lows[1]
        self.up_lane = ((lane >= slots.rates[1]) & (lane < slots.lows[0])) | low_up
        sums = jnp.where(
            self.up_lane,
            jnp.concatenate([both[block:] for both in sums], axis=0),
            jnp.concatenate([both[:block] for both in sums], axis=0),
        )
        wide = params.astype(F32)
        turned = pltpu.roll(wide, LANES - slots.reads[0], 1)
        first, second = lane < states, (lane >= states) & (lane < 2 * states)
        self.inputs = [jnp.where(mask, wide, 0.0).astype(BF16) for mask in (first, second)]
        self.reads = [jnp.where(mask, turned, 0.0).astype(BF16) for mask in (first, second)]
        scores = [
            nt(jnp.concatenate([read[span] for read in self.reads], axis=0), params[span])
            for span in spans
        ]
        self.scores = [
            [
                jnp.where(self.reach[way], both[way * block : (way + 1) * block], 0.0).astype(BF16)
                for both in scores
            ]
            for way in (0, 1)
        ]
        sums = sums + pltpu.roll(sums, LANES - (slots.lows[0] - slots.rates[0]), 1)
        rated = (lane >= slots.rates[0]) & (lane < slots.lows[0])
        sums = jnp.where(rated, sums, 0.0)
        spread = tables[3][...]

        def widen(narrow):
            wide = nn(jnp.concatenate(halves_of(narrow), axis=1), spread)
            return wide[:, :width], wide[:, width:]

        self.losses, self.gains = widen(jnp.exp(sums)), widen(jnp.exp(-sums))

    def per_block(self, way, product, right):
        return jnp.concatenate(
            [
                product(score, right[span])
                for score, span in zip(self.scores[way], self.spans)
            ],
            axis=0,
        )

    def values(self, feats):
        wide = feats.astype(F32)
        self.lost = [(wide * loss).astype(BF16) for loss in self.losses]
        self.mixed = [self.per_block(way, nn, self.lost[way]) for way in (0, 1)]

    def forward(self, feats):
        self.values(feats)
        return self.gains[0] * self.mixed[0] + self.gains[1] * self.mixed[1]

    def backward(self, feats, grads):
        self.values(feats)
        slots, spans = self.slots, self.spans
        wide = grads.astype(F32)
        gained = [(wide * gain).astype(BF16) for gain in self.gains]
        back = [self.per_block(way, tn, gained[way]) for way in (0, 1)]
        gx = self.losses[0] * back[0] + self.losses[1] * back[1]
        score_grads = [
            [
                jnp.where(
                    self.reach[way], nt(gained[way][span], self.lost[way][span]), 0.0
                ).astype(BF16)
                for way in (0, 1)
            ]
            for span in spans
        ]
        change = jnp.concatenate(
            [
                self.lost[way].astype(F32) * back[way] - gained[way].astype(F32) * self.mixed[way]
                for way in (0, 1)
            ],
            axis=1,
        )
        heads = nn(jnp.concatenate(halves_of(change), axis=1), self.tables[4][...])
        read_grads = [
            nn(
                jnp.concatenate(score_grads[at], axis=1),
                jnp.concatenate([part[span] for part in self.inputs], axis=0),
            )
            for at, span in enumerate(spans)
        ]
        input_grads = [
            tn(
                jnp.concatenate(score_grads[at], axis=0),
                jnp.concatenate([part[span] for part in self.reads], axis=0),
            )
            for at, span in enumerate(spans)
        ]
        since, till = (mask.astype(F32).astype(BF16) for mask in self.reach)
        both = jnp.concatenate(
            [jnp.concatenate([till, till], axis=1), jnp.concatenate([since, since], axis=1)], axis=0
        )
        high, low = halves_of(heads)
        reached = [
            nn(both, jnp.concatenate([high[span], low[span]], axis=0)) for span in spans
        ]
        rates = jnp.where(
            self.up_lane,
            jnp.concatenate([pair[self.block :] for pair in reached], axis=0),
            jnp.concatenate([pair[: self.block] for pair in reached], axis=0),
        )
        smalls = jnp.concatenate(input_grads, axis=0) + pltpu.roll(
            jnp.concatenate(read_grads, axis=0), slots.reads[0], 1
        )
        lane = iota(smalls.shape, 1)
        return gx, jnp.where(lane >= slots.rates[0], rates, smalls)


LONGEST_SHORT = 64


def forward_kernel(slots, ranks, tile_rows, recv_ref, part_ref, *refs):
    *tables, mine_ref, other_ref, order_ref = refs
    width, model = part_ref.shape
    tokens = recv_ref.shape[0]
    line = ranks * tile_rows
    block, spans = blocks_of(line, tokens)
    order = tables[0][...]
    params = nn(order, recv_ref[:, width + model :]).astype(BF16)
    feats = nn(order, recv_ref[:, :width]).astype(BF16)
    cots = nn(order, recv_ref[:, width : width + model]).astype(BF16)
    order_ref[:, width + model :] = params
    order_ref[:, :width] = feats
    order_ref[:, width : width + model] = cots
    if line <= LONGEST_SHORT:
        lines = ShortLines(params, slots, line, block, spans, width, tables)
        down = lines.forward(feats).astype(BF16)
    else:
        outs = []
        for span in spans:
            lines = long_lines(params, span, slots, line, block)
            outs.append(scan_block(feats[span], None, lines, slots, None, None, True, False)[0])
        down = jnp.concatenate(outs, axis=0).astype(BF16)
    total = part_ref[...] + tn(down, cots)
    even = lax.rem(lax.axis_index("row"), 2) == 0
    half = width // 2
    mine_ref[...] = jnp.where(even, total[:half], total[half:])
    other_ref[...] = jnp.where(even, total[half:], total[:half]).astype(BF16)


def backward_kernel(slots, ranks, tile_rows, chunk, order_ref, weight_ref, skip_ref, *refs):
    *tables, back_ref, small_ref = refs
    width, model = weight_ref.shape
    tokens = order_ref.shape[0]
    line = ranks * tile_rows
    block, spans = blocks_of(line, tokens)
    params = order_ref[:, width + model :]
    feats = order_ref[:, :width]
    grads = nt(order_ref[:, width : width + model], weight_ref[...]).astype(BF16)
    if line <= LONGEST_SHORT:
        lines = ShortLines(params, slots, line, block, spans, width, tables)
        gx, small = lines.backward(feats, grads)
        gx, small = gx.astype(BF16), small.astype(BF16)
    else:
        small_ref[...] = jnp.zeros_like(small_ref)
        gxs = []
        for span in spans:
            lines = long_lines(params, span, slots, line, block)
            gxs.append(
                scan_block(feats[span], grads[span], lines, slots, small_ref, span, False, True)[1]
            )
        gx = jnp.concatenate(gxs, axis=0).astype(BF16)
        small = jnp.transpose(small_ref[...]).astype(BF16)
    order_back = tables[1][...]
    back_ref[:, :width] = nn(order_back, gx).astype(BF16)
    small = nn(order_back, small)
    if chunk is not None:
        small = small + jnp.concatenate([skip_ref[...]] * ranks, axis=0)
    back_ref[:, width:] = small.astype(BF16)


def strip(array):
    return [array[:, at : at + LANES] for at in range(0, array.shape[1], LANES)]


class Tiles:
    def __init__(self, rows, model, ranks):
        self.unit = 8
        steps = rows // self.unit
        self.places = [
            (at * self.unit, lane) for lane in range(0, model, LANES) for at in range(steps)
        ]
        count = len(self.places)
        self.starts = [count * rank // ranks for rank in range(ranks + 1)]
        self.size = self.unit * -(-count // ranks)

    def of(self, rank):
        return self.places[self.starts[rank] : self.starts[rank + 1]]


def merge_kernel(ranks, mine_ref, theirs_ref, back_ref, out_ref):
    total = mine_ref[...] + theirs_ref[...].astype(F32)
    tokens = back_ref.shape[0] // ranks
    tiles = Tiles(*mine_ref.shape, ranks)
    unit = tiles.unit
    for rank in range(ranks):
        at = 0
        for piece in strip(back_ref[rank * tokens : (rank + 1) * tokens, :]):
            out_ref[rank, at : at + tokens, :] = piece
            at += tokens
        end = at + tiles.size
        for row, lane in tiles.of(rank):
            out_ref[rank, at : at + unit, :] = total[row : row + unit, lane : lane + LANES].astype(
                BF16
            )
            at += unit
        while at < end:
            out_ref[rank, at : at + unit, :] = jnp.zeros((unit, LANES), BF16)
            at += unit


def sum_kernel(recv_ref, out_ref):
    ranks, size = out_ref.shape[:2]
    own = slice(recv_ref.shape[1] - size, recv_ref.shape[1])
    for half in (0, 1):
        total = recv_ref[half, own, :].astype(F32)
        for rank in range(half + 2, ranks, 2):
            total = total + recv_ref[rank, own, :].astype(F32)
        total = total.astype(BF16)
        for rank in range(half, ranks, 2):
            out_ref[rank] = total


def weight_kernel(mine_ref, theirs_ref, out_ref):
    ranks = mine_ref.shape[0]
    width, model = out_ref.shape
    tiles = Tiles(width // 2, model, ranks)
    unit = tiles.unit
    even = lax.rem(lax.axis_index("row"), 2) == 0
    mine, theirs = mine_ref[...].astype(F32), theirs_ref[...].astype(F32)
    pair = (jnp.where(even, mine, theirs), jnp.where(even, theirs, mine))
    for half in (0, 1):
        for rank in range(ranks):
            for step, (row, lane) in enumerate(tiles.of(rank)):
                row += half * (width // 2)
                out_ref[row : row + unit, lane : lane + LANES] = pair[half][
                    rank, step * unit : (step + 1) * unit, :
                ]


def finish_kernel(
    slots, ranks, chunk, recv_ref, gx_ref, small_ref,
    feat_out, rate_out, input_out, read_out, *skip_out,
):
    tile_rows, columns, width = feat_out.shape
    narrow = columns // ranks
    group = tile_rows * narrow
    lanes = width // LANES

    def part_of(part):
        return recv_ref[:, part * group : (part + 1) * group, :].astype(F32)

    def row_of(array, row):
        return jnp.concatenate(
            [array[rank, row * narrow : (row + 1) * narrow] for rank in range(ranks)], axis=0
        )

    for part in range(lanes):
        lane = slice(part * LANES, (part + 1) * LANES)
        back = part_of(part)
        for row in range(tile_rows):
            span = slice(row * columns, (row + 1) * columns)
            feat_out[row, :, lane] = (gx_ref[span, lane] + row_of(back, row)).astype(BF16)
    back = part_of(lanes)
    for row in range(tile_rows):
        span = slice(row * columns, (row + 1) * columns)
        held = jnp.transpose(row_of(back, row))
        for way in (0, 1):
            at = slots.inputs[way]
            input_out[way, :, row, :] = small_ref[at : at + slots.states, span]
            input_out[2 + way, :, row, :] = held[at : at + slots.states]
            at = slots.reads[way]
            read_out[way, :, row, :] = small_ref[at : at + slots.states, span]
            read_out[2 + way, :, row, :] = held[at : at + slots.states]
            at = slots.rates[way]
            rate_out[way, :, row, :] = small_ref[at : at + slots.heads, span]
            rate_out[2 + way, :, row, :] = held[at : at + slots.heads]
    if chunk is not None:
        piece = width // chunk
        gathered = jnp.sum(back, axis=0)
        places = skip_places(slots, width, piece)
        places = places[:width] + places[width:]
        high, low = halves_of(gathered)
        spread = nt(high, places) + nt(low, places)
        lane_of = iota((chunk, width), 1)
        start = iota((chunk, width), 0) * piece
        owned = (lane_of >= start) & (lane_of < start + piece)
        skip_out[0][...] = jnp.sum(jnp.where(owned, spread, 0.0), axis=0)


def call(kernel, name, out_shape, operands, scratch=(), flops=0, moved=0, grant=VMEM_GRANT):
    return pl.pallas_call(
        kernel,
        name=name,
        out_shape=out_shape,
        in_specs=[pl.BlockSpec(memory_space=pltpu.VMEM)] * len(operands),
        out_specs=jax.tree.map(lambda leaf: pl.BlockSpec(memory_space=pltpu.VMEM), out_shape),
        scratch_shapes=list(scratch),
        compiler_params=pltpu.CompilerParams(vmem_limit_bytes=grant),
        cost_estimate=pl.CostEstimate(flops=flops, bytes_accessed=moved, transcendentals=0),
    )(*operands)


def local(ranks, features, decay_rate, input_proj, read_proj, skip_gain, out_weight, out_cotangent):
    tile_rows, columns, width = features.shape
    model = out_cotangent.shape[2]
    heads, states = decay_rate.shape[1], input_proj.shape[1]
    slots = Slots(heads, states)
    tokens = tile_rows * columns
    chunk = tokens // ranks
    room = chunk * (LANES - slots.used)
    if chunk % 8 or width % chunk or 2 * width > room:
        chunk = None
    shape = jax.ShapeDtypeStruct

    def exchange(array):
        return lax.all_to_all(array, "row", split_axis=0, concat_axis=0, tiled=True)

    packed = call(
        functools.partial(pack_kernel, slots, ranks), "pack",
        shape((tokens, width + model + LANES), BF16),
        (features, out_cotangent, decay_rate, input_proj, read_proj),
        [pltpu.VMEM((LANES, tokens), F32)],
        flops=2 * tokens * tokens * (width + model), moved=4 * tokens * (width + model), grant=None,
    )
    received = exchange(packed)
    skip_shape = (1, width) if chunk is None else (chunk, LANES)
    tables = Tables(slots, ranks, tile_rows, tokens, width)
    gx_rows, small_rows, partial, skip_part, *table = call(
        functools.partial(rows_kernel, slots, chunk, tables), "rows",
        (
            shape((tokens, width), F32),
            shape((LANES, tokens), F32),
            shape((width, model), F32),
            shape(skip_shape, F32),
            *(shape(sizes, BF16) for sizes in tables.shapes),
        ),
        (
            features, out_cotangent, out_weight, skip_gain.reshape(1, width),
            decay_rate, input_proj, read_proj,
        ),
        [pltpu.VMEM((LANES, columns), F32)],
        flops=2 * tokens * width * (2 * model + 3 * columns), moved=8 * tokens * width,
    )
    half = width // 2
    partners = [(rank, rank ^ 1) for rank in range(ranks)]
    mine, other, ordered = call(
        functools.partial(forward_kernel, slots, ranks, tile_rows), "forward",
        (
            shape((half, model), F32),
            shape((half, model), BF16),
            shape(received.shape, BF16),
        ),
        (received, partial, *table),
        flops=2 * tokens * width * (2 * model + columns), moved=8 * tokens * width,
    )
    theirs = lax.ppermute(other, "row", partners)
    back = call(
        functools.partial(backward_kernel, slots, ranks, tile_rows, chunk), "backward",
        shape((tokens, width + LANES), BF16), (ordered, out_weight, skip_part, *table),
        [pltpu.VMEM((LANES, tokens), F32)],
        flops=2 * tokens * width * (2 * model + 3 * columns), moved=8 * tokens * width,
    )
    group = tokens // ranks
    size = Tiles(half, model, ranks).size
    merged = call(
        functools.partial(merge_kernel, ranks), "merge",
        shape((ranks, (width // LANES + 1) * group + size, LANES), BF16), (mine, theirs, back),
        flops=width * model, moved=2 * width * model,
    )
    returned = exchange(merged)
    summed = call(
        sum_kernel, "sum", shape((ranks, size, LANES), BF16), (returned,),
        flops=width * model, moved=2 * width * model,
    )
    held = exchange(summed)
    swapped = lax.ppermute(held, "row", partners)
    returned, held = lax.optimization_barrier((returned, held))
    outs = [
        shape(features.shape, BF16),
        shape(decay_rate.shape, F32),
        shape(input_proj.shape, F32),
        shape(read_proj.shape, F32),
    ]
    if chunk is not None:
        outs.append(shape((width,), F32))
    done = call(
        functools.partial(finish_kernel, slots, ranks, chunk), "finish",
        tuple(outs), (returned, gx_rows, small_rows),
        flops=2 * tokens * tokens * width, moved=8 * tokens * width,
    )
    grad_weight = call(
        weight_kernel, "weight", shape((width, model), F32), (held, swapped),
        flops=width * model, moved=6 * width * model,
    )
    if chunk is None:
        grad_skip = lax.psum(skip_part, "row").reshape(width)
    else:
        grad_skip = done[4]
    return (*done[:4], grad_skip, grad_weight)


def solution(mesh):
    in_specs = (
        P(("grp", "row"), None, None),
        P(None, None, ("grp", "row"), None),
        P(None, None, ("grp", "row"), None),
        P(None, None, ("grp", "row"), None),
        P(),
        P(),
        P(("grp", "row"), None, None),
    )
    out_specs = (
        P(("grp", "row"), None, None),
        P(None, None, ("grp", "row"), None),
        P(None, None, ("grp", "row"), None),
        P(None, None, ("grp", "row"), None),
        P("grp"),
        P("grp", None),
    )
    body = functools.partial(local, mesh.shape["row"])
    return jax.shard_map(body, mesh=mesh, in_specs=in_specs, out_specs=out_specs, check_vma=False)
```

```python
import functools

import jax
import jax.numpy as jnp
from jax import lax
from jax.experimental import pallas as pl
from jax.experimental.pallas import tpu as pltpu
from jax.sharding import PartitionSpec as P

F32 = jnp.float32
BF16 = jnp.bfloat16
HI = lax.Precision.HIGHEST
LANES = 128
FAR = -1e30
VMEM_GRANT = 16 << 20


def iota(shape, dim):
    return lax.broadcasted_iota(jnp.int32, shape, dim)


def nt(a, b):
    return lax.dot_general(a, b, (((1,), (1,)), ((), ())), preferred_element_type=F32)


def nn(a, b):
    return jnp.dot(a, b, preferred_element_type=F32)


def tn(a, b):
    return lax.dot_general(a, b, (((0,), (0,)), ((), ())), preferred_element_type=F32)


def split_index(index, sizes):
    parts = []
    for size in reversed(sizes):
        if size & (size - 1) == 0:
            parts.append(index & (size - 1))
            index = index >> (size.bit_length() - 1)
        else:
            parts.append(lax.rem(index, size))
            index = lax.div(index, size)
    return parts[::-1]


class Slots:
    def __init__(self, heads, states):
        self.heads = heads
        self.states = states
        self.inputs = (0, states)
        self.reads = (2 * states, 3 * states)
        pad = -(-heads // 8) * 8
        self.pad = pad
        self.rates = (4 * states, 4 * states + pad)
        self.lows = (4 * states + 2 * pad, 4 * states + 3 * pad)
        self.used = 4 * states + 2 * pad


class Lines:
    def __init__(self, rows, rates, slots, lines, block):
        at_t, at_u = iota((block, block), 0), iota((block, block), 1)
        self.same = None
        if lines > 1:
            at_t, line_t = split_index(at_t, (block // lines, lines))
            at_u, line_u = split_index(at_u, (block // lines, lines))
            self.same = line_t == line_u
        self.below, self.above = at_t > at_u, at_t < at_u
        self.till = self.within(at_t <= at_u)
        self.since = self.within(at_t >= at_u)
        self.sums = (
            -jnp.dot(rates[0], self.till.astype(F32), precision=HI, preferred_element_type=F32),
            -jnp.dot(rates[1], self.since.astype(F32), precision=HI, preferred_element_type=F32),
        )
        self.columns = jnp.transpose(jnp.concatenate(self.sums, axis=0))
        self.inputs = [rows[at : at + slots.states].astype(BF16) for at in slots.inputs]
        self.reads = [rows[at : at + slots.states].astype(BF16) for at in slots.reads]
        down, up = (tn(self.reads[way], self.inputs[way]) for way in (0, 1))
        self.scores = jnp.where(self.below, down, jnp.where(self.above, up, down + up))
        self.pad = slots.pad

    def within(self, mask):
        return mask if self.same is None else mask & self.same

    def kernel(self, head):
        up = self.pad + head
        spread = jnp.where(
            self.below,
            self.columns[:, head : head + 1] - self.sums[0][head : head + 1],
            self.columns[:, up : up + 1] - self.sums[1][head : head + 1],
        )
        if self.same is not None:
            spread = jnp.where(self.same, spread, FAR)
        return jnp.exp(spread)


def head_mask(block, head_size, member):
    lane = iota((block, LANES), 1)
    return (lane >= member * head_size) & (lane < (member + 1) * head_size)


def scan_block(feats, grads, lines, slots, small_ref, row_slice, forward, backward):
    block = feats.shape[0]
    heads = slots.heads
    head_size = feats.shape[1] // heads
    per_group = LANES // head_size
    below = lines.below
    grad_scores = jnp.zeros((block, block), F32)
    out_parts, grad_parts = [], []
    lane_pad = iota((block, LANES), 1)
    row_sums = jnp.zeros((block, LANES), F32)
    row_at = iota((2 * slots.pad, block), 0)
    col_sums = jnp.zeros((2 * slots.pad, block), F32)
    for group in range(heads // per_group):
        span = slice(group * LANES, (group + 1) * LANES)
        feat_group = feats[:, span]
        grad_group = grads[:, span] if backward else None
        mixes, feat_own, grad_own = [], [], []
        for member in range(per_group):
            head = group * per_group + member
            up = slots.pad + head
            mine = head_mask(block, head_size, member)
            feat_head = jnp.where(mine, feat_group, jnp.zeros_like(feat_group))
            kernel = lines.kernel(head)
            mix = kernel * lines.scores
            mixes.append(mix.astype(BF16))
            feat_own.append(feat_head)
            if not backward:
                continue
            grad_own.append(jnp.where(mine, grad_group, jnp.zeros_like(grad_group)))
            grad_mix = nt(grad_group, feat_head)
            grad_scores = grad_scores + kernel * grad_mix
            flow = mix * grad_mix
            flow_down = jnp.where(below, flow, 0.0)
            row_down = jnp.sum(flow_down, axis=1, keepdims=True)
            row_all = jnp.sum(flow, axis=1, keepdims=True)
            col_down = jnp.sum(flow_down, axis=0, keepdims=True)
            col_all = jnp.sum(flow, axis=0, keepdims=True)
            row_sums = jnp.where(lane_pad == head, row_down, row_sums)
            row_sums = jnp.where(lane_pad == up, row_all - row_down, row_sums)
            col_sums = jnp.where(row_at == head, col_down, col_sums)
            col_sums = jnp.where(row_at == up, col_all - col_down, col_sums)
        if forward:
            out_parts.append(
                nn(jnp.concatenate(mixes, axis=1), jnp.concatenate(feat_own, axis=0))
            )
        if backward:
            grad_parts.append(
                tn(jnp.concatenate(mixes, axis=0), jnp.concatenate(grad_own, axis=0))
            )
    out = jnp.concatenate(out_parts, axis=1) if forward else None
    if not backward:
        return out, None
    change = col_sums - jnp.transpose(row_sums)[: 2 * slots.pad]
    reach = (lines.since, lines.till)
    for way in (0, 1):
        score_grad = jnp.where(reach[way], grad_scores, 0.0).astype(BF16)
        at = slots.inputs[way]
        small_ref[at : at + slots.states, row_slice] = nn(lines.reads[way], score_grad)
        at = slots.reads[way]
        small_ref[at : at + slots.states, row_slice] = nt(lines.inputs[way], score_grad)
        at = slots.rates[way]
        part = change[way * slots.pad : (way + 1) * slots.pad]
        small_ref[at : at + slots.pad, row_slice] = jnp.dot(
            part, reach[way].astype(F32), precision=HI, preferred_element_type=F32
        )
    return out, jnp.concatenate(grad_parts, axis=1)


def by_rank(array, ranks):
    narrow = array[0].shape[0] // ranks
    return [
        jnp.concatenate([row[rank * narrow : (rank + 1) * narrow] for row in array], axis=0)
        for rank in range(ranks)
    ]


def pack_kernel(slots, ranks, feat_ref, cot_ref, rate_ref, input_ref, read_ref, out_ref, rows_ref):
    tile_rows, columns, width = feat_ref.shape
    model = cot_ref.shape[2]
    group = tile_rows * columns // ranks
    rows_ref[...] = jnp.zeros_like(rows_ref)
    for way in (0, 1):
        for row in range(tile_rows):
            span = slice(row * columns, (row + 1) * columns)
            at = slots.inputs[way]
            rows_ref[at : at + slots.states, span] = input_ref[2 + way, :, row, :]
            at = slots.reads[way]
            rows_ref[at : at + slots.states, span] = read_ref[2 + way, :, row, :]
            at = slots.rates[way]
            rate = rate_ref[2 + way, :, row, :]
            rows_ref[at : at + slots.heads, span] = rate
            at = slots.lows[way]
            rows_ref[at : at + slots.heads, span] = rate - rate.astype(BF16).astype(F32)
    values = [
        (0, [feat_ref[row].astype(F32) for row in range(tile_rows)]),
        (width, [cot_ref[row].astype(F32) for row in range(tile_rows)]),
        (
            width + model,
            [
                jnp.transpose(rows_ref[:, row * columns : (row + 1) * columns])
                for row in range(tile_rows)
            ],
        ),
    ]
    for lane, array in values:
        for rank, piece in enumerate(by_rank(array, ranks)):
            out_ref[rank * group : (rank + 1) * group, lane : lane + piece.shape[1]] = (
                piece.astype(BF16)
            )


def rows_kernel(
    slots, chunk, tables, feat_ref, cot_ref, weight_ref, skip_ref, rate_ref, input_ref, read_ref,
    gx_ref, small_ref, part_ref, skip_out_ref, *refs,
):
    *table_refs, rows_ref = refs
    tables.fill(table_refs)
    tile_rows, columns, width = feat_ref.shape
    tokens = tile_rows * columns
    skip = skip_ref[...]
    rows_ref[...] = jnp.zeros_like(rows_ref)
    partial = jnp.zeros(part_ref.shape, F32)
    skip_part = jnp.zeros((1, width), F32)
    for row in range(tile_rows):
        feats, cots = feat_ref[row], cot_ref[row]
        grads = nt(cots, weight_ref[...]).astype(BF16)
        for way in (0, 1):
            at = slots.inputs[way]
            rows_ref[at : at + slots.states, :] = input_ref[way, :, row, :]
            at = slots.reads[way]
            rows_ref[at : at + slots.states, :] = read_ref[way, :, row, :]
            at = slots.rates[way]
            rows_ref[at : at + slots.heads, :] = rate_ref[way, :, row, :]
        rates = [rows_ref[at : at + slots.pad, :] for at in slots.rates]
        lines = Lines(rows_ref, rates, slots, 1, columns)
        outs, gx = scan_block(
            feats, grads, lines, slots, small_ref,
            slice(row * columns, (row + 1) * columns), True, True,
        )
        feat_f32, grad_f32 = feats.astype(F32), grads.astype(F32)
        across = (outs + skip * feat_f32).astype(BF16)
        partial = partial + tn(across, cots)
        gx_ref[row * columns : (row + 1) * columns, :] = gx + skip * grad_f32
        skip_part = skip_part + jnp.sum(feat_f32 * grad_f32, axis=0, keepdims=True)
    part_ref[...] = partial
    if chunk is None:
        skip_out_ref[...] = skip_part
    else:
        high = skip_part.astype(BF16).astype(F32)
        piece = width // chunk
        lane_of = iota((chunk, width), 1)
        start = iota((chunk, width), 0) * piece
        owned = (lane_of >= start) & (lane_of < start + piece)
        spread = jnp.concatenate(
            [jnp.where(owned, high, 0.0), jnp.where(owned, skip_part - high, 0.0)], axis=1
        ).astype(BF16)
        skip_out_ref[...] = nn(spread, skip_places(slots, width, piece))


def skip_places(slots, width, piece):
    at = iota((width, 1), 0)
    whole = ((at.astype(F32) + 0.5) * (1.0 / piece)).astype(jnp.int32)
    place = at - whole * piece + slots.used
    lane = iota((width, LANES), 1)
    high, low = place == lane, place + piece == lane
    return jnp.concatenate([high.astype(F32), low.astype(F32)], axis=0).astype(BF16)


def long_lines(params, slots, lines):
    rows = jnp.transpose(params.astype(F32))
    rates = [
        rows[hi : hi + slots.pad] + rows[lo : lo + slots.pad]
        for hi, lo in zip(slots.rates, slots.lows)
    ]
    return Lines(rows, rates, slots, lines, params.shape[0])


def halves_of(array):
    high = array.astype(BF16)
    return high, (array - high.astype(F32)).astype(BF16)


def reach_of(lines, block):
    at_t, line_t = split_index(iota((block, block), 0), (block // lines, lines))
    at_u, line_u = split_index(iota((block, block), 1), (block // lines, lines))
    same = line_t == line_u
    return same, (same & (at_t >= at_u), same & (at_t <= at_u))


class Tables:
    def __init__(self, slots, lines, tokens, width):
        self.slots, self.lines, self.tokens, self.width = slots, lines, tokens, width
        self.short = tokens // lines <= LONGEST_SHORT
        self.shapes = []
        if self.short:
            self.shapes = [(2 * tokens, tokens), (2 * LANES, 2 * width), (4 * width, LANES)]

    def fill(self, refs):
        if not self.short:
            return
        slots, width, tokens = self.slots, self.width, self.tokens
        size = width // slots.heads
        same, reach = reach_of(self.lines, tokens)
        half = jnp.where(same, 0.5, 0.0)
        for way in (0, 1):
            refs[0][way * tokens : (way + 1) * tokens, :] = (
                reach[way].astype(F32) - half
            ).astype(BF16)
            at = iota((LANES, width), 0)
            head = split_index(iota((LANES, width), 1), (slots.heads, size))[0]
            spread = (at == head + slots.rates[way]).astype(F32).astype(BF16)
            lanes = slice(way * width, (way + 1) * width)
            refs[1][:LANES, lanes] = spread
            refs[1][LANES:, lanes] = spread
            at = iota((width, LANES), 1)
            head = split_index(iota((width, LANES), 0), (slots.heads, size))[0]
            gather = (at == head + slots.rates[way]).astype(F32).astype(BF16)
            refs[2][way * width : (way + 1) * width, :] = gather
            refs[2][(2 + way) * width : (3 + way) * width, :] = gather


class ShortLines:
    def __init__(self, params, slots, lines, width, tables):
        self.slots, self.tables = slots, tables
        tokens = self.tokens = params.shape[0]
        self.reach = reach_of(lines, tokens)[1]
        lane = iota((tokens, LANES), 1)
        states = slots.states
        sums = nn(tables[0][...], params)
        low_up = lane >= slots.lows[1]
        self.up_lane = ((lane >= slots.rates[1]) & (lane < slots.lows[0])) | low_up
        sums = jnp.where(self.up_lane, sums[tokens:], sums[:tokens])
        wide = params.astype(F32)
        turned = pltpu.roll(wide, LANES - slots.reads[0], 1)
        first, second = lane < states, (lane >= states) & (lane < 2 * states)
        self.inputs = [jnp.where(mask, wide, 0.0).astype(BF16) for mask in (first, second)]
        self.reads = [jnp.where(mask, turned, 0.0).astype(BF16) for mask in (first, second)]
        self.scores = [
            jnp.where(self.reach[way], nt(self.reads[way], params), 0.0).astype(BF16)
            for way in (0, 1)
        ]
        sums = sums + pltpu.roll(sums, LANES - (slots.lows[0] - slots.rates[0]), 1)
        rated = (lane >= slots.rates[0]) & (lane < slots.lows[0])
        sums = jnp.where(rated, sums, 0.0)
        spread = tables[1][...]

        def widen(narrow):
            wide = nn(jnp.concatenate(halves_of(narrow), axis=1), spread)
            return wide[:, :width], wide[:, width:]

        self.losses, self.gains = widen(jnp.exp(sums)), widen(jnp.exp(-sums))

    def values(self, feats):
        wide = feats.astype(F32)
        self.lost = [(wide * loss).astype(BF16) for loss in self.losses]
        self.mixed = [nn(self.scores[way], self.lost[way]) for way in (0, 1)]

    def forward(self, feats):
        self.values(feats)
        return self.gains[0] * self.mixed[0] + self.gains[1] * self.mixed[1]

    def backward(self, feats, grads):
        self.values(feats)
        slots, tokens = self.slots, self.tokens
        wide = grads.astype(F32)
        gained = [(wide * gain).astype(BF16) for gain in self.gains]
        back = [tn(self.scores[way], gained[way]) for way in (0, 1)]
        gx = self.losses[0] * back[0] + self.losses[1] * back[1]
        score_grads = [
            jnp.where(self.reach[way], nt(gained[way], self.lost[way]), 0.0).astype(BF16)
            for way in (0, 1)
        ]
        change = jnp.concatenate(
            [
                self.lost[way].astype(F32) * back[way] - gained[way].astype(F32) * self.mixed[way]
                for way in (0, 1)
            ],
            axis=1,
        )
        heads = nn(jnp.concatenate(halves_of(change), axis=1), self.tables[2][...])
        read_grads = nn(score_grads[0], self.inputs[0]) + nn(score_grads[1], self.inputs[1])
        input_grads = tn(score_grads[0], self.reads[0]) + tn(score_grads[1], self.reads[1])
        since, till = (mask.astype(F32).astype(BF16) for mask in self.reach)
        high, low = halves_of(heads)
        both = jnp.concatenate([high, low], axis=1)
        down, up = nn(till, both), nn(since, both)
        rates = jnp.where(
            self.up_lane, up[:, :LANES] + up[:, LANES:], down[:, :LANES] + down[:, LANES:]
        )
        smalls = input_grads + pltpu.roll(read_grads, slots.reads[0], 1)
        lane = iota((tokens, LANES), 1)
        return gx, jnp.where(lane >= slots.rates[0], rates, smalls)


LONGEST_SHORT = 64


def forward_kernel(slots, lines, recv_ref, part_ref, *refs):
    *tables, mine_ref, other_ref = refs
    width, model = part_ref.shape
    tokens = recv_ref.shape[0]
    feats, cots = recv_ref[:, :width], recv_ref[:, width : width + model]
    params = recv_ref[:, width + model :]
    if tokens // lines <= LONGEST_SHORT:
        down = ShortLines(params, slots, lines, width, tables).forward(feats)
    else:
        masks = long_lines(params, slots, lines)
        down = scan_block(feats, None, masks, slots, None, None, True, False)[0]
    total = part_ref[...] + tn(down.astype(BF16), cots)
    even = lax.rem(lax.axis_index("row"), 2) == 0
    half = width // 2
    mine_ref[...] = jnp.where(even, total[:half], total[half:])
    other_ref[...] = jnp.where(even, total[half:], total[:half]).astype(BF16)


def backward_kernel(slots, ranks, lines, chunk, recv_ref, weight_ref, skip_ref, *refs):
    *tables, back_ref, small_ref = refs
    width, model = weight_ref.shape
    tokens = recv_ref.shape[0]
    feats = recv_ref[:, :width]
    params = recv_ref[:, width + model :]
    grads = nt(recv_ref[:, width : width + model], weight_ref[...]).astype(BF16)
    if tokens // lines <= LONGEST_SHORT:
        gx, small = ShortLines(params, slots, lines, width, tables).backward(feats, grads)
    else:
        small_ref[...] = jnp.zeros_like(small_ref)
        masks = long_lines(params, slots, lines)
        span = slice(0, tokens)
        gx = scan_block(feats, grads, masks, slots, small_ref, span, False, True)[1]
        small = jnp.transpose(small_ref[...])
    back_ref[:, :width] = gx.astype(BF16)
    if chunk is not None:
        small = small + jnp.concatenate([skip_ref[...]] * ranks, axis=0)
    back_ref[:, width:] = small.astype(BF16)


def strip(array):
    return [array[:, at : at + LANES] for at in range(0, array.shape[1], LANES)]


class Tiles:
    def __init__(self, rows, model, ranks):
        self.unit = 8
        steps = rows // self.unit
        self.places = [
            (at * self.unit, lane) for lane in range(0, model, LANES) for at in range(steps)
        ]
        count = len(self.places)
        self.starts = [count * rank // ranks for rank in range(ranks + 1)]
        self.size = self.unit * -(-count // ranks)

    def of(self, rank):
        return self.places[self.starts[rank] : self.starts[rank + 1]]


def lay_out(out_ref, rank, pieces):
    at = 0
    for piece in pieces:
        out_ref[rank, at : at + piece.shape[0], :] = piece
        at += piece.shape[0]
    if at < out_ref.shape[1]:
        out_ref[rank, at:, :] = jnp.zeros((out_ref.shape[1] - at, LANES), BF16)


def merge_kernel(ranks, early, mine_ref, theirs_ref, back_ref, out_ref):
    total = mine_ref[...] + theirs_ref[...].astype(F32)
    group = back_ref.shape[0] // ranks
    tiles = Tiles(*mine_ref.shape, ranks)
    for rank in range(ranks):
        strips = strip(back_ref[rank * group : (rank + 1) * group, :])[:early]
        blocks = [
            total[row : row + tiles.unit, lane : lane + LANES].astype(BF16)
            for row, lane in tiles.of(rank)
        ]
        lay_out(out_ref, rank, strips + blocks)


def sum_kernel(early, size, recv_ref, back_ref, out_ref):
    ranks = out_ref.shape[0]
    group = back_ref.shape[0] // ranks
    own = slice(recv_ref.shape[1] - size, recv_ref.shape[1])
    for half in (0, 1):
        total = recv_ref[half, own, :].astype(F32)
        for rank in range(half + 2, ranks, 2):
            total = total + recv_ref[rank, own, :].astype(F32)
        total = total.astype(BF16)
        for rank in range(half, ranks, 2):
            strips = strip(back_ref[rank * group : (rank + 1) * group, :])[early:]
            lay_out(out_ref, rank, strips + [total])


def half_kernel(recv_ref, out_ref):
    size = out_ref.shape[1]
    out_ref[...] = recv_ref[:, recv_ref.shape[1] - size :, :]


def weight_kernel(mine_ref, theirs_ref, out_ref):
    ranks = mine_ref.shape[0]
    width, model = out_ref.shape
    tiles = Tiles(width // 2, model, ranks)
    unit = tiles.unit
    even = lax.rem(lax.axis_index("row"), 2) == 0
    mine, theirs = mine_ref[...].astype(F32), theirs_ref[...].astype(F32)
    pair = (jnp.where(even, mine, theirs), jnp.where(even, theirs, mine))
    for half in (0, 1):
        for rank in range(ranks):
            for step, (row, lane) in enumerate(tiles.of(rank)):
                row += half * (width // 2)
                out_ref[row : row + unit, lane : lane + LANES] = pair[half][
                    rank, step * unit : (step + 1) * unit, :
                ]


def finish_kernel(
    slots, ranks, chunk, early, early_ref, late_ref, gx_ref, small_ref,
    feat_out, rate_out, input_out, read_out, *skip_out,
):
    tile_rows, columns, width = feat_out.shape
    narrow = columns // ranks
    group = tile_rows * narrow
    lanes = width // LANES

    def part_of(part):
        ref, part = (early_ref, part) if part < early else (late_ref, part - early)
        return ref[:, part * group : (part + 1) * group, :].astype(F32)

    def row_of(array, row):
        return jnp.concatenate(
            [array[rank, row * narrow : (row + 1) * narrow] for rank in range(ranks)], axis=0
        )

    for part in range(lanes):
        lane = slice(part * LANES, (part + 1) * LANES)
        back = part_of(part)
        for row in range(tile_rows):
            span = slice(row * columns, (row + 1) * columns)
            feat_out[row, :, lane] = (gx_ref[span, lane] + row_of(back, row)).astype(BF16)
    back = part_of(lanes)
    for row in range(tile_rows):
        span = slice(row * columns, (row + 1) * columns)
        held = jnp.transpose(row_of(back, row))
        for way in (0, 1):
            at = slots.inputs[way]
            input_out[way, :, row, :] = small_ref[at : at + slots.states, span]
            input_out[2 + way, :, row, :] = held[at : at + slots.states]
            at = slots.reads[way]
            read_out[way, :, row, :] = small_ref[at : at + slots.states, span]
            read_out[2 + way, :, row, :] = held[at : at + slots.states]
            at = slots.rates[way]
            rate_out[way, :, row, :] = small_ref[at : at + slots.heads, span]
            rate_out[2 + way, :, row, :] = held[at : at + slots.heads]
    if chunk is not None:
        piece = width // chunk
        gathered = jnp.sum(back, axis=0)
        places = skip_places(slots, width, piece)
        places = places[:width] + places[width:]
        high, low = halves_of(gathered)
        spread = nt(high, places) + nt(low, places)
        lane_of = iota((chunk, width), 1)
        start = iota((chunk, width), 0) * piece
        owned = (lane_of >= start) & (lane_of < start + piece)
        skip_out[0][...] = jnp.sum(jnp.where(owned, spread, 0.0), axis=0)


def call(kernel, name, out_shape, operands, scratch=(), flops=0, moved=0, grant=VMEM_GRANT):
    return pl.pallas_call(
        kernel,
        name=name,
        out_shape=out_shape,
        in_specs=[pl.BlockSpec(memory_space=pltpu.VMEM)] * len(operands),
        out_specs=jax.tree.map(lambda leaf: pl.BlockSpec(memory_space=pltpu.VMEM), out_shape),
        scratch_shapes=list(scratch),
        compiler_params=pltpu.CompilerParams(vmem_limit_bytes=grant),
        cost_estimate=pl.CostEstimate(flops=flops, bytes_accessed=moved, transcendentals=0),
    )(*operands)


def local(ranks, features, decay_rate, input_proj, read_proj, skip_gain, out_weight, out_cotangent):
    tile_rows, columns, width = features.shape
    model = out_cotangent.shape[2]
    heads, states = decay_rate.shape[1], input_proj.shape[1]
    slots = Slots(heads, states)
    tokens = tile_rows * columns
    chunk = tokens // ranks
    room = chunk * (LANES - slots.used)
    if chunk % 8 or width % chunk or 2 * width > room:
        chunk = None
    shape = jax.ShapeDtypeStruct

    def exchange(array):
        return lax.all_to_all(array, "row", split_axis=0, concat_axis=0, tiled=True)

    packed = call(
        functools.partial(pack_kernel, slots, ranks), "pack",
        shape((tokens, width + model + LANES), BF16),
        (features, out_cotangent, decay_rate, input_proj, read_proj),
        [pltpu.VMEM((LANES, tokens), F32)],
        flops=2 * tokens * tokens * (width + model), moved=4 * tokens * (width + model), grant=None,
    )
    received = exchange(packed)
    skip_shape = (1, width) if chunk is None else (chunk, LANES)
    lines = columns // ranks
    tables = Tables(slots, lines, tokens, width)
    gx_rows, small_rows, partial, skip_part, *table = call(
        functools.partial(rows_kernel, slots, chunk, tables), "rows",
        (
            shape((tokens, width), F32),
            shape((LANES, tokens), F32),
            shape((width, model), F32),
            shape(skip_shape, F32),
            *(shape(sizes, BF16) for sizes in tables.shapes),
        ),
        (
            features, out_cotangent, out_weight, skip_gain.reshape(1, width),
            decay_rate, input_proj, read_proj,
        ),
        [pltpu.VMEM((LANES, columns), F32)],
        flops=2 * tokens * width * (2 * model + 3 * columns), moved=8 * tokens * width,
    )
    half = width // 2
    partners = [(rank, rank ^ 1) for rank in range(ranks)]
    mine, other = call(
        functools.partial(forward_kernel, slots, lines), "forward",
        (
            shape((half, model), F32),
            shape((half, model), BF16),
        ),
        (received, partial, *table),
        flops=2 * tokens * width * (2 * model + columns), moved=8 * tokens * width,
    )
    theirs = lax.ppermute(other, "row", partners)
    back = call(
        functools.partial(backward_kernel, slots, ranks, lines, chunk), "backward",
        shape((tokens, width + LANES), BF16), (received, out_weight, skip_part, *table),
        [pltpu.VMEM((LANES, tokens), F32)],
        flops=2 * tokens * width * (2 * model + 3 * columns), moved=8 * tokens * width,
    )
    group = tokens // ranks
    size = Tiles(half, model, ranks).size
    strips = width // LANES + 1
    early = strips // 2
    merged = call(
        functools.partial(merge_kernel, ranks, early), "merge",
        shape((ranks, early * group + size, LANES), BF16), (mine, theirs, back),
        flops=width * model, moved=2 * width * model,
    )
    returned = exchange(merged)
    summed = call(
        functools.partial(sum_kernel, early, size), "sum",
        shape((ranks, (strips - early) * group + size, LANES), BF16), (returned, back),
        flops=width * model, moved=2 * width * model,
    )
    last = exchange(summed)
    held = call(
        half_kernel, "half", shape((ranks, size, LANES), BF16), (last,),
        flops=width * model, moved=2 * width * model,
    )
    swapped = lax.ppermute(held, "row", partners)
    outs = [
        shape(features.shape, BF16),
        shape(decay_rate.shape, F32),
        shape(input_proj.shape, F32),
        shape(read_proj.shape, F32),
    ]
    if chunk is not None:
        outs.append(shape((width,), F32))
    done = call(
        functools.partial(finish_kernel, slots, ranks, chunk, early), "finish",
        tuple(outs), (returned, last, gx_rows, small_rows),
        flops=2 * tokens * tokens * width, moved=8 * tokens * width,
    )
    grad_weight = call(
        weight_kernel, "weight", shape((width, model), F32), (held, swapped),
        flops=width * model, moved=6 * width * model,
    )
    if chunk is None:
        grad_skip = lax.psum(skip_part, "row").reshape(width)
    else:
        grad_skip = done[4]
    return (*done[:4], grad_skip, grad_weight)


def solution(mesh):
    in_specs = (
        P(("grp", "row"), None, None),
        P(None, None, ("grp", "row"), None),
        P(None, None, ("grp", "row"), None),
        P(None, None, ("grp", "row"), None),
        P(),
        P(),
        P(("grp", "row"), None, None),
    )
    out_specs = (
        P(("grp", "row"), None, None),
        P(None, None, ("grp", "row"), None),
        P(None, None, ("grp", "row"), None),
        P(None, None, ("grp", "row"), None),
        P("grp"),
        P("grp", None),
    )
    body = functools.partial(local, mesh.shape["row"])
    return jax.shard_map(body, mesh=mesh, in_specs=in_specs, out_specs=out_specs, check_vma=False)
```

```python
import functools

import jax
import jax.numpy as jnp
from jax import lax
from jax.experimental import pallas as pl
from jax.experimental.pallas import tpu as pltpu
from jax.sharding import PartitionSpec as P

F32 = jnp.float32
BF16 = jnp.bfloat16
HI = lax.Precision.HIGHEST
LANES = 128
FAR = -1e30
VMEM_GRANT = 16 << 20


def iota(shape, dim):
    return lax.broadcasted_iota(jnp.int32, shape, dim)


def nt(a, b):
    return lax.dot_general(a, b, (((1,), (1,)), ((), ())), preferred_element_type=F32)


def nn(a, b):
    return jnp.dot(a, b, preferred_element_type=F32)


def tn(a, b):
    return lax.dot_general(a, b, (((0,), (0,)), ((), ())), preferred_element_type=F32)


def split_index(index, sizes):
    parts = []
    for size in reversed(sizes):
        if size & (size - 1) == 0:
            parts.append(index & (size - 1))
            index = index >> (size.bit_length() - 1)
        else:
            parts.append(lax.rem(index, size))
            index = lax.div(index, size)
    return parts[::-1]


class Slots:
    def __init__(self, heads, states):
        self.heads = heads
        self.states = states
        self.inputs = (0, states)
        self.reads = (2 * states, 3 * states)
        pad = -(-heads // 8) * 8
        self.pad = pad
        self.rates = (4 * states, 4 * states + pad)
        self.lows = (4 * states + 2 * pad, 4 * states + 3 * pad)
        self.used = 4 * states + 2 * pad


class Lines:
    def __init__(self, rows, rates, slots, lines, block):
        at_t, at_u = iota((block, block), 0), iota((block, block), 1)
        self.same = None
        if lines > 1:
            at_t, line_t = split_index(at_t, (block // lines, lines))
            at_u, line_u = split_index(at_u, (block // lines, lines))
            self.same = line_t == line_u
        self.below, self.above = at_t > at_u, at_t < at_u
        self.till = self.within(at_t <= at_u)
        self.since = self.within(at_t >= at_u)
        self.sums = (
            -jnp.dot(rates[0], self.till.astype(F32), precision=HI, preferred_element_type=F32),
            -jnp.dot(rates[1], self.since.astype(F32), precision=HI, preferred_element_type=F32),
        )
        self.columns = jnp.transpose(jnp.concatenate(self.sums, axis=0))
        self.inputs = [rows[at : at + slots.states].astype(BF16) for at in slots.inputs]
        self.reads = [rows[at : at + slots.states].astype(BF16) for at in slots.reads]
        down, up = (tn(self.reads[way], self.inputs[way]) for way in (0, 1))
        self.scores = jnp.where(self.below, down, jnp.where(self.above, up, down + up))
        self.pad = slots.pad

    def within(self, mask):
        return mask if self.same is None else mask & self.same

    def kernel(self, head):
        up = self.pad + head
        spread = jnp.where(
            self.below,
            self.columns[:, head : head + 1] - self.sums[0][head : head + 1],
            self.columns[:, up : up + 1] - self.sums[1][head : head + 1],
        )
        if self.same is not None:
            spread = jnp.where(self.same, spread, FAR)
        return jnp.exp(spread)


def head_mask(block, head_size, member):
    lane = iota((block, LANES), 1)
    return (lane >= member * head_size) & (lane < (member + 1) * head_size)


def scan_block(feats, grads, lines, slots, small_ref, row_slice, forward, backward):
    block = feats.shape[0]
    heads = slots.heads
    head_size = feats.shape[1] // heads
    per_group = LANES // head_size
    below = lines.below
    grad_scores = jnp.zeros((block, block), F32)
    out_parts, grad_parts = [], []
    lane_pad = iota((block, LANES), 1)
    row_sums = jnp.zeros((block, LANES), F32)
    row_at = iota((2 * slots.pad, block), 0)
    col_sums = jnp.zeros((2 * slots.pad, block), F32)
    for group in range(heads // per_group):
        span = slice(group * LANES, (group + 1) * LANES)
        feat_group = feats[:, span]
        grad_group = grads[:, span] if backward else None
        mixes, feat_own, grad_own = [], [], []
        for member in range(per_group):
            head = group * per_group + member
            up = slots.pad + head
            mine = head_mask(block, head_size, member)
            feat_head = jnp.where(mine, feat_group, jnp.zeros_like(feat_group))
            kernel = lines.kernel(head)
            mix = kernel * lines.scores
            mixes.append(mix.astype(BF16))
            feat_own.append(feat_head)
            if not backward:
                continue
            grad_own.append(jnp.where(mine, grad_group, jnp.zeros_like(grad_group)))
            grad_mix = nt(grad_group, feat_head)
            grad_scores = grad_scores + kernel * grad_mix
            flow = mix * grad_mix
            flow_down = jnp.where(below, flow, 0.0)
            row_down = jnp.sum(flow_down, axis=1, keepdims=True)
            row_all = jnp.sum(flow, axis=1, keepdims=True)
            col_down = jnp.sum(flow_down, axis=0, keepdims=True)
            col_all = jnp.sum(flow, axis=0, keepdims=True)
            row_sums = jnp.where(lane_pad == head, row_down, row_sums)
            row_sums = jnp.where(lane_pad == up, row_all - row_down, row_sums)
            col_sums = jnp.where(row_at == head, col_down, col_sums)
            col_sums = jnp.where(row_at == up, col_all - col_down, col_sums)
        if forward:
            out_parts.append(
                nn(jnp.concatenate(mixes, axis=1), jnp.concatenate(feat_own, axis=0))
            )
        if backward:
            grad_parts.append(
                tn(jnp.concatenate(mixes, axis=0), jnp.concatenate(grad_own, axis=0))
            )
    out = jnp.concatenate(out_parts, axis=1) if forward else None
    if not backward:
        return out, None
    change = col_sums - jnp.transpose(row_sums)[: 2 * slots.pad]
    reach = (lines.since, lines.till)
    for way in (0, 1):
        score_grad = jnp.where(reach[way], grad_scores, 0.0).astype(BF16)
        at = slots.inputs[way]
        small_ref[at : at + slots.states, row_slice] = nn(lines.reads[way], score_grad)
        at = slots.reads[way]
        small_ref[at : at + slots.states, row_slice] = nt(lines.inputs[way], score_grad)
        at = slots.rates[way]
        part = change[way * slots.pad : (way + 1) * slots.pad]
        small_ref[at : at + slots.pad, row_slice] = jnp.dot(
            part, reach[way].astype(F32), precision=HI, preferred_element_type=F32
        )
    return out, jnp.concatenate(grad_parts, axis=1)


def by_rank(array, ranks):
    narrow = array[0].shape[0] // ranks
    return [
        jnp.concatenate([row[rank * narrow : (rank + 1) * narrow] for row in array], axis=0)
        for rank in range(ranks)
    ]


def pack_kernel(slots, ranks, feat_ref, cot_ref, rate_ref, input_ref, read_ref, out_ref, rows_ref):
    tile_rows, columns, width = feat_ref.shape
    model = cot_ref.shape[2]
    group = tile_rows * columns // ranks
    rows_ref[...] = jnp.zeros_like(rows_ref)
    for way in (0, 1):
        for row in range(tile_rows):
            span = slice(row * columns, (row + 1) * columns)
            at = slots.inputs[way]
            rows_ref[at : at + slots.states, span] = input_ref[2 + way, :, row, :]
            at = slots.reads[way]
            rows_ref[at : at + slots.states, span] = read_ref[2 + way, :, row, :]
            at = slots.rates[way]
            rate = rate_ref[2 + way, :, row, :]
            rows_ref[at : at + slots.heads, span] = rate
            at = slots.lows[way]
            rows_ref[at : at + slots.heads, span] = rate - rate.astype(BF16).astype(F32)
    values = [
        (0, [feat_ref[row].astype(F32) for row in range(tile_rows)]),
        (width, [cot_ref[row].astype(F32) for row in range(tile_rows)]),
        (
            width + model,
            [
                jnp.transpose(rows_ref[:, row * columns : (row + 1) * columns])
                for row in range(tile_rows)
            ],
        ),
    ]
    for lane, array in values:
        for rank, piece in enumerate(by_rank(array, ranks)):
            out_ref[rank * group : (rank + 1) * group, lane : lane + piece.shape[1]] = (
                piece.astype(BF16)
            )


def rows_kernel(
    slots, chunk, tables, feat_ref, cot_ref, weight_ref, skip_ref, rate_ref, input_ref, read_ref,
    gx_ref, small_ref, part_ref, skip_out_ref, *refs,
):
    *table_refs, rows_ref = refs
    tables.fill(table_refs)
    tile_rows, columns, width = feat_ref.shape
    tokens = tile_rows * columns
    skip = skip_ref[...]
    rows_ref[...] = jnp.zeros_like(rows_ref)
    partial = jnp.zeros(part_ref.shape, F32)
    skip_part = jnp.zeros((1, width), F32)
    for row in range(tile_rows):
        feats, cots = feat_ref[row], cot_ref[row]
        grads = nt(cots, weight_ref[...]).astype(BF16)
        for way in (0, 1):
            at = slots.inputs[way]
            rows_ref[at : at + slots.states, :] = input_ref[way, :, row, :]
            at = slots.reads[way]
            rows_ref[at : at + slots.states, :] = read_ref[way, :, row, :]
            at = slots.rates[way]
            rows_ref[at : at + slots.heads, :] = rate_ref[way, :, row, :]
        rates = [rows_ref[at : at + slots.pad, :] for at in slots.rates]
        lines = Lines(rows_ref, rates, slots, 1, columns)
        outs, gx = scan_block(
            feats, grads, lines, slots, small_ref,
            slice(row * columns, (row + 1) * columns), True, True,
        )
        feat_f32, grad_f32 = feats.astype(F32), grads.astype(F32)
        across = (outs + skip * feat_f32).astype(BF16)
        partial = partial + tn(across, cots)
        gx_ref[row * columns : (row + 1) * columns, :] = gx + skip * grad_f32
        skip_part = skip_part + jnp.sum(feat_f32 * grad_f32, axis=0, keepdims=True)
    part_ref[...] = partial
    if chunk is None:
        skip_out_ref[...] = skip_part
    else:
        high = skip_part.astype(BF16).astype(F32)
        piece = width // chunk
        lane_of = iota((chunk, width), 1)
        start = iota((chunk, width), 0) * piece
        owned = (lane_of >= start) & (lane_of < start + piece)
        spread = jnp.concatenate(
            [jnp.where(owned, high, 0.0), jnp.where(owned, skip_part - high, 0.0)], axis=1
        ).astype(BF16)
        skip_out_ref[...] = nn(spread, skip_places(slots, width, piece))


def skip_places(slots, width, piece):
    at = iota((width, 1), 0)
    whole = ((at.astype(F32) + 0.5) * (1.0 / piece)).astype(jnp.int32)
    place = at - whole * piece + slots.used
    lane = iota((width, LANES), 1)
    high, low = place == lane, place + piece == lane
    return jnp.concatenate([high.astype(F32), low.astype(F32)], axis=0).astype(BF16)


def long_lines(params, slots, lines):
    rows = jnp.transpose(params.astype(F32))
    rates = [
        rows[hi : hi + slots.pad] + rows[lo : lo + slots.pad]
        for hi, lo in zip(slots.rates, slots.lows)
    ]
    return Lines(rows, rates, slots, lines, params.shape[0])


def halves_of(array):
    high = array.astype(BF16)
    return high, (array - high.astype(F32)).astype(BF16)


def reach_of(lines, block):
    at_t, line_t = split_index(iota((block, block), 0), (block // lines, lines))
    at_u, line_u = split_index(iota((block, block), 1), (block // lines, lines))
    same = line_t == line_u
    return same, (same & (at_t >= at_u), same & (at_t <= at_u))


class Tables:
    def __init__(self, slots, lines, tokens, width):
        self.slots, self.lines, self.tokens, self.width = slots, lines, tokens, width
        self.short = tokens // lines <= LONGEST_SHORT
        self.shapes = []
        self.kept = []
        if self.short:
            values = ((2, tokens, width), F32)
            self.kept = [
                ((2, tokens, 2 * LANES), BF16), ((2, tokens, width), BF16), values,
                ((2, tokens, tokens), BF16),
            ]
            self.shapes = [(2 * tokens, tokens), (2 * LANES, 2 * width), (4 * width, LANES)]

    def fill(self, refs):
        if not self.short:
            return
        slots, width, tokens = self.slots, self.width, self.tokens
        size = width // slots.heads
        same, reach = reach_of(self.lines, tokens)
        half = jnp.where(same, 0.5, 0.0)
        for way in (0, 1):
            refs[0][way * tokens : (way + 1) * tokens, :] = (
                reach[way].astype(F32) - half
            ).astype(BF16)
            at = iota((LANES, width), 0)
            head = split_index(iota((LANES, width), 1), (slots.heads, size))[0]
            spread = (at == head + slots.rates[way]).astype(F32).astype(BF16)
            lanes = slice(way * width, (way + 1) * width)
            refs[1][:LANES, lanes] = spread
            refs[1][LANES:, lanes] = spread
            at = iota((width, LANES), 1)
            head = split_index(iota((width, LANES), 0), (slots.heads, size))[0]
            gather = (at == head + slots.rates[way]).astype(F32).astype(BF16)
            refs[2][2 * way * width : (2 * way + 1) * width, :] = gather
            refs[2][(2 * way + 1) * width : (2 * way + 2) * width, :] = gather


class ShortLines:
    def __init__(self, params, slots, lines, tables):
        self.slots, self.tables, self.params = slots, tables, params
        tokens = self.tokens = params.shape[0]
        self.reach = reach_of(lines, tokens)[1]
        self.lane = lane = iota((tokens, LANES), 1)
        self.up_lane = ((lane >= slots.rates[1]) & (lane < slots.lows[0])) | (
            lane >= slots.lows[1]
        )
        states = slots.states
        wide = params.astype(F32)
        turned = pltpu.roll(wide, LANES - slots.reads[0], 1)
        first, second = lane < states, (lane >= states) & (lane < 2 * states)
        self.inputs = [jnp.where(mask, wide, 0.0).astype(BF16) for mask in (first, second)]
        self.reads = [jnp.where(mask, turned, 0.0).astype(BF16) for mask in (first, second)]

    def factors(self, width, narrows):
        spread = self.tables[1][...]
        pairs = [nn(narrows[at], spread) for at in (0, 1)]
        return [(pair[:, :width], pair[:, width:]) for pair in pairs]

    def forward(self, feats, kept):
        slots, tokens, lane = self.slots, self.tokens, self.lane
        width = feats.shape[1]
        narrows, lost, mixed, scores = kept
        sums = nn(self.tables[0][...], self.params)
        sums = jnp.where(self.up_lane, sums[tokens:], sums[:tokens])
        sums = sums + pltpu.roll(sums, LANES - (slots.lows[0] - slots.rates[0]), 1)
        rated = (lane >= slots.rates[0]) & (lane < slots.lows[0])
        sums = jnp.where(rated, sums, 0.0)
        for at, narrow in enumerate((jnp.exp(sums), jnp.exp(-sums))):
            narrows[at] = jnp.concatenate(halves_of(narrow), axis=1)
        losses, gains = self.factors(width, narrows)
        wide = feats.astype(F32)
        out = None
        for way in (0, 1):
            score = jnp.where(self.reach[way], nt(self.reads[way], self.params), 0.0).astype(BF16)
            scores[way] = score
            held = (wide * losses[way]).astype(BF16)
            lost[way] = held
            mix = nn(score, held)
            mixed[way] = mix
            part = gains[way] * mix
            out = part if out is None else out + part
        return out

    def backward(self, grads, kept):
        slots = self.slots
        width = grads.shape[1]
        narrows, lost, mixed, scores = kept
        losses, gains = self.factors(width, narrows)
        wide = grads.astype(F32)
        gx = heads = read_grads = input_grads = 0.0
        for way in (0, 1):
            gained = (wide * gains[way]).astype(BF16)
            back = tn(scores[way], gained)
            gx = gx + losses[way] * back
            held = lost[way]
            score_grad = jnp.where(self.reach[way], nt(gained, held), 0.0).astype(BF16)
            change = held.astype(F32) * back - gained.astype(F32) * mixed[way]
            places = self.tables[2][2 * way * width : 2 * (way + 1) * width, :]
            heads = heads + nn(jnp.concatenate(halves_of(change), axis=1), places)
            read_grads = read_grads + nn(score_grad, self.inputs[way])
            input_grads = input_grads + tn(score_grad, self.reads[way])
        since, till = (mask.astype(F32).astype(BF16) for mask in self.reach)
        both = jnp.concatenate(halves_of(heads), axis=1)
        down, up = nn(till, both), nn(since, both)
        rates = jnp.where(
            self.up_lane, up[:, :LANES] + up[:, LANES:], down[:, :LANES] + down[:, LANES:]
        )
        smalls = input_grads + pltpu.roll(read_grads, slots.reads[0], 1)
        return gx, jnp.where(self.lane >= slots.rates[0], rates, smalls)


LONGEST_SHORT = 32


def forward_kernel(slots, lines, sizes, recv_ref, part_ref, *refs):
    tables, refs = refs[: len(sizes.shapes)], refs[len(sizes.shapes) :]
    mine_ref, other_ref, *kept = refs
    width, model = part_ref.shape
    tokens = recv_ref.shape[0]
    feats, cots = recv_ref[:, :width], recv_ref[:, width : width + model]
    params = recv_ref[:, width + model :]
    if sizes.short:
        down = ShortLines(params, slots, lines, tables).forward(feats, kept)
    else:
        masks = long_lines(params, slots, lines)
        down = scan_block(feats, None, masks, slots, None, None, True, False)[0]
    total = part_ref[...] + tn(down.astype(BF16), cots)
    even = lax.rem(lax.axis_index("row"), 2) == 0
    half = width // 2
    mine_ref[...] = jnp.where(even, total[:half], total[half:])
    other_ref[...] = jnp.where(even, total[half:], total[:half]).astype(BF16)


def backward_kernel(slots, ranks, lines, chunk, sizes, recv_ref, weight_ref, skip_ref, *refs):
    tables, refs = refs[: len(sizes.shapes)], refs[len(sizes.shapes) :]
    *kept, back_ref, small_ref = refs
    width, model = weight_ref.shape
    tokens = recv_ref.shape[0]
    feats = recv_ref[:, :width]
    params = recv_ref[:, width + model :]
    grads = nt(recv_ref[:, width : width + model], weight_ref[...]).astype(BF16)
    if sizes.short:
        gx, small = ShortLines(params, slots, lines, tables).backward(grads, kept)
    else:
        small_ref[...] = jnp.zeros_like(small_ref)
        masks = long_lines(params, slots, lines)
        span = slice(0, tokens)
        gx = scan_block(feats, grads, masks, slots, small_ref, span, False, True)[1]
        small = jnp.transpose(small_ref[...])
    back_ref[:, :width] = gx.astype(BF16)
    if chunk is not None:
        small = small + jnp.concatenate([skip_ref[...]] * ranks, axis=0)
    back_ref[:, width:] = small.astype(BF16)


def strip(array):
    return [array[:, at : at + LANES] for at in range(0, array.shape[1], LANES)]


class Tiles:
    def __init__(self, rows, model, ranks, group):
        self.unit = unit = 8
        steps = rows // unit
        self.places = [(at * unit, lane) for lane in range(0, model, LANES) for at in range(steps)]
        count = len(self.places)
        per = 2 * count // ranks
        self.split = 2 * count % ranks == 0 and per % 2 == 1 and ranks % 2 == 0 and group > 4
        self.per = per
        self.full = per // 2 if self.split else -(-count // ranks)
        self.starts = [count * rank // ranks for rank in range(ranks + 1)]
        self.moved = unit // 2 if self.split else 0
        self.size = unit * (self.full + self.split)

    def of(self, rank):
        if not self.split:
            return self.places[self.starts[rank] : self.starts[rank + 1]]
        first = self.per * (rank // 2) + (rank % 2) * (self.full + 1)
        return self.places[first : first + self.full]

    def shared(self, rank):
        return self.places[self.per * (rank // 2) + self.full]


def lay_out(out_ref, rank, pieces):
    at = 0
    for piece in pieces:
        out_ref[rank, at : at + piece.shape[0], :] = piece
        at += piece.shape[0]


def merge_kernel(ranks, early, mine_ref, theirs_ref, back_ref, out_ref):
    total = mine_ref[...] + theirs_ref[...].astype(F32)
    group = back_ref.shape[0] // ranks
    tiles = Tiles(*mine_ref.shape, ranks, group)
    unit = tiles.unit
    for rank in range(ranks):
        pieces = strip(back_ref[rank * group : (rank + 1) * group, :])
        blocks = [
            total[row : row + unit, lane : lane + LANES].astype(BF16)
            for row, lane in tiles.of(rank)
        ]
        blocks += [jnp.zeros((unit, LANES), BF16)] * (tiles.full - len(blocks))
        if tiles.split:
            row, lane = tiles.shared(rank)
            half = unit // 2
            row += (rank % 2) * half
            moved = pieces[-1].astype(F32)[group - tiles.moved :]
            blocks.append(
                jnp.concatenate([total[row : row + half, lane : lane + LANES], moved], axis=0)
                .astype(BF16)
            )
        lay_out(out_ref, rank, pieces[:early] + blocks)


def sum_kernel(early, recv_ref, back_ref, out_ref, tiles):
    ranks = out_ref.shape[0]
    group = back_ref.shape[0] // ranks
    unit = tiles.unit
    own = slice(recv_ref.shape[1] - tiles.size, recv_ref.shape[1])
    whole = tiles.full * unit
    for half in (0, 1):
        total = recv_ref[half, own, :].astype(F32)
        for rank in range(half + 2, ranks, 2):
            total = total + recv_ref[rank, own, :].astype(F32)
        for rank in range(half, ranks, 2):
            pieces = strip(back_ref[rank * group : (rank + 1) * group, :])
            small = pieces[-1]
            if tiles.split:
                small = jnp.concatenate(
                    [total[whole : whole + unit // 2], small.astype(F32)[: group - tiles.moved]],
                    axis=0,
                ).astype(BF16)
            lay_out(out_ref, rank, pieces[early:-1] + [total[:whole].astype(BF16), small])


def half_kernel(start, recv_ref, out_ref):
    out_ref[...] = recv_ref[:, start : start + out_ref.shape[1], :]


def widen_half(halves_ref, store, tiles):
    ranks = halves_ref.shape[0]
    unit = tiles.unit
    for rank in range(ranks):
        for step, (row, lane) in enumerate(tiles.of(rank)):
            store(row, lane, halves_ref[rank, step * unit : (step + 1) * unit, :].astype(F32))
    if tiles.split:
        at = tiles.full * unit
        for rank in range(0, ranks, 2):
            pair = [
                halves_ref[rank + side, at : at + unit, :].astype(F32)[: unit // 2]
                for side in (0, 1)
            ]
            store(*tiles.shared(rank), jnp.concatenate(pair, axis=0))


def weight_kernel(tiles, theirs_ref, weight_in, weight_out, wide_ref, done):
    rows, model = wide_ref.shape

    def store(row, lane, block):
        wide_ref[row : row + block.shape[0], lane : lane + LANES] = block

    widen_half(theirs_ref, store, tiles)
    half = lax.rem(lax.axis_index("row") + 1, 2)
    start = pl.multiple_of(half * rows, 8)
    copy = pltpu.make_async_copy(wide_ref, weight_out.at[pl.ds(start, rows), :], done)
    copy.start()
    copy.wait()


def finish_kernel(
    slots, ranks, chunk, early, tiles, early_ref, late_ref, gx_ref, small_ref, held_ref,
    weight_out, feat_out, rate_out, input_out, read_out, *skip_out,
):
    rows = weight_out.shape[0] // 2
    start = pl.multiple_of(lax.rem(lax.axis_index("row"), 2) * rows, 8)

    def store(row, lane, block):
        weight_out[pl.ds(start + row, block.shape[0]), lane : lane + LANES] = block

    widen_half(held_ref, store, tiles)
    tile_rows, columns, width = feat_out.shape
    narrow = columns // ranks
    group = tile_rows * narrow
    lanes = width // LANES

    def part_of(part):
        ref, part = (early_ref, part) if part < early else (late_ref, part - early)
        return ref[:, part * group : (part + 1) * group, :].astype(F32)

    def row_of(array, row):
        return jnp.concatenate(
            [array[rank, row * narrow : (row + 1) * narrow] for rank in range(ranks)], axis=0
        )

    for part in range(lanes):
        lane = slice(part * LANES, (part + 1) * LANES)
        back = part_of(part)
        for row in range(tile_rows):
            span = slice(row * columns, (row + 1) * columns)
            feat_out[row, :, lane] = (gx_ref[span, lane] + row_of(back, row)).astype(BF16)
    back = late_ref[:, late_ref.shape[1] - group :, :].astype(F32)
    if tiles.split:
        tail = early_ref[:, early_ref.shape[1] - tiles.unit :, :].astype(F32)
        back = jnp.concatenate([back[:, tiles.moved :], tail[:, tiles.unit - tiles.moved :]], axis=1)
    for row in range(tile_rows):
        span = slice(row * columns, (row + 1) * columns)
        held = jnp.transpose(row_of(back, row))
        for way in (0, 1):
            at = slots.inputs[way]
            input_out[way, :, row, :] = small_ref[at : at + slots.states, span]
            input_out[2 + way, :, row, :] = held[at : at + slots.states]
            at = slots.reads[way]
            read_out[way, :, row, :] = small_ref[at : at + slots.states, span]
            read_out[2 + way, :, row, :] = held[at : at + slots.states]
            at = slots.rates[way]
            rate_out[way, :, row, :] = small_ref[at : at + slots.heads, span]
            rate_out[2 + way, :, row, :] = held[at : at + slots.heads]
    if chunk is not None:
        piece = width // chunk
        gathered = jnp.sum(back, axis=0)
        places = skip_places(slots, width, piece)
        places = places[:width] + places[width:]
        high, low = halves_of(gathered)
        spread = nt(high, places) + nt(low, places)
        lane_of = iota((chunk, width), 1)
        start = iota((chunk, width), 0) * piece
        owned = (lane_of >= start) & (lane_of < start + piece)
        skip_out[0][...] = jnp.sum(jnp.where(owned, spread, 0.0), axis=0)


def call(
    kernel, name, out_shape, operands, scratch=(), flops=0, moved=0, grant=VMEM_GRANT,
    whole=(), aliases=None,
):
    def spec(side, at):
        return pl.BlockSpec(memory_space=pl.ANY if (side, at) in whole else pltpu.VMEM)

    many = isinstance(out_shape, tuple)
    outs = tuple(spec("out", at) for at in range(len(out_shape) if many else 1))
    return pl.pallas_call(
        kernel,
        name=name,
        out_shape=out_shape,
        in_specs=[spec("in", at) for at in range(len(operands))],
        out_specs=outs if many else outs[0],
        scratch_shapes=list(scratch),
        input_output_aliases=aliases or {},
        compiler_params=pltpu.CompilerParams(vmem_limit_bytes=grant),
        cost_estimate=pl.CostEstimate(flops=flops, bytes_accessed=moved, transcendentals=0),
    )(*operands)


def local(ranks, features, decay_rate, input_proj, read_proj, skip_gain, out_weight, out_cotangent):
    tile_rows, columns, width = features.shape
    model = out_cotangent.shape[2]
    heads, states = decay_rate.shape[1], input_proj.shape[1]
    slots = Slots(heads, states)
    tokens = tile_rows * columns
    chunk = tokens // ranks
    room = chunk * (LANES - slots.used)
    if chunk % 8 or width % chunk or 2 * width > room:
        chunk = None
    shape = jax.ShapeDtypeStruct

    def exchange(array):
        return lax.all_to_all(array, "row", split_axis=0, concat_axis=0, tiled=True)

    packed = call(
        functools.partial(pack_kernel, slots, ranks), "pack",
        shape((tokens, width + model + LANES), BF16),
        (features, out_cotangent, decay_rate, input_proj, read_proj),
        [pltpu.VMEM((LANES, tokens), F32)],
        flops=2 * tokens * tokens * (width + model), moved=4 * tokens * (width + model), grant=None,
    )
    received = exchange(packed)
    skip_shape = (1, width) if chunk is None else (chunk, LANES)
    lines = columns // ranks
    tables = Tables(slots, lines, tokens, width)
    gx_rows, small_rows, partial, skip_part, *table = call(
        functools.partial(rows_kernel, slots, chunk, tables), "rows",
        (
            shape((tokens, width), F32),
            shape((LANES, tokens), F32),
            shape((width, model), F32),
            shape(skip_shape, F32),
            *(shape(sizes, BF16) for sizes in tables.shapes),
        ),
        (
            features, out_cotangent, out_weight, skip_gain.reshape(1, width),
            decay_rate, input_proj, read_proj,
        ),
        [pltpu.VMEM((LANES, columns), F32)],
        flops=2 * tokens * width * (2 * model + 3 * columns), moved=8 * tokens * width,
    )
    half = width // 2
    partners = [(rank, rank ^ 1) for rank in range(ranks)]
    mine, other, *kept = call(
        functools.partial(forward_kernel, slots, lines, tables), "forward",
        (
            shape((half, model), F32),
            shape((half, model), BF16),
            *(shape(*leaf) for leaf in tables.kept),
        ),
        (received, partial, *table),
        flops=2 * tokens * width * (2 * model + columns), moved=8 * tokens * width,
    )
    theirs = lax.ppermute(other, "row", partners)
    back = call(
        functools.partial(backward_kernel, slots, ranks, lines, chunk, tables), "backward",
        shape((tokens, width + LANES), BF16), (received, out_weight, skip_part, *table, *kept),
        [pltpu.VMEM((LANES, tokens), F32)],
        flops=2 * tokens * width * (2 * model + 3 * columns), moved=8 * tokens * width,
    )
    group = tokens // ranks
    tiles = Tiles(half, model, ranks, group)
    strips = width // LANES + 1
    early = strips // 2
    merged = call(
        functools.partial(merge_kernel, ranks, early), "merge",
        shape((ranks, early * group + tiles.size, LANES), BF16), (mine, theirs, back),
        flops=width * model, moved=2 * width * model,
    )
    returned = exchange(merged)
    whole = tiles.full * tiles.unit
    late_rows = (strips - early) * group + whole
    summed = call(
        functools.partial(sum_kernel, early, tiles=tiles), "sum",
        shape((ranks, late_rows, LANES), BF16), (returned, back),
        flops=width * model, moved=2 * width * model,
    )
    last = exchange(summed)
    held = call(
        functools.partial(half_kernel, (strips - early - 1) * group), "half",
        shape((ranks, tiles.size, LANES), BF16), (last,),
        flops=width * model, moved=2 * width * model,
    )
    swapped = lax.ppermute(held, "row", partners)
    outs = [
        shape((width, model), F32),
        shape(features.shape, BF16),
        shape(decay_rate.shape, F32),
        shape(input_proj.shape, F32),
        shape(read_proj.shape, F32),
    ]
    if chunk is not None:
        outs.append(shape((width,), F32))
    done = call(
        functools.partial(finish_kernel, slots, ranks, chunk, early, tiles), "finish",
        tuple(outs), (returned, last, gx_rows, small_rows, held),
        flops=2 * tokens * tokens * width, moved=8 * tokens * width,
    )
    grad_weight = call(
        functools.partial(weight_kernel, tiles), "weight", shape((width, model), F32),
        (swapped, done[0]),
        [pltpu.VMEM((half, model), F32), pltpu.SemaphoreType.DMA(())],
        flops=width * model, moved=6 * width * model,
        whole=[("in", 1), ("out", 0)], aliases={1: 0},
    )
    if chunk is None:
        grad_skip = lax.psum(skip_part, "row").reshape(width)
    else:
        grad_skip = done[5]
    return (*done[1:5], grad_skip, grad_weight)


def solution(mesh):
    in_specs = (
        P(("grp", "row"), None, None),
        P(None, None, ("grp", "row"), None),
        P(None, None, ("grp", "row"), None),
        P(None, None, ("grp", "row"), None),
        P(),
        P(),
        P(("grp", "row"), None, None),
    )
    out_specs = (
        P(("grp", "row"), None, None),
        P(None, None, ("grp", "row"), None),
        P(None, None, ("grp", "row"), None),
        P(None, None, ("grp", "row"), None),
        P("grp"),
        P("grp", None),
    )
    body = functools.partial(local, mesh.shape["row"])
    return jax.shard_map(body, mesh=mesh, in_specs=in_specs, out_specs=out_specs, check_vma=False)
```

```python
import functools

import jax
import jax.numpy as jnp
from jax import lax
from jax.experimental import pallas as pl
from jax.experimental.pallas import tpu as pltpu
from jax.sharding import PartitionSpec as P

F32 = jnp.float32
BF16 = jnp.bfloat16
HI = lax.Precision.HIGHEST
LANES = 128
FAR = -1e30
VMEM_GRANT = 16 << 20


def iota(shape, dim):
    return lax.broadcasted_iota(jnp.int32, shape, dim)


def nt(a, b):
    return lax.dot_general(a, b, (((1,), (1,)), ((), ())), preferred_element_type=F32)


def nn(a, b):
    return jnp.dot(a, b, preferred_element_type=F32)


def tn(a, b):
    return lax.dot_general(a, b, (((0,), (0,)), ((), ())), preferred_element_type=F32)


def split_index(index, sizes):
    parts = []
    for size in reversed(sizes):
        if size & (size - 1) == 0:
            parts.append(index & (size - 1))
            index = index >> (size.bit_length() - 1)
        else:
            parts.append(lax.rem(index, size))
            index = lax.div(index, size)
    return parts[::-1]


class Slots:
    def __init__(self, heads, states):
        self.heads = heads
        self.states = states
        self.inputs = (0, states)
        self.reads = (2 * states, 3 * states)
        pad = -(-heads // 8) * 8
        self.pad = pad
        self.rates = (4 * states, 4 * states + pad)
        self.lows = (4 * states + 2 * pad, 4 * states + 3 * pad)
        self.used = 4 * states + 2 * pad


class Lines:
    def __init__(self, rows, rates, slots, lines, block):
        at_t, at_u = iota((block, block), 0), iota((block, block), 1)
        self.same = None
        if lines > 1:
            at_t, line_t = split_index(at_t, (block // lines, lines))
            at_u, line_u = split_index(at_u, (block // lines, lines))
            self.same = line_t == line_u
        self.below, self.above = at_t > at_u, at_t < at_u
        self.till = self.within(at_t <= at_u)
        self.since = self.within(at_t >= at_u)
        self.sums = (
            -jnp.dot(rates[0], self.till.astype(F32), precision=HI, preferred_element_type=F32),
            -jnp.dot(rates[1], self.since.astype(F32), precision=HI, preferred_element_type=F32),
        )
        self.columns = jnp.transpose(jnp.concatenate(self.sums, axis=0))
        self.inputs = [rows[at : at + slots.states].astype(BF16) for at in slots.inputs]
        self.reads = [rows[at : at + slots.states].astype(BF16) for at in slots.reads]
        down, up = (tn(self.reads[way], self.inputs[way]) for way in (0, 1))
        self.scores = jnp.where(self.below, down, jnp.where(self.above, up, down + up))
        self.pad = slots.pad

    def within(self, mask):
        return mask if self.same is None else mask & self.same

    def kernel(self, head):
        up = self.pad + head
        spread = jnp.where(
            self.below,
            self.columns[:, head : head + 1] - self.sums[0][head : head + 1],
            self.columns[:, up : up + 1] - self.sums[1][head : head + 1],
        )
        if self.same is not None:
            spread = jnp.where(self.same, spread, FAR)
        return jnp.exp(spread)


def head_mask(block, head_size, member):
    lane = iota((block, LANES), 1)
    return (lane >= member * head_size) & (lane < (member + 1) * head_size)


def scan_block(feats, grads, lines, slots, small_ref, row_slice, forward, backward):
    block = feats.shape[0]
    heads = slots.heads
    head_size = feats.shape[1] // heads
    per_group = LANES // head_size
    below = lines.below
    grad_scores = jnp.zeros((block, block), F32)
    out_parts, grad_parts = [], []
    lane_pad = iota((block, LANES), 1)
    row_sums = jnp.zeros((block, LANES), F32)
    row_at = iota((2 * slots.pad, block), 0)
    col_sums = jnp.zeros((2 * slots.pad, block), F32)
    for group in range(heads // per_group):
        span = slice(group * LANES, (group + 1) * LANES)
        feat_group = feats[:, span]
        grad_group = grads[:, span] if backward else None
        mixes, feat_own, grad_own = [], [], []
        for member in range(per_group):
            head = group * per_group + member
            up = slots.pad + head
            mine = head_mask(block, head_size, member)
            feat_head = jnp.where(mine, feat_group, jnp.zeros_like(feat_group))
            kernel = lines.kernel(head)
            mix = kernel * lines.scores
            mixes.append(mix.astype(BF16))
            feat_own.append(feat_head)
            if not backward:
                continue
            grad_own.append(jnp.where(mine, grad_group, jnp.zeros_like(grad_group)))
            grad_mix = nt(grad_group, feat_head)
            grad_scores = grad_scores + kernel * grad_mix
            flow = mix * grad_mix
            flow_down = jnp.where(below, flow, 0.0)
            row_down = jnp.sum(flow_down, axis=1, keepdims=True)
            row_all = jnp.sum(flow, axis=1, keepdims=True)
            col_down = jnp.sum(flow_down, axis=0, keepdims=True)
            col_all = jnp.sum(flow, axis=0, keepdims=True)
            row_sums = jnp.where(lane_pad == head, row_down, row_sums)
            row_sums = jnp.where(lane_pad == up, row_all - row_down, row_sums)
            col_sums = jnp.where(row_at == head, col_down, col_sums)
            col_sums = jnp.where(row_at == up, col_all - col_down, col_sums)
        if forward:
            out_parts.append(
                nn(jnp.concatenate(mixes, axis=1), jnp.concatenate(feat_own, axis=0))
            )
        if backward:
            grad_parts.append(
                tn(jnp.concatenate(mixes, axis=0), jnp.concatenate(grad_own, axis=0))
            )
    out = jnp.concatenate(out_parts, axis=1) if forward else None
    if not backward:
        return out, None
    change = col_sums - jnp.transpose(row_sums)[: 2 * slots.pad]
    reach = (lines.since, lines.till)
    for way in (0, 1):
        score_grad = jnp.where(reach[way], grad_scores, 0.0).astype(BF16)
        at = slots.inputs[way]
        small_ref[at : at + slots.states, row_slice] = nn(lines.reads[way], score_grad)
        at = slots.reads[way]
        small_ref[at : at + slots.states, row_slice] = nt(lines.inputs[way], score_grad)
        at = slots.rates[way]
        part = change[way * slots.pad : (way + 1) * slots.pad]
        small_ref[at : at + slots.pad, row_slice] = jnp.dot(
            part, reach[way].astype(F32), precision=HI, preferred_element_type=F32
        )
    return out, jnp.concatenate(grad_parts, axis=1)


def by_rank(array, ranks):
    narrow = array[0].shape[0] // ranks
    return [
        jnp.concatenate([row[rank * narrow : (rank + 1) * narrow] for row in array], axis=0)
        for rank in range(ranks)
    ]


def pack_kernel(slots, ranks, feat_ref, cot_ref, rate_ref, input_ref, read_ref, out_ref, rows_ref):
    tile_rows, columns, width = feat_ref.shape
    model = cot_ref.shape[2]
    group = tile_rows * columns // ranks
    rows_ref[...] = jnp.zeros_like(rows_ref)
    for way in (0, 1):
        for row in range(tile_rows):
            span = slice(row * columns, (row + 1) * columns)
            at = slots.inputs[way]
            rows_ref[at : at + slots.states, span] = input_ref[2 + way, :, row, :]
            at = slots.reads[way]
            rows_ref[at : at + slots.states, span] = read_ref[2 + way, :, row, :]
            at = slots.rates[way]
            rate = rate_ref[2 + way, :, row, :]
            rows_ref[at : at + slots.heads, span] = rate
            at = slots.lows[way]
            rows_ref[at : at + slots.heads, span] = rate - rate.astype(BF16).astype(F32)
    values = [
        (0, [feat_ref[row].astype(F32) for row in range(tile_rows)]),
        (width, [cot_ref[row].astype(F32) for row in range(tile_rows)]),
        (
            width + model,
            [
                jnp.transpose(rows_ref[:, row * columns : (row + 1) * columns])
                for row in range(tile_rows)
            ],
        ),
    ]
    for lane, array in values:
        for rank, piece in enumerate(by_rank(array, ranks)):
            out_ref[rank * group : (rank + 1) * group, lane : lane + piece.shape[1]] = (
                piece.astype(BF16)
            )


def rows_kernel(
    slots, chunk, tables, feat_ref, cot_ref, weight_ref, skip_ref, rate_ref, input_ref, read_ref,
    gx_ref, small_ref, part_ref, skip_out_ref, *refs,
):
    *table_refs, rows_ref = refs
    tables.fill(table_refs)
    tile_rows, columns, width = feat_ref.shape
    tokens = tile_rows * columns
    skip = skip_ref[...]
    rows_ref[...] = jnp.zeros_like(rows_ref)
    partial = jnp.zeros(part_ref.shape, F32)
    skip_part = jnp.zeros((1, width), F32)
    for row in range(tile_rows):
        feats, cots = feat_ref[row], cot_ref[row]
        grads = nt(cots, weight_ref[...]).astype(BF16)
        for way in (0, 1):
            at = slots.inputs[way]
            rows_ref[at : at + slots.states, :] = input_ref[way, :, row, :]
            at = slots.reads[way]
            rows_ref[at : at + slots.states, :] = read_ref[way, :, row, :]
            at = slots.rates[way]
            rows_ref[at : at + slots.heads, :] = rate_ref[way, :, row, :]
        rates = [rows_ref[at : at + slots.pad, :] for at in slots.rates]
        lines = Lines(rows_ref, rates, slots, 1, columns)
        outs, gx = scan_block(
            feats, grads, lines, slots, small_ref,
            slice(row * columns, (row + 1) * columns), True, True,
        )
        feat_f32, grad_f32 = feats.astype(F32), grads.astype(F32)
        across = (outs + skip * feat_f32).astype(BF16)
        partial = partial + tn(across, cots)
        gx_ref[row * columns : (row + 1) * columns, :] = gx + skip * grad_f32
        skip_part = skip_part + jnp.sum(feat_f32 * grad_f32, axis=0, keepdims=True)
    part_ref[...] = partial
    if chunk is None:
        skip_out_ref[...] = skip_part
    else:
        high = skip_part.astype(BF16).astype(F32)
        piece = width // chunk
        lane_of = iota((chunk, width), 1)
        start = iota((chunk, width), 0) * piece
        owned = (lane_of >= start) & (lane_of < start + piece)
        spread = jnp.concatenate(
            [jnp.where(owned, high, 0.0), jnp.where(owned, skip_part - high, 0.0)], axis=1
        ).astype(BF16)
        skip_out_ref[...] = nn(spread, skip_places(slots, width, piece))


def skip_places(slots, width, piece):
    at = iota((width, 1), 0)
    whole = ((at.astype(F32) + 0.5) * (1.0 / piece)).astype(jnp.int32)
    place = at - whole * piece + slots.used
    lane = iota((width, LANES), 1)
    high, low = place == lane, place + piece == lane
    return jnp.concatenate([high.astype(F32), low.astype(F32)], axis=0).astype(BF16)


def long_lines(params, slots, lines):
    rows = jnp.transpose(params.astype(F32))
    rates = [
        rows[hi : hi + slots.pad] + rows[lo : lo + slots.pad]
        for hi, lo in zip(slots.rates, slots.lows)
    ]
    return Lines(rows, rates, slots, lines, params.shape[0])


def halves_of(array):
    high = array.astype(BF16)
    return high, (array - high.astype(F32)).astype(BF16)


def reach_of(lines, block):
    at_t, line_t = split_index(iota((block, block), 0), (block // lines, lines))
    at_u, line_u = split_index(iota((block, block), 1), (block // lines, lines))
    same = line_t == line_u
    return same, (same & (at_t >= at_u), same & (at_t <= at_u))


class Tables:
    def __init__(self, slots, lines, tokens, width):
        self.slots, self.lines, self.tokens, self.width = slots, lines, tokens, width
        self.short = tokens // lines <= LONGEST_SHORT
        self.shapes = []
        self.kept = []
        if self.short:
            values = ((2, tokens, width), F32)
            self.kept = [
                ((2, tokens, 2 * LANES), BF16), ((2, tokens, width), BF16), values,
                ((2, tokens, tokens), BF16),
            ]
            self.shapes = [(tokens, tokens), (2 * LANES, 2 * width), (4 * width, LANES)]

    def fill(self, refs):
        if not self.short:
            return
        slots, width, tokens = self.slots, self.width, self.tokens
        size = width // slots.heads
        same, reach = reach_of(self.lines, tokens)
        half = jnp.where(same, 0.5, 0.0)
        refs[0][...] = (reach[0].astype(F32) - half).astype(BF16)
        for way in (0, 1):
            at = iota((LANES, width), 0)
            head = split_index(iota((LANES, width), 1), (slots.heads, size))[0]
            spread = (at == head + slots.rates[way]).astype(F32).astype(BF16)
            lanes = slice(way * width, (way + 1) * width)
            refs[1][:LANES, lanes] = spread
            refs[1][LANES:, lanes] = spread
            at = iota((width, LANES), 1)
            head = split_index(iota((width, LANES), 0), (slots.heads, size))[0]
            gather = (at == head + slots.rates[way]).astype(F32).astype(BF16)
            refs[2][2 * way * width : (2 * way + 1) * width, :] = gather
            refs[2][(2 * way + 1) * width : (2 * way + 2) * width, :] = gather


class ShortLines:
    def __init__(self, params, slots, lines, tables):
        self.slots, self.tables, self.params = slots, tables, params
        tokens = self.tokens = params.shape[0]
        self.reach = reach_of(lines, tokens)[1]
        self.lane = lane = iota((tokens, LANES), 1)
        self.up_lane = ((lane >= slots.rates[1]) & (lane < slots.lows[0])) | (
            lane >= slots.lows[1]
        )
        states = slots.states
        wide = params.astype(F32)
        turned = pltpu.roll(wide, LANES - slots.reads[0], 1)
        first, second = lane < states, (lane >= states) & (lane < 2 * states)
        self.inputs = [jnp.where(mask, wide, 0.0).astype(BF16) for mask in (first, second)]
        self.reads = [jnp.where(mask, turned, 0.0).astype(BF16) for mask in (first, second)]

    def factors(self, width, narrows):
        spread = self.tables[1][...]
        pairs = [nn(narrows[at], spread) for at in (0, 1)]
        return [(pair[:, :width], pair[:, width:]) for pair in pairs]

    def forward(self, feats, kept):
        slots, lane = self.slots, self.lane
        width = feats.shape[1]
        narrows, lost, mixed, scores = kept
        for way in (0, 1):
            score = nt(self.reads[way], self.params)
            scores[way] = jnp.where(self.reach[way], score, 0.0).astype(BF16)
        sums = nn(self.tables[0][...], self.params)
        sums = jnp.where(self.up_lane, self.params.astype(F32) - sums, sums)
        sums = sums + pltpu.roll(sums, LANES - (slots.lows[0] - slots.rates[0]), 1)
        rated = (lane >= slots.rates[0]) & (lane < slots.lows[0])
        sums = jnp.where(rated, sums, 0.0)
        for at, narrow in enumerate((jnp.exp(sums), jnp.exp(-sums))):
            narrows[at] = jnp.concatenate(halves_of(narrow), axis=1)
        losses, gains = self.factors(width, narrows)
        wide = feats.astype(F32)
        out = None
        for way in (0, 1):
            held = (wide * losses[way]).astype(BF16)
            lost[way] = held
            mix = nn(scores[way], held)
            mixed[way] = mix
            part = gains[way] * mix
            out = part if out is None else out + part
        return out

    def backward(self, grads, kept):
        slots = self.slots
        width = grads.shape[1]
        narrows, lost, mixed, scores = kept
        losses, gains = self.factors(width, narrows)
        wide = grads.astype(F32)
        gx = heads = read_grads = input_grads = 0.0
        for way in (0, 1):
            gained = (wide * gains[way]).astype(BF16)
            back = tn(scores[way], gained)
            gx = gx + losses[way] * back
            held = lost[way]
            score_grad = jnp.where(self.reach[way], nt(gained, held), 0.0).astype(BF16)
            change = held.astype(F32) * back - gained.astype(F32) * mixed[way]
            places = self.tables[2][2 * way * width : 2 * (way + 1) * width, :]
            heads = heads + nn(jnp.concatenate(halves_of(change), axis=1), places)
            read_grads = read_grads + nn(score_grad, self.inputs[way])
            input_grads = input_grads + tn(score_grad, self.reads[way])
        since, till = (mask.astype(F32).astype(BF16) for mask in self.reach)
        both = jnp.concatenate(halves_of(heads), axis=1)
        down, up = nn(till, both), nn(since, both)
        rates = jnp.where(
            self.up_lane, up[:, :LANES] + up[:, LANES:], down[:, :LANES] + down[:, LANES:]
        )
        smalls = input_grads + pltpu.roll(read_grads, slots.reads[0], 1)
        return gx, jnp.where(self.lane >= slots.rates[0], rates, smalls)


LONGEST_SHORT = 32


def forward_kernel(slots, lines, sizes, recv_ref, part_ref, *refs):
    tables, refs = refs[: len(sizes.shapes)], refs[len(sizes.shapes) :]
    mine_ref, other_ref, *kept = refs
    width, model = part_ref.shape
    tokens = recv_ref.shape[0]
    feats, cots = recv_ref[:, :width], recv_ref[:, width : width + model]
    params = recv_ref[:, width + model :]
    if sizes.short:
        down = ShortLines(params, slots, lines, tables).forward(feats, kept)
    else:
        masks = long_lines(params, slots, lines)
        down = scan_block(feats, None, masks, slots, None, None, True, False)[0]
    total = part_ref[...] + tn(down.astype(BF16), cots)
    even = lax.rem(lax.axis_index("row"), 2) == 0
    half = width // 2
    mine_ref[...] = jnp.where(even, total[:half], total[half:])
    other_ref[...] = jnp.where(even, total[half:], total[:half]).astype(BF16)


def backward_kernel(slots, ranks, lines, chunk, sizes, recv_ref, weight_ref, skip_ref, *refs):
    tables, refs = refs[: len(sizes.shapes)], refs[len(sizes.shapes) :]
    *kept, back_ref, small_ref = refs
    width, model = weight_ref.shape
    tokens = recv_ref.shape[0]
    feats = recv_ref[:, :width]
    params = recv_ref[:, width + model :]
    grads = nt(recv_ref[:, width : width + model], weight_ref[...]).astype(BF16)
    if sizes.short:
        gx, small = ShortLines(params, slots, lines, tables).backward(grads, kept)
    else:
        small_ref[...] = jnp.zeros_like(small_ref)
        masks = long_lines(params, slots, lines)
        span = slice(0, tokens)
        gx = scan_block(feats, grads, masks, slots, small_ref, span, False, True)[1]
        small = jnp.transpose(small_ref[...])
    back_ref[:, :width] = gx.astype(BF16)
    if chunk is not None:
        small = small + jnp.concatenate([skip_ref[...]] * ranks, axis=0)
    back_ref[:, width:] = small.astype(BF16)


def strip(array):
    return [array[:, at : at + LANES] for at in range(0, array.shape[1], LANES)]


class Tiles:
    def __init__(self, rows, model, ranks, group):
        self.unit = unit = 8
        steps = rows // unit
        self.places = [(at * unit, lane) for lane in range(0, model, LANES) for at in range(steps)]
        count = len(self.places)
        per = 2 * count // ranks
        self.split = 2 * count % ranks == 0 and per % 2 == 1 and ranks % 2 == 0 and group > 4
        self.per = per
        self.full = per // 2 if self.split else -(-count // ranks)
        self.starts = [count * rank // ranks for rank in range(ranks + 1)]
        self.moved = unit // 2 if self.split else 0
        self.size = unit * (self.full + self.split)

    def of(self, rank):
        if not self.split:
            return self.places[self.starts[rank] : self.starts[rank + 1]]
        first = self.per * (rank // 2) + (rank % 2) * (self.full + 1)
        return self.places[first : first + self.full]

    def shared(self, rank):
        return self.places[self.per * (rank // 2) + self.full]


def lay_out(out_ref, rank, pieces):
    at = 0
    for piece in pieces:
        out_ref[rank, at : at + piece.shape[0], :] = piece
        at += piece.shape[0]


def merge_kernel(ranks, early, mine_ref, theirs_ref, back_ref, out_ref):
    total = mine_ref[...] + theirs_ref[...].astype(F32)
    group = back_ref.shape[0] // ranks
    tiles = Tiles(*mine_ref.shape, ranks, group)
    unit = tiles.unit
    for rank in range(ranks):
        pieces = strip(back_ref[rank * group : (rank + 1) * group, :])
        blocks = [
            total[row : row + unit, lane : lane + LANES].astype(BF16)
            for row, lane in tiles.of(rank)
        ]
        blocks += [jnp.zeros((unit, LANES), BF16)] * (tiles.full - len(blocks))
        if tiles.split:
            row, lane = tiles.shared(rank)
            half = unit // 2
            row += (rank % 2) * half
            moved = pieces[-1].astype(F32)[group - tiles.moved :]
            blocks.append(
                jnp.concatenate([total[row : row + half, lane : lane + LANES], moved], axis=0)
                .astype(BF16)
            )
        lay_out(out_ref, rank, pieces[:early] + blocks)


def sum_kernel(early, recv_ref, back_ref, out_ref, tiles):
    ranks = out_ref.shape[0]
    group = back_ref.shape[0] // ranks
    unit = tiles.unit
    own = slice(recv_ref.shape[1] - tiles.size, recv_ref.shape[1])
    whole = tiles.full * unit
    for half in (0, 1):
        total = recv_ref[half, own, :].astype(F32)
        for rank in range(half + 2, ranks, 2):
            total = total + recv_ref[rank, own, :].astype(F32)
        for rank in range(half, ranks, 2):
            pieces = strip(back_ref[rank * group : (rank + 1) * group, :])
            small = pieces[-1]
            if tiles.split:
                small = jnp.concatenate(
                    [total[whole : whole + unit // 2], small.astype(F32)[: group - tiles.moved]],
                    axis=0,
                ).astype(BF16)
            lay_out(out_ref, rank, pieces[early:-1] + [total[:whole].astype(BF16), small])


def half_kernel(start, recv_ref, out_ref):
    out_ref[...] = recv_ref[:, start : start + out_ref.shape[1], :]


def widen_half(halves_ref, store, tiles):
    ranks = halves_ref.shape[0]
    unit = tiles.unit
    for rank in range(ranks):
        for step, (row, lane) in enumerate(tiles.of(rank)):
            store(row, lane, halves_ref[rank, step * unit : (step + 1) * unit, :].astype(F32))
    if tiles.split:
        at = tiles.full * unit
        for rank in range(0, ranks, 2):
            pair = [
                halves_ref[rank + side, at : at + unit, :].astype(F32)[: unit // 2]
                for side in (0, 1)
            ]
            store(*tiles.shared(rank), jnp.concatenate(pair, axis=0))


def weight_kernel(tiles, theirs_ref, weight_in, weight_out, wide_ref, done):
    rows, model = wide_ref.shape

    def store(row, lane, block):
        wide_ref[row : row + block.shape[0], lane : lane + LANES] = block

    widen_half(theirs_ref, store, tiles)
    half = lax.rem(lax.axis_index("row") + 1, 2)
    start = pl.multiple_of(half * rows, 8)
    copy = pltpu.make_async_copy(wide_ref, weight_out.at[pl.ds(start, rows), :], done)
    copy.start()
    copy.wait()


def finish_kernel(
    slots, ranks, chunk, early, tiles, early_ref, late_ref, gx_ref, small_ref, held_ref,
    weight_out, feat_out, rate_out, input_out, read_out, *skip_out,
):
    rows = weight_out.shape[0] // 2
    start = pl.multiple_of(lax.rem(lax.axis_index("row"), 2) * rows, 8)

    def store(row, lane, block):
        weight_out[pl.ds(start + row, block.shape[0]), lane : lane + LANES] = block

    widen_half(held_ref, store, tiles)
    tile_rows, columns, width = feat_out.shape
    narrow = columns // ranks
    group = tile_rows * narrow
    lanes = width // LANES

    def part_of(part):
        ref, part = (early_ref, part) if part < early else (late_ref, part - early)
        return ref[:, part * group : (part + 1) * group, :].astype(F32)

    def row_of(array, row):
        return jnp.concatenate(
            [array[rank, row * narrow : (row + 1) * narrow] for rank in range(ranks)], axis=0
        )

    for part in range(lanes):
        lane = slice(part * LANES, (part + 1) * LANES)
        back = part_of(part)
        for row in range(tile_rows):
            span = slice(row * columns, (row + 1) * columns)
            feat_out[row, :, lane] = (gx_ref[span, lane] + row_of(back, row)).astype(BF16)
    back = late_ref[:, late_ref.shape[1] - group :, :].astype(F32)
    if tiles.split:
        tail = early_ref[:, early_ref.shape[1] - tiles.unit :, :].astype(F32)
        back = jnp.concatenate([back[:, tiles.moved :], tail[:, tiles.unit - tiles.moved :]], axis=1)
    for row in range(tile_rows):
        span = slice(row * columns, (row + 1) * columns)
        held = jnp.transpose(row_of(back, row))
        for way in (0, 1):
            at = slots.inputs[way]
            input_out[way, :, row, :] = small_ref[at : at + slots.states, span]
            input_out[2 + way, :, row, :] = held[at : at + slots.states]
            at = slots.reads[way]
            read_out[way, :, row, :] = small_ref[at : at + slots.states, span]
            read_out[2 + way, :, row, :] = held[at : at + slots.states]
            at = slots.rates[way]
            rate_out[way, :, row, :] = small_ref[at : at + slots.heads, span]
            rate_out[2 + way, :, row, :] = held[at : at + slots.heads]
    if chunk is not None:
        piece = width // chunk
        gathered = jnp.sum(back, axis=0)
        places = skip_places(slots, width, piece)
        places = places[:width] + places[width:]
        high, low = halves_of(gathered)
        spread = nt(high, places) + nt(low, places)
        lane_of = iota((chunk, width), 1)
        start = iota((chunk, width), 0) * piece
        owned = (lane_of >= start) & (lane_of < start + piece)
        skip_out[0][...] = jnp.sum(jnp.where(owned, spread, 0.0), axis=0)


def call(
    kernel, name, out_shape, operands, scratch=(), flops=0, moved=0, grant=VMEM_GRANT,
    whole=(), aliases=None,
):
    def spec(side, at):
        return pl.BlockSpec(memory_space=pl.ANY if (side, at) in whole else pltpu.VMEM)

    many = isinstance(out_shape, tuple)
    outs = tuple(spec("out", at) for at in range(len(out_shape) if many else 1))
    return pl.pallas_call(
        kernel,
        name=name,
        out_shape=out_shape,
        in_specs=[spec("in", at) for at in range(len(operands))],
        out_specs=outs if many else outs[0],
        scratch_shapes=list(scratch),
        input_output_aliases=aliases or {},
        compiler_params=pltpu.CompilerParams(vmem_limit_bytes=grant),
        cost_estimate=pl.CostEstimate(flops=flops, bytes_accessed=moved, transcendentals=0),
    )(*operands)


def local(ranks, features, decay_rate, input_proj, read_proj, skip_gain, out_weight, out_cotangent):
    tile_rows, columns, width = features.shape
    model = out_cotangent.shape[2]
    heads, states = decay_rate.shape[1], input_proj.shape[1]
    slots = Slots(heads, states)
    tokens = tile_rows * columns
    chunk = tokens // ranks
    room = chunk * (LANES - slots.used)
    if chunk % 8 or width % chunk or 2 * width > room:
        chunk = None
    shape = jax.ShapeDtypeStruct

    def exchange(array):
        return lax.all_to_all(array, "row", split_axis=0, concat_axis=0, tiled=True)

    packed = call(
        functools.partial(pack_kernel, slots, ranks), "pack",
        shape((tokens, width + model + LANES), BF16),
        (features, out_cotangent, decay_rate, input_proj, read_proj),
        [pltpu.VMEM((LANES, tokens), F32)],
        flops=2 * tokens * tokens * (width + model), moved=4 * tokens * (width + model), grant=None,
    )
    received = exchange(packed)
    skip_shape = (1, width) if chunk is None else (chunk, LANES)
    lines = columns // ranks
    tables = Tables(slots, lines, tokens, width)
    gx_rows, small_rows, partial, skip_part, *table = call(
        functools.partial(rows_kernel, slots, chunk, tables), "rows",
        (
            shape((tokens, width), F32),
            shape((LANES, tokens), F32),
            shape((width, model), F32),
            shape(skip_shape, F32),
            *(shape(sizes, BF16) for sizes in tables.shapes),
        ),
        (
            features, out_cotangent, out_weight, skip_gain.reshape(1, width),
            decay_rate, input_proj, read_proj,
        ),
        [pltpu.VMEM((LANES, columns), F32)],
        flops=2 * tokens * width * (2 * model + 3 * columns), moved=8 * tokens * width,
    )
    half = width // 2
    partners = [(rank, rank ^ 1) for rank in range(ranks)]
    mine, other, *kept = call(
        functools.partial(forward_kernel, slots, lines, tables), "forward",
        (
            shape((half, model), F32),
            shape((half, model), BF16),
            *(shape(*leaf) for leaf in tables.kept),
        ),
        (received, partial, *table),
        flops=2 * tokens * width * (2 * model + columns), moved=8 * tokens * width,
    )
    theirs = lax.ppermute(other, "row", partners)
    back = call(
        functools.partial(backward_kernel, slots, ranks, lines, chunk, tables), "backward",
        shape((tokens, width + LANES), BF16), (received, out_weight, skip_part, *table, *kept),
        [pltpu.VMEM((LANES, tokens), F32)],
        flops=2 * tokens * width * (2 * model + 3 * columns), moved=8 * tokens * width,
    )
    group = tokens // ranks
    tiles = Tiles(half, model, ranks, group)
    strips = width // LANES + 1
    early = strips // 2
    merged = call(
        functools.partial(merge_kernel, ranks, early), "merge",
        shape((ranks, early * group + tiles.size, LANES), BF16), (mine, theirs, back),
        flops=width * model, moved=2 * width * model,
    )
    returned = exchange(merged)
    whole = tiles.full * tiles.unit
    late_rows = (strips - early) * group + whole
    summed = call(
        functools.partial(sum_kernel, early, tiles=tiles), "sum",
        shape((ranks, late_rows, LANES), BF16), (returned, back),
        flops=width * model, moved=2 * width * model,
    )
    last = exchange(summed)
    held = call(
        functools.partial(half_kernel, (strips - early - 1) * group), "half",
        shape((ranks, tiles.size, LANES), BF16), (last,),
        flops=width * model, moved=2 * width * model,
    )
    swapped = lax.ppermute(held, "row", partners)
    outs = [
        shape((width, model), F32),
        shape(features.shape, BF16),
        shape(decay_rate.shape, F32),
        shape(input_proj.shape, F32),
        shape(read_proj.shape, F32),
    ]
    if chunk is not None:
        outs.append(shape((width,), F32))
    done = call(
        functools.partial(finish_kernel, slots, ranks, chunk, early, tiles), "finish",
        tuple(outs), (returned, last, gx_rows, small_rows, held),
        flops=2 * tokens * tokens * width, moved=8 * tokens * width,
    )
    grad_weight = call(
        functools.partial(weight_kernel, tiles), "weight", shape((width, model), F32),
        (swapped, done[0]),
        [pltpu.VMEM((half, model), F32), pltpu.SemaphoreType.DMA(())],
        flops=width * model, moved=6 * width * model,
        whole=[("in", 1), ("out", 0)], aliases={1: 0},
    )
    if chunk is None:
        grad_skip = lax.psum(skip_part, "row").reshape(width)
    else:
        grad_skip = done[5]
    return (*done[1:5], grad_skip, grad_weight)


def solution(mesh):
    in_specs = (
        P(("grp", "row"), None, None),
        P(None, None, ("grp", "row"), None),
        P(None, None, ("grp", "row"), None),
        P(None, None, ("grp", "row"), None),
        P(),
        P(),
        P(("grp", "row"), None, None),
    )
    out_specs = (
        P(("grp", "row"), None, None),
        P(None, None, ("grp", "row"), None),
        P(None, None, ("grp", "row"), None),
        P(None, None, ("grp", "row"), None),
        P("grp"),
        P("grp", None),
    )
    body = functools.partial(local, mesh.shape["row"])
    return jax.shard_map(body, mesh=mesh, in_specs=in_specs, out_specs=out_specs, check_vma=False)
```

```python
import functools

import jax
import jax.numpy as jnp
from jax import lax
from jax.experimental import pallas as pl
from jax.experimental.pallas import tpu as pltpu
from jax.sharding import PartitionSpec as P

F32 = jnp.float32
BF16 = jnp.bfloat16
HI = lax.Precision.HIGHEST
LANES = 128
FAR = -1e30
VMEM_GRANT = 16 << 20


def iota(shape, dim):
    return lax.broadcasted_iota(jnp.int32, shape, dim)


def nt(a, b):
    return lax.dot_general(a, b, (((1,), (1,)), ((), ())), preferred_element_type=F32)


def nn(a, b):
    return jnp.dot(a, b, preferred_element_type=F32)


def tn(a, b):
    return lax.dot_general(a, b, (((0,), (0,)), ((), ())), preferred_element_type=F32)


def split_index(index, sizes):
    parts = []
    for size in reversed(sizes):
        if size & (size - 1) == 0:
            parts.append(index & (size - 1))
            index = index >> (size.bit_length() - 1)
        else:
            parts.append(lax.rem(index, size))
            index = lax.div(index, size)
    return parts[::-1]


class Slots:
    def __init__(self, heads, states):
        self.heads = heads
        self.states = states
        self.inputs = (0, states)
        self.reads = (2 * states, 3 * states)
        pad = -(-heads // 8) * 8
        self.pad = pad
        self.rates = (4 * states, 4 * states + pad)
        self.lows = (4 * states + 2 * pad, 4 * states + 3 * pad)
        self.used = 4 * states + 2 * pad


class Lines:
    def __init__(self, rows, rates, slots, lines, block):
        at_t, at_u = iota((block, block), 0), iota((block, block), 1)
        self.same = None
        if lines > 1:
            at_t, line_t = split_index(at_t, (block // lines, lines))
            at_u, line_u = split_index(at_u, (block // lines, lines))
            self.same = line_t == line_u
        self.below, self.above = at_t > at_u, at_t < at_u
        self.till = self.within(at_t <= at_u)
        self.since = self.within(at_t >= at_u)
        self.sums = (
            -jnp.dot(rates[0], self.till.astype(F32), precision=HI, preferred_element_type=F32),
            -jnp.dot(rates[1], self.since.astype(F32), precision=HI, preferred_element_type=F32),
        )
        self.columns = jnp.transpose(jnp.concatenate(self.sums, axis=0))
        self.inputs = [rows[at : at + slots.states].astype(BF16) for at in slots.inputs]
        self.reads = [rows[at : at + slots.states].astype(BF16) for at in slots.reads]
        down, up = (tn(self.reads[way], self.inputs[way]) for way in (0, 1))
        self.scores = jnp.where(self.below, down, jnp.where(self.above, up, down + up))
        self.pad = slots.pad

    def within(self, mask):
        return mask if self.same is None else mask & self.same

    def kernel(self, head):
        up = self.pad + head
        spread = jnp.where(
            self.below,
            self.columns[:, head : head + 1] - self.sums[0][head : head + 1],
            self.columns[:, up : up + 1] - self.sums[1][head : head + 1],
        )
        if self.same is not None:
            spread = jnp.where(self.same, spread, FAR)
        return jnp.exp(spread)


def head_mask(block, head_size, member):
    lane = iota((block, LANES), 1)
    return (lane >= member * head_size) & (lane < (member + 1) * head_size)


def scan_block(feats, grads, lines, slots, small_ref, row_slice, forward, backward):
    block = feats.shape[0]
    heads = slots.heads
    head_size = feats.shape[1] // heads
    per_group = LANES // head_size
    below = lines.below
    grad_scores = jnp.zeros((block, block), F32)
    out_parts, grad_parts = [], []
    lane_pad = iota((block, LANES), 1)
    row_sums = jnp.zeros((block, LANES), F32)
    row_at = iota((2 * slots.pad, block), 0)
    col_sums = jnp.zeros((2 * slots.pad, block), F32)
    for group in range(heads // per_group):
        span = slice(group * LANES, (group + 1) * LANES)
        feat_group = feats[:, span]
        grad_group = grads[:, span] if backward else None
        mixes, feat_own, grad_own = [], [], []
        for member in range(per_group):
            head = group * per_group + member
            up = slots.pad + head
            mine = head_mask(block, head_size, member)
            feat_head = jnp.where(mine, feat_group, jnp.zeros_like(feat_group))
            kernel = lines.kernel(head)
            mix = kernel * lines.scores
            mixes.append(mix.astype(BF16))
            feat_own.append(feat_head)
            if not backward:
                continue
            grad_own.append(jnp.where(mine, grad_group, jnp.zeros_like(grad_group)))
            grad_mix = nt(grad_group, feat_head)
            grad_scores = grad_scores + kernel * grad_mix
            flow = mix * grad_mix
            flow_down = jnp.where(below, flow, 0.0)
            row_down = jnp.sum(flow_down, axis=1, keepdims=True)
            row_all = jnp.sum(flow, axis=1, keepdims=True)
            col_down = jnp.sum(flow_down, axis=0, keepdims=True)
            col_all = jnp.sum(flow, axis=0, keepdims=True)
            row_sums = jnp.where(lane_pad == head, row_down, row_sums)
            row_sums = jnp.where(lane_pad == up, row_all - row_down, row_sums)
            col_sums = jnp.where(row_at == head, col_down, col_sums)
            col_sums = jnp.where(row_at == up, col_all - col_down, col_sums)
        if forward:
            out_parts.append(
                nn(jnp.concatenate(mixes, axis=1), jnp.concatenate(feat_own, axis=0))
            )
        if backward:
            grad_parts.append(
                tn(jnp.concatenate(mixes, axis=0), jnp.concatenate(grad_own, axis=0))
            )
    out = jnp.concatenate(out_parts, axis=1) if forward else None
    if not backward:
        return out, None
    change = col_sums - jnp.transpose(row_sums)[: 2 * slots.pad]
    reach = (lines.since, lines.till)
    for way in (0, 1):
        score_grad = jnp.where(reach[way], grad_scores, 0.0).astype(BF16)
        at = slots.inputs[way]
        small_ref[at : at + slots.states, row_slice] = nn(lines.reads[way], score_grad)
        at = slots.reads[way]
        small_ref[at : at + slots.states, row_slice] = nt(lines.inputs[way], score_grad)
        at = slots.rates[way]
        part = change[way * slots.pad : (way + 1) * slots.pad]
        small_ref[at : at + slots.pad, row_slice] = jnp.dot(
            part, reach[way].astype(F32), precision=HI, preferred_element_type=F32
        )
    return out, jnp.concatenate(grad_parts, axis=1)


def by_rank(array, ranks):
    narrow = array[0].shape[0] // ranks
    return [
        jnp.concatenate([row[rank * narrow : (rank + 1) * narrow] for row in array], axis=0)
        for rank in range(ranks)
    ]


def pack_kernel(slots, ranks, feat_ref, cot_ref, rate_ref, input_ref, read_ref, out_ref, rows_ref):
    tile_rows, columns, width = feat_ref.shape
    model = cot_ref.shape[2]
    group = tile_rows * columns // ranks
    rows_ref[...] = jnp.zeros_like(rows_ref)
    for way in (0, 1):
        for row in range(tile_rows):
            span = slice(row * columns, (row + 1) * columns)
            at = slots.inputs[way]
            rows_ref[at : at + slots.states, span] = input_ref[2 + way, :, row, :]
            at = slots.reads[way]
            rows_ref[at : at + slots.states, span] = read_ref[2 + way, :, row, :]
            at = slots.rates[way]
            rate = rate_ref[2 + way, :, row, :]
            rows_ref[at : at + slots.heads, span] = rate
            at = slots.lows[way]
            rows_ref[at : at + slots.heads, span] = rate - rate.astype(BF16).astype(F32)
    values = [
        (0, [feat_ref[row].astype(F32) for row in range(tile_rows)]),
        (width, [cot_ref[row].astype(F32) for row in range(tile_rows)]),
        (
            width + model,
            [
                jnp.transpose(rows_ref[:, row * columns : (row + 1) * columns])
                for row in range(tile_rows)
            ],
        ),
    ]
    for lane, array in values:
        for rank, piece in enumerate(by_rank(array, ranks)):
            out_ref[rank * group : (rank + 1) * group, lane : lane + piece.shape[1]] = (
                piece.astype(BF16)
            )


def rows_kernel(
    slots, chunk, tables, feat_hbm, cot_hbm, weight_ref, skip_ref, rate_hbm, input_hbm, read_hbm,
    gx_ref, small_ref, part_ref, skip_out_ref, *refs,
):
    *table_refs, rows_ref, feat_ref, cot_ref, rate_ref, input_ref, read_ref, arrived = refs
    ways = pl.ds(0, 2)
    copies = [
        pltpu.make_async_copy(source, target, arrived.at[at])
        for at, (source, target) in enumerate(
            [
                (feat_hbm, feat_ref),
                (cot_hbm, cot_ref),
                (rate_hbm.at[ways], rate_ref),
                (input_hbm.at[ways], input_ref),
                (read_hbm.at[ways], read_ref),
            ]
        )
    ]
    for copy in copies:
        copy.start()
    tables.fill(table_refs)
    for copy in copies:
        copy.wait()
    tile_rows, columns, width = feat_ref.shape
    tokens = tile_rows * columns
    skip = skip_ref[...]
    rows_ref[...] = jnp.zeros_like(rows_ref)
    partial = jnp.zeros(part_ref.shape, F32)
    skip_part = jnp.zeros((1, width), F32)
    for row in range(tile_rows):
        feats, cots = feat_ref[row], cot_ref[row]
        grads = nt(cots, weight_ref[...]).astype(BF16)
        for way in (0, 1):
            at = slots.inputs[way]
            rows_ref[at : at + slots.states, :] = input_ref[way, :, row, :]
            at = slots.reads[way]
            rows_ref[at : at + slots.states, :] = read_ref[way, :, row, :]
            at = slots.rates[way]
            rows_ref[at : at + slots.heads, :] = rate_ref[way, :, row, :]
        rates = [rows_ref[at : at + slots.pad, :] for at in slots.rates]
        lines = Lines(rows_ref, rates, slots, 1, columns)
        outs, gx = scan_block(
            feats, grads, lines, slots, small_ref,
            slice(row * columns, (row + 1) * columns), True, True,
        )
        feat_f32, grad_f32 = feats.astype(F32), grads.astype(F32)
        across = (outs + skip * feat_f32).astype(BF16)
        partial = partial + tn(across, cots)
        gx_ref[row * columns : (row + 1) * columns, :] = gx + skip * grad_f32
        skip_part = skip_part + jnp.sum(feat_f32 * grad_f32, axis=0, keepdims=True)
    part_ref[...] = partial
    if chunk is None:
        skip_out_ref[...] = skip_part
    else:
        high = skip_part.astype(BF16).astype(F32)
        piece = width // chunk
        lane_of = iota((chunk, width), 1)
        start = iota((chunk, width), 0) * piece
        owned = (lane_of >= start) & (lane_of < start + piece)
        spread = jnp.concatenate(
            [jnp.where(owned, high, 0.0), jnp.where(owned, skip_part - high, 0.0)], axis=1
        ).astype(BF16)
        skip_out_ref[...] = nn(spread, skip_places(slots, width, piece))


def skip_places(slots, width, piece):
    at = iota((width, 1), 0)
    whole = ((at.astype(F32) + 0.5) * (1.0 / piece)).astype(jnp.int32)
    place = at - whole * piece + slots.used
    lane = iota((width, LANES), 1)
    high, low = place == lane, place + piece == lane
    return jnp.concatenate([high.astype(F32), low.astype(F32)], axis=0).astype(BF16)


def long_lines(params, slots, lines):
    rows = jnp.transpose(params.astype(F32))
    rates = [
        rows[hi : hi + slots.pad] + rows[lo : lo + slots.pad]
        for hi, lo in zip(slots.rates, slots.lows)
    ]
    return Lines(rows, rates, slots, lines, params.shape[0])


def halves_of(array):
    high = array.astype(BF16)
    return high, (array - high.astype(F32)).astype(BF16)


def reach_of(lines, block):
    at_t, line_t = split_index(iota((block, block), 0), (block // lines, lines))
    at_u, line_u = split_index(iota((block, block), 1), (block // lines, lines))
    same = line_t == line_u
    return same, (same & (at_t >= at_u), same & (at_t <= at_u))


class Tables:
    def __init__(self, slots, lines, tokens, width):
        self.slots, self.lines, self.tokens, self.width = slots, lines, tokens, width
        self.short = tokens // lines <= LONGEST_SHORT
        self.shapes = []
        self.kept = []
        if self.short:
            values = ((2, tokens, width), F32)
            self.kept = [
                ((2, tokens, 2 * LANES), BF16), ((2, tokens, width), BF16), values,
                ((2, tokens, tokens), BF16),
            ]
            self.shapes = [(tokens, tokens), (2 * LANES, 2 * width), (4 * width, LANES)]

    def fill(self, refs):
        if not self.short:
            return
        slots, width, tokens = self.slots, self.width, self.tokens
        size = width // slots.heads
        same, reach = reach_of(self.lines, tokens)
        half = jnp.where(same, 0.5, 0.0)
        refs[0][...] = (reach[0].astype(F32) - half).astype(BF16)
        for way in (0, 1):
            at = iota((LANES, width), 0)
            head = split_index(iota((LANES, width), 1), (slots.heads, size))[0]
            spread = (at == head + slots.rates[way]).astype(F32).astype(BF16)
            lanes = slice(way * width, (way + 1) * width)
            refs[1][:LANES, lanes] = spread
            refs[1][LANES:, lanes] = spread
            at = iota((width, LANES), 1)
            head = split_index(iota((width, LANES), 0), (slots.heads, size))[0]
            gather = (at == head + slots.rates[way]).astype(F32).astype(BF16)
            refs[2][2 * way * width : (2 * way + 1) * width, :] = gather
            refs[2][(2 * way + 1) * width : (2 * way + 2) * width, :] = gather


class ShortLines:
    def __init__(self, params, slots, lines, tables):
        self.slots, self.tables, self.params = slots, tables, params
        tokens = self.tokens = params.shape[0]
        self.reach = reach_of(lines, tokens)[1]
        self.lane = lane = iota((tokens, LANES), 1)
        self.up_lane = ((lane >= slots.rates[1]) & (lane < slots.lows[0])) | (
            lane >= slots.lows[1]
        )
        states = slots.states
        wide = params.astype(F32)
        turned = pltpu.roll(wide, LANES - slots.reads[0], 1)
        first, second = lane < states, (lane >= states) & (lane < 2 * states)
        self.inputs = [jnp.where(mask, wide, 0.0).astype(BF16) for mask in (first, second)]
        self.reads = [jnp.where(mask, turned, 0.0).astype(BF16) for mask in (first, second)]

    def factors(self, width, narrows):
        spread = self.tables[1][...]
        pairs = [nn(narrows[at], spread) for at in (0, 1)]
        return [(pair[:, :width], pair[:, width:]) for pair in pairs]

    def forward(self, feats, kept):
        slots, lane = self.slots, self.lane
        width = feats.shape[1]
        narrows, lost, mixed, scores = kept
        for way in (0, 1):
            score = nt(self.reads[way], self.params)
            scores[way] = jnp.where(self.reach[way], score, 0.0).astype(BF16)
        sums = nn(self.tables[0][...], self.params)
        sums = jnp.where(self.up_lane, self.params.astype(F32) - sums, sums)
        sums = sums + pltpu.roll(sums, LANES - (slots.lows[0] - slots.rates[0]), 1)
        rated = (lane >= slots.rates[0]) & (lane < slots.lows[0])
        sums = jnp.where(rated, sums, 0.0)
        for at, narrow in enumerate((jnp.exp(sums), jnp.exp(-sums))):
            narrows[at] = jnp.concatenate(halves_of(narrow), axis=1)
        losses, gains = self.factors(width, narrows)
        wide = feats.astype(F32)
        out = None
        for way in (0, 1):
            held = (wide * losses[way]).astype(BF16)
            lost[way] = held
            mix = nn(scores[way], held)
            mixed[way] = mix
            part = gains[way] * mix
            out = part if out is None else out + part
        return out

    def backward(self, grads, kept):
        slots = self.slots
        width = grads.shape[1]
        narrows, lost, mixed, scores = kept
        losses, gains = self.factors(width, narrows)
        wide = grads.astype(F32)
        gx = heads = read_grads = input_grads = 0.0
        for way in (0, 1):
            gained = (wide * gains[way]).astype(BF16)
            back = tn(scores[way], gained)
            gx = gx + losses[way] * back
            held = lost[way]
            score_grad = jnp.where(self.reach[way], nt(gained, held), 0.0).astype(BF16)
            change = held.astype(F32) * back - gained.astype(F32) * mixed[way]
            places = self.tables[2][2 * way * width : 2 * (way + 1) * width, :]
            heads = heads + nn(jnp.concatenate(halves_of(change), axis=1), places)
            read_grads = read_grads + nn(score_grad, self.inputs[way])
            input_grads = input_grads + tn(score_grad, self.reads[way])
        since, till = (mask.astype(F32).astype(BF16) for mask in self.reach)
        both = jnp.concatenate(halves_of(heads), axis=1)
        down, up = nn(till, both), nn(since, both)
        rates = jnp.where(
            self.up_lane, up[:, :LANES] + up[:, LANES:], down[:, :LANES] + down[:, LANES:]
        )
        smalls = input_grads + pltpu.roll(read_grads, slots.reads[0], 1)
        return gx, jnp.where(self.lane >= slots.rates[0], rates, smalls)


LONGEST_SHORT = 32


def forward_kernel(slots, lines, sizes, recv_ref, part_ref, *refs):
    tables, refs = refs[: len(sizes.shapes)], refs[len(sizes.shapes) :]
    mine_ref, other_ref, *kept = refs
    width, model = part_ref.shape
    tokens = recv_ref.shape[0]
    feats, cots = recv_ref[:, :width], recv_ref[:, width : width + model]
    params = recv_ref[:, width + model :]
    if sizes.short:
        down = ShortLines(params, slots, lines, tables).forward(feats, kept)
    else:
        masks = long_lines(params, slots, lines)
        down = scan_block(feats, None, masks, slots, None, None, True, False)[0]
    total = part_ref[...] + tn(down.astype(BF16), cots)
    even = lax.rem(lax.axis_index("row"), 2) == 0
    half = width // 2
    mine_ref[...] = jnp.where(even, total[:half], total[half:])
    other_ref[...] = jnp.where(even, total[half:], total[:half]).astype(BF16)


def backward_kernel(slots, ranks, lines, chunk, sizes, recv_ref, weight_ref, skip_ref, *refs):
    tables, refs = refs[: len(sizes.shapes)], refs[len(sizes.shapes) :]
    *kept, back_ref, small_ref = refs
    width, model = weight_ref.shape
    tokens = recv_ref.shape[0]
    feats = recv_ref[:, :width]
    params = recv_ref[:, width + model :]
    grads = nt(recv_ref[:, width : width + model], weight_ref[...]).astype(BF16)
    if sizes.short:
        gx, small = ShortLines(params, slots, lines, tables).backward(grads, kept)
    else:
        small_ref[...] = jnp.zeros_like(small_ref)
        masks = long_lines(params, slots, lines)
        span = slice(0, tokens)
        gx = scan_block(feats, grads, masks, slots, small_ref, span, False, True)[1]
        small = jnp.transpose(small_ref[...])
    back_ref[:, :width] = gx.astype(BF16)
    if chunk is not None:
        small = small + jnp.concatenate([skip_ref[...]] * ranks, axis=0)
    back_ref[:, width:] = small.astype(BF16)


def strip(array):
    return [array[:, at : at + LANES] for at in range(0, array.shape[1], LANES)]


class Tiles:
    def __init__(self, rows, model, ranks, group):
        self.unit = unit = 8
        steps = rows // unit
        self.places = [(at * unit, lane) for lane in range(0, model, LANES) for at in range(steps)]
        count = len(self.places)
        per = 2 * count // ranks
        self.split = 2 * count % ranks == 0 and per % 2 == 1 and ranks % 2 == 0 and group > 4
        self.per = per
        self.full = per // 2 if self.split else -(-count // ranks)
        self.starts = [count * rank // ranks for rank in range(ranks + 1)]
        self.moved = unit // 2 if self.split else 0
        self.size = unit * (self.full + self.split)

    def of(self, rank):
        if not self.split:
            return self.places[self.starts[rank] : self.starts[rank + 1]]
        first = self.per * (rank // 2) + (rank % 2) * (self.full + 1)
        return self.places[first : first + self.full]

    def shared(self, rank):
        return self.places[self.per * (rank // 2) + self.full]


def lay_out(out_ref, rank, pieces):
    at = 0
    for piece in pieces:
        out_ref[rank, at : at + piece.shape[0], :] = piece
        at += piece.shape[0]


def merge_kernel(ranks, early, mine_ref, theirs_ref, back_ref, out_ref):
    total = mine_ref[...] + theirs_ref[...].astype(F32)
    group = back_ref.shape[0] // ranks
    tiles = Tiles(*mine_ref.shape, ranks, group)
    unit = tiles.unit
    for rank in range(ranks):
        pieces = strip(back_ref[rank * group : (rank + 1) * group, :])
        blocks = [
            total[row : row + unit, lane : lane + LANES].astype(BF16)
            for row, lane in tiles.of(rank)
        ]
        blocks += [jnp.zeros((unit, LANES), BF16)] * (tiles.full - len(blocks))
        if tiles.split:
            row, lane = tiles.shared(rank)
            half = unit // 2
            row += (rank % 2) * half
            moved = pieces[-1].astype(F32)[group - tiles.moved :]
            blocks.append(
                jnp.concatenate([total[row : row + half, lane : lane + LANES], moved], axis=0)
                .astype(BF16)
            )
        lay_out(out_ref, rank, pieces[:early] + blocks)


def sum_kernel(early, recv_ref, back_ref, out_ref, tiles):
    ranks = out_ref.shape[0]
    group = back_ref.shape[0] // ranks
    unit = tiles.unit
    own = slice(recv_ref.shape[1] - tiles.size, recv_ref.shape[1])
    whole = tiles.full * unit
    for half in (0, 1):
        total = recv_ref[half, own, :].astype(F32)
        for rank in range(half + 2, ranks, 2):
            total = total + recv_ref[rank, own, :].astype(F32)
        for rank in range(half, ranks, 2):
            pieces = strip(back_ref[rank * group : (rank + 1) * group, :])
            small = pieces[-1]
            if tiles.split:
                small = jnp.concatenate(
                    [total[whole : whole + unit // 2], small.astype(F32)[: group - tiles.moved]],
                    axis=0,
                ).astype(BF16)
            lay_out(out_ref, rank, pieces[early:-1] + [total[:whole].astype(BF16), small])


def half_kernel(start, recv_ref, out_ref):
    out_ref[...] = recv_ref[:, start : start + out_ref.shape[1], :]


def widen_half(halves_ref, store, tiles):
    ranks = halves_ref.shape[0]
    unit = tiles.unit
    for rank in range(ranks):
        for step, (row, lane) in enumerate(tiles.of(rank)):
            store(row, lane, halves_ref[rank, step * unit : (step + 1) * unit, :].astype(F32))
    if tiles.split:
        at = tiles.full * unit
        for rank in range(0, ranks, 2):
            pair = [
                halves_ref[rank + side, at : at + unit, :].astype(F32)[: unit // 2]
                for side in (0, 1)
            ]
            store(*tiles.shared(rank), jnp.concatenate(pair, axis=0))


def weight_kernel(tiles, theirs_ref, weight_in, weight_out, wide_ref, done):
    rows, model = wide_ref.shape

    def store(row, lane, block):
        wide_ref[row : row + block.shape[0], lane : lane + LANES] = block

    widen_half(theirs_ref, store, tiles)
    half = lax.rem(lax.axis_index("row") + 1, 2)
    start = pl.multiple_of(half * rows, 8)
    copy = pltpu.make_async_copy(wide_ref, weight_out.at[pl.ds(start, rows), :], done)
    copy.start()
    copy.wait()


def finish_kernel(
    slots, ranks, chunk, early, tiles, early_ref, late_ref, gx_ref, small_ref, held_ref,
    weight_out, feat_out, rate_out, input_out, read_out, *skip_out,
):
    rows = weight_out.shape[0] // 2
    start = pl.multiple_of(lax.rem(lax.axis_index("row"), 2) * rows, 8)

    def store(row, lane, block):
        weight_out[pl.ds(start + row, block.shape[0]), lane : lane + LANES] = block

    widen_half(held_ref, store, tiles)
    tile_rows, columns, width = feat_out.shape
    narrow = columns // ranks
    group = tile_rows * narrow
    lanes = width // LANES

    def part_of(part):
        ref, part = (early_ref, part) if part < early else (late_ref, part - early)
        return ref[:, part * group : (part + 1) * group, :].astype(F32)

    def row_of(array, row):
        return jnp.concatenate(
            [array[rank, row * narrow : (row + 1) * narrow] for rank in range(ranks)], axis=0
        )

    for part in range(lanes):
        lane = slice(part * LANES, (part + 1) * LANES)
        back = part_of(part)
        for row in range(tile_rows):
            span = slice(row * columns, (row + 1) * columns)
            feat_out[row, :, lane] = (gx_ref[span, lane] + row_of(back, row)).astype(BF16)
    back = late_ref[:, late_ref.shape[1] - group :, :].astype(F32)
    if tiles.split:
        tail = early_ref[:, early_ref.shape[1] - tiles.unit :, :].astype(F32)
        back = jnp.concatenate([back[:, tiles.moved :], tail[:, tiles.unit - tiles.moved :]], axis=1)
    for row in range(tile_rows):
        span = slice(row * columns, (row + 1) * columns)
        held = jnp.transpose(row_of(back, row))
        for way in (0, 1):
            at = slots.inputs[way]
            input_out[way, :, row, :] = small_ref[at : at + slots.states, span]
            input_out[2 + way, :, row, :] = held[at : at + slots.states]
            at = slots.reads[way]
            read_out[way, :, row, :] = small_ref[at : at + slots.states, span]
            read_out[2 + way, :, row, :] = held[at : at + slots.states]
            at = slots.rates[way]
            rate_out[way, :, row, :] = small_ref[at : at + slots.heads, span]
            rate_out[2 + way, :, row, :] = held[at : at + slots.heads]
    if chunk is not None:
        piece = width // chunk
        gathered = jnp.sum(back, axis=0)
        places = skip_places(slots, width, piece)
        places = places[:width] + places[width:]
        high, low = halves_of(gathered)
        spread = nt(high, places) + nt(low, places)
        lane_of = iota((chunk, width), 1)
        start = iota((chunk, width), 0) * piece
        owned = (lane_of >= start) & (lane_of < start + piece)
        skip_out[0][...] = jnp.sum(jnp.where(owned, spread, 0.0), axis=0)


def call(
    kernel, name, out_shape, operands, scratch=(), flops=0, moved=0, grant=VMEM_GRANT,
    whole=(), aliases=None,
):
    def spec(side, at):
        return pl.BlockSpec(memory_space=pltpu.HBM if (side, at) in whole else pltpu.VMEM)

    many = isinstance(out_shape, tuple)
    outs = tuple(spec("out", at) for at in range(len(out_shape) if many else 1))
    return pl.pallas_call(
        kernel,
        name=name,
        out_shape=out_shape,
        in_specs=[spec("in", at) for at in range(len(operands))],
        out_specs=outs if many else outs[0],
        scratch_shapes=list(scratch),
        input_output_aliases=aliases or {},
        compiler_params=pltpu.CompilerParams(vmem_limit_bytes=grant),
        cost_estimate=pl.CostEstimate(flops=flops, bytes_accessed=moved, transcendentals=0),
    )(*operands)


def local(ranks, features, decay_rate, input_proj, read_proj, skip_gain, out_weight, out_cotangent):
    tile_rows, columns, width = features.shape
    model = out_cotangent.shape[2]
    heads, states = decay_rate.shape[1], input_proj.shape[1]
    slots = Slots(heads, states)
    tokens = tile_rows * columns
    chunk = tokens // ranks
    room = chunk * (LANES - slots.used)
    if chunk % 8 or width % chunk or 2 * width > room:
        chunk = None
    shape = jax.ShapeDtypeStruct

    def exchange(array):
        return lax.all_to_all(array, "row", split_axis=0, concat_axis=0, tiled=True)

    packed = call(
        functools.partial(pack_kernel, slots, ranks), "pack",
        shape((tokens, width + model + LANES), BF16),
        (features, out_cotangent, decay_rate, input_proj, read_proj),
        [pltpu.VMEM((LANES, tokens), F32)],
        flops=2 * tokens * tokens * (width + model), moved=4 * tokens * (width + model), grant=None,
    )
    received = exchange(packed)
    skip_shape = (1, width) if chunk is None else (chunk, LANES)
    lines = columns // ranks
    tables = Tables(slots, lines, tokens, width)
    gx_rows, small_rows, partial, skip_part, *table = call(
        functools.partial(rows_kernel, slots, chunk, tables), "rows",
        (
            shape((tokens, width), F32),
            shape((LANES, tokens), F32),
            shape((width, model), F32),
            shape(skip_shape, F32),
            *(shape(sizes, BF16) for sizes in tables.shapes),
        ),
        (
            features, out_cotangent, out_weight, skip_gain.reshape(1, width),
            decay_rate, input_proj, read_proj,
        ),
        [
            pltpu.VMEM((LANES, columns), F32),
            pltpu.VMEM(features.shape, BF16),
            pltpu.VMEM(out_cotangent.shape, BF16),
            pltpu.VMEM((2, *decay_rate.shape[1:]), F32),
            pltpu.VMEM((2, *input_proj.shape[1:]), F32),
            pltpu.VMEM((2, *read_proj.shape[1:]), F32),
            pltpu.SemaphoreType.DMA((5,)),
        ],
        whole=[("in", at) for at in (0, 1, 4, 5, 6)],
        flops=2 * tokens * width * (2 * model + 3 * columns), moved=8 * tokens * width,
    )
    half = width // 2
    partners = [(rank, rank ^ 1) for rank in range(ranks)]
    mine, other, *kept = call(
        functools.partial(forward_kernel, slots, lines, tables), "forward",
        (
            shape((half, model), F32),
            shape((half, model), BF16),
            *(shape(*leaf) for leaf in tables.kept),
        ),
        (received, partial, *table),
        flops=2 * tokens * width * (2 * model + columns), moved=8 * tokens * width,
    )
    theirs = lax.ppermute(other, "row", partners)
    back = call(
        functools.partial(backward_kernel, slots, ranks, lines, chunk, tables), "backward",
        shape((tokens, width + LANES), BF16), (received, out_weight, skip_part, *table, *kept),
        [pltpu.VMEM((LANES, tokens), F32)],
        flops=2 * tokens * width * (2 * model + 3 * columns), moved=8 * tokens * width,
    )
    group = tokens // ranks
    tiles = Tiles(half, model, ranks, group)
    strips = width // LANES + 1
    early = strips // 4
    merged = call(
        functools.partial(merge_kernel, ranks, early), "merge",
        shape((ranks, early * group + tiles.size, LANES), BF16), (mine, theirs, back),
        flops=width * model, moved=2 * width * model,
    )
    returned = exchange(merged)
    whole = tiles.full * tiles.unit
    late_rows = (strips - early) * group + whole
    summed = call(
        functools.partial(sum_kernel, early, tiles=tiles), "sum",
        shape((ranks, late_rows, LANES), BF16), (returned, back),
        flops=width * model, moved=2 * width * model,
    )
    last = exchange(summed)
    held = call(
        functools.partial(half_kernel, (strips - early - 1) * group), "half",
        shape((ranks, tiles.size, LANES), BF16), (last,),
        flops=width * model, moved=2 * width * model,
    )
    swapped = lax.ppermute(held, "row", partners)
    outs = [
        shape((width, model), F32),
        shape(features.shape, BF16),
        shape(decay_rate.shape, F32),
        shape(input_proj.shape, F32),
        shape(read_proj.shape, F32),
    ]
    if chunk is not None:
        outs.append(shape((width,), F32))
    done = call(
        functools.partial(finish_kernel, slots, ranks, chunk, early, tiles), "finish",
        tuple(outs), (returned, last, gx_rows, small_rows, held),
        flops=2 * tokens * tokens * width, moved=8 * tokens * width,
    )
    grad_weight = call(
        functools.partial(weight_kernel, tiles), "weight", shape((width, model), F32),
        (swapped, done[0]),
        [pltpu.VMEM((half, model), F32), pltpu.SemaphoreType.DMA(())],
        flops=width * model, moved=6 * width * model,
        whole=[("in", 1), ("out", 0)], aliases={1: 0},
    )
    if chunk is None:
        grad_skip = lax.psum(skip_part, "row").reshape(width)
    else:
        grad_skip = done[5]
    return (*done[1:5], grad_skip, grad_weight)


def solution(mesh):
    in_specs = (
        P(("grp", "row"), None, None),
        P(None, None, ("grp", "row"), None),
        P(None, None, ("grp", "row"), None),
        P(None, None, ("grp", "row"), None),
        P(),
        P(),
        P(("grp", "row"), None, None),
    )
    out_specs = (
        P(("grp", "row"), None, None),
        P(None, None, ("grp", "row"), None),
        P(None, None, ("grp", "row"), None),
        P(None, None, ("grp", "row"), None),
        P("grp"),
        P("grp", None),
    )
    body = functools.partial(local, mesh.shape["row"])
    return jax.shard_map(body, mesh=mesh, in_specs=in_specs, out_specs=out_specs, check_vma=False)
```

```python
import functools

import jax
import jax.numpy as jnp
from jax import lax
from jax.experimental import pallas as pl
from jax.experimental.pallas import tpu as pltpu
from jax.sharding import PartitionSpec as P

F32 = jnp.float32
BF16 = jnp.bfloat16
HI = lax.Precision.HIGHEST
LANES = 128
FAR = -1e30
VMEM_GRANT = 16 << 20


def iota(shape, dim):
    return lax.broadcasted_iota(jnp.int32, shape, dim)


def nt(a, b):
    return lax.dot_general(a, b, (((1,), (1,)), ((), ())), preferred_element_type=F32)


def nn(a, b):
    return jnp.dot(a, b, preferred_element_type=F32)


def tn(a, b):
    return lax.dot_general(a, b, (((0,), (0,)), ((), ())), preferred_element_type=F32)


def split_index(index, sizes):
    parts = []
    for size in reversed(sizes):
        if size & (size - 1) == 0:
            parts.append(index & (size - 1))
            index = index >> (size.bit_length() - 1)
        else:
            parts.append(lax.rem(index, size))
            index = lax.div(index, size)
    return parts[::-1]


class Slots:
    def __init__(self, heads, states):
        self.heads = heads
        self.states = states
        self.inputs = (0, states)
        self.reads = (2 * states, 3 * states)
        pad = -(-heads // 8) * 8
        self.pad = pad
        self.rates = (4 * states, 4 * states + pad)
        self.lows = (4 * states + 2 * pad, 4 * states + 3 * pad)
        self.used = 4 * states + 2 * pad


class Lines:
    def __init__(self, rows, rates, slots, lines, block):
        at_t, at_u = iota((block, block), 0), iota((block, block), 1)
        self.same = None
        if lines > 1:
            at_t, line_t = split_index(at_t, (block // lines, lines))
            at_u, line_u = split_index(at_u, (block // lines, lines))
            self.same = line_t == line_u
        self.below, self.above = at_t > at_u, at_t < at_u
        self.till = self.within(at_t <= at_u)
        self.since = self.within(at_t >= at_u)
        self.sums = (
            -jnp.dot(rates[0], self.till.astype(F32), precision=HI, preferred_element_type=F32),
            -jnp.dot(rates[1], self.since.astype(F32), precision=HI, preferred_element_type=F32),
        )
        self.columns = jnp.transpose(jnp.concatenate(self.sums, axis=0))
        self.inputs = [rows[at : at + slots.states].astype(BF16) for at in slots.inputs]
        self.reads = [rows[at : at + slots.states].astype(BF16) for at in slots.reads]
        down, up = (tn(self.reads[way], self.inputs[way]) for way in (0, 1))
        self.scores = jnp.where(self.below, down, jnp.where(self.above, up, down + up))
        self.pad = slots.pad

    def within(self, mask):
        return mask if self.same is None else mask & self.same

    def kernel(self, head):
        up = self.pad + head
        spread = jnp.where(
            self.below,
            self.columns[:, head : head + 1] - self.sums[0][head : head + 1],
            self.columns[:, up : up + 1] - self.sums[1][head : head + 1],
        )
        if self.same is not None:
            spread = jnp.where(self.same, spread, FAR)
        return jnp.exp(spread)


def head_mask(block, head_size, member):
    lane = iota((block, LANES), 1)
    return (lane >= member * head_size) & (lane < (member + 1) * head_size)


def scan_block(feats, grads, lines, slots, small_ref, row_slice, forward, backward):
    block = feats.shape[0]
    heads = slots.heads
    head_size = feats.shape[1] // heads
    per_group = LANES // head_size
    below = lines.below
    grad_scores = jnp.zeros((block, block), F32)
    out_parts, grad_parts = [], []
    lane_pad = iota((block, LANES), 1)
    row_sums = jnp.zeros((block, LANES), F32)
    row_at = iota((2 * slots.pad, block), 0)
    col_sums = jnp.zeros((2 * slots.pad, block), F32)
    for group in range(heads // per_group):
        span = slice(group * LANES, (group + 1) * LANES)
        feat_group = feats[:, span]
        grad_group = grads[:, span] if backward else None
        mixes, feat_own, grad_own = [], [], []
        for member in range(per_group):
            head = group * per_group + member
            up = slots.pad + head
            mine = head_mask(block, head_size, member)
            feat_head = jnp.where(mine, feat_group, jnp.zeros_like(feat_group))
            kernel = lines.kernel(head)
            mix = kernel * lines.scores
            mixes.append(mix.astype(BF16))
            feat_own.append(feat_head)
            if not backward:
                continue
            grad_own.append(jnp.where(mine, grad_group, jnp.zeros_like(grad_group)))
            grad_mix = nt(grad_group, feat_head)
            grad_scores = grad_scores + kernel * grad_mix
            flow = mix * grad_mix
            flow_down = jnp.where(below, flow, 0.0)
            row_down = jnp.sum(flow_down, axis=1, keepdims=True)
            row_all = jnp.sum(flow, axis=1, keepdims=True)
            col_down = jnp.sum(flow_down, axis=0, keepdims=True)
            col_all = jnp.sum(flow, axis=0, keepdims=True)
            row_sums = jnp.where(lane_pad == head, row_down, row_sums)
            row_sums = jnp.where(lane_pad == up, row_all - row_down, row_sums)
            col_sums = jnp.where(row_at == head, col_down, col_sums)
            col_sums = jnp.where(row_at == up, col_all - col_down, col_sums)
        if forward:
            out_parts.append(
                nn(jnp.concatenate(mixes, axis=1), jnp.concatenate(feat_own, axis=0))
            )
        if backward:
            grad_parts.append(
                tn(jnp.concatenate(mixes, axis=0), jnp.concatenate(grad_own, axis=0))
            )
    out = jnp.concatenate(out_parts, axis=1) if forward else None
    if not backward:
        return out, None
    change = col_sums - jnp.transpose(row_sums)[: 2 * slots.pad]
    reach = (lines.since, lines.till)
    for way in (0, 1):
        score_grad = jnp.where(reach[way], grad_scores, 0.0).astype(BF16)
        at = slots.inputs[way]
        small_ref[at : at + slots.states, row_slice] = nn(lines.reads[way], score_grad)
        at = slots.reads[way]
        small_ref[at : at + slots.states, row_slice] = nt(lines.inputs[way], score_grad)
        at = slots.rates[way]
        part = change[way * slots.pad : (way + 1) * slots.pad]
        small_ref[at : at + slots.pad, row_slice] = jnp.dot(
            part, reach[way].astype(F32), precision=HI, preferred_element_type=F32
        )
    return out, jnp.concatenate(grad_parts, axis=1)


def by_rank(array, ranks):
    narrow = array[0].shape[0] // ranks
    return [
        jnp.concatenate([row[rank * narrow : (rank + 1) * narrow] for row in array], axis=0)
        for rank in range(ranks)
    ]


def pack_kernel(slots, ranks, feat_ref, cot_ref, rate_ref, input_ref, read_ref, out_ref, rows_ref):
    tile_rows, columns, width = feat_ref.shape
    model = cot_ref.shape[2]
    group = tile_rows * columns // ranks
    rows_ref[...] = jnp.zeros_like(rows_ref)
    for way in (0, 1):
        for row in range(tile_rows):
            span = slice(row * columns, (row + 1) * columns)
            at = slots.inputs[way]
            rows_ref[at : at + slots.states, span] = input_ref[2 + way, :, row, :]
            at = slots.reads[way]
            rows_ref[at : at + slots.states, span] = read_ref[2 + way, :, row, :]
            at = slots.rates[way]
            rate = rate_ref[2 + way, :, row, :]
            rows_ref[at : at + slots.heads, span] = rate
            at = slots.lows[way]
            rows_ref[at : at + slots.heads, span] = rate - rate.astype(BF16).astype(F32)
    values = [
        (0, [feat_ref[row].astype(F32) for row in range(tile_rows)]),
        (width, [cot_ref[row].astype(F32) for row in range(tile_rows)]),
        (
            width + model,
            [
                jnp.transpose(rows_ref[:, row * columns : (row + 1) * columns])
                for row in range(tile_rows)
            ],
        ),
    ]
    for lane, array in values:
        for rank, piece in enumerate(by_rank(array, ranks)):
            out_ref[rank * group : (rank + 1) * group, lane : lane + piece.shape[1]] = (
                piece.astype(BF16)
            )


def rows_kernel(
    slots, chunk, tables, feat_ref, cot_ref, weight_ref, skip_ref, rate_ref, input_ref, read_ref,
    gx_ref, small_ref, part_ref, skip_out_ref, *refs,
):
    *table_refs, rows_ref = refs
    tables.fill(table_refs)
    tile_rows, columns, width = feat_ref.shape
    tokens = tile_rows * columns
    skip = skip_ref[...]
    rows_ref[...] = jnp.zeros_like(rows_ref)
    partial = jnp.zeros(part_ref.shape, F32)
    skip_part = jnp.zeros((1, width), F32)
    for row in range(tile_rows):
        feats, cots = feat_ref[row], cot_ref[row]
        grads = nt(cots, weight_ref[...]).astype(BF16)
        for way in (0, 1):
            at = slots.inputs[way]
            rows_ref[at : at + slots.states, :] = input_ref[way, :, row, :]
            at = slots.reads[way]
            rows_ref[at : at + slots.states, :] = read_ref[way, :, row, :]
            at = slots.rates[way]
            rows_ref[at : at + slots.heads, :] = rate_ref[way, :, row, :]
        rates = [rows_ref[at : at + slots.pad, :] for at in slots.rates]
        lines = Lines(rows_ref, rates, slots, 1, columns)
        outs, gx = scan_block(
            feats, grads, lines, slots, small_ref,
            slice(row * columns, (row + 1) * columns), True, True,
        )
        feat_f32, grad_f32 = feats.astype(F32), grads.astype(F32)
        across = (outs + skip * feat_f32).astype(BF16)
        partial = partial + tn(across, cots)
        gx_ref[row * columns : (row + 1) * columns, :] = gx + skip * grad_f32
        skip_part = skip_part + jnp.sum(feat_f32 * grad_f32, axis=0, keepdims=True)
    part_ref[...] = partial
    if chunk is None:
        skip_out_ref[...] = skip_part
    else:
        high = skip_part.astype(BF16).astype(F32)
        piece = width // chunk
        lane_of = iota((chunk, width), 1)
        start = iota((chunk, width), 0) * piece
        owned = (lane_of >= start) & (lane_of < start + piece)
        spread = jnp.concatenate(
            [jnp.where(owned, high, 0.0), jnp.where(owned, skip_part - high, 0.0)], axis=1
        ).astype(BF16)
        skip_out_ref[...] = nn(spread, skip_places(slots, width, piece))


def skip_places(slots, width, piece):
    at = iota((width, 1), 0)
    whole = ((at.astype(F32) + 0.5) * (1.0 / piece)).astype(jnp.int32)
    place = at - whole * piece + slots.used
    lane = iota((width, LANES), 1)
    high, low = place == lane, place + piece == lane
    return jnp.concatenate([high.astype(F32), low.astype(F32)], axis=0).astype(BF16)


def long_lines(params, slots, lines):
    rows = jnp.transpose(params.astype(F32))
    rates = [
        rows[hi : hi + slots.pad] + rows[lo : lo + slots.pad]
        for hi, lo in zip(slots.rates, slots.lows)
    ]
    return Lines(rows, rates, slots, lines, params.shape[0])


def halves_of(array):
    high = array.astype(BF16)
    return high, (array - high.astype(F32)).astype(BF16)


def reach_of(lines, block):
    at_t, line_t = split_index(iota((block, block), 0), (block // lines, lines))
    at_u, line_u = split_index(iota((block, block), 1), (block // lines, lines))
    same = line_t == line_u
    return same, (same & (at_t >= at_u), same & (at_t <= at_u))


class Tables:
    def __init__(self, slots, lines, tokens, width):
        self.slots, self.lines, self.tokens, self.width = slots, lines, tokens, width
        self.short = tokens // lines <= LONGEST_SHORT
        self.shapes = []
        self.kept = []
        if self.short:
            values = ((2, tokens, width), F32)
            self.kept = [
                ((2, tokens, 2 * LANES), BF16), ((2, tokens, width), BF16), values,
                ((2, tokens, tokens), BF16),
            ]
            self.shapes = [(tokens, tokens), (2 * LANES, 2 * width), (4 * width, LANES)]

    def fill(self, refs):
        if not self.short:
            return
        slots, width, tokens = self.slots, self.width, self.tokens
        size = width // slots.heads
        same, reach = reach_of(self.lines, tokens)
        half = jnp.where(same, 0.5, 0.0)
        refs[0][...] = (reach[0].astype(F32) - half).astype(BF16)
        for way in (0, 1):
            at = iota((LANES, width), 0)
            head = split_index(iota((LANES, width), 1), (slots.heads, size))[0]
            spread = (at == head + slots.rates[way]).astype(F32).astype(BF16)
            lanes = slice(way * width, (way + 1) * width)
            refs[1][:LANES, lanes] = spread
            refs[1][LANES:, lanes] = spread
            at = iota((width, LANES), 1)
            head = split_index(iota((width, LANES), 0), (slots.heads, size))[0]
            gather = (at == head + slots.rates[way]).astype(F32).astype(BF16)
            refs[2][2 * way * width : (2 * way + 1) * width, :] = gather
            refs[2][(2 * way + 1) * width : (2 * way + 2) * width, :] = gather


class ShortLines:
    def __init__(self, params, slots, lines, tables):
        self.slots, self.tables, self.params = slots, tables, params
        tokens = self.tokens = params.shape[0]
        self.reach = reach_of(lines, tokens)[1]
        self.lane = lane = iota((tokens, LANES), 1)
        self.up_lane = ((lane >= slots.rates[1]) & (lane < slots.lows[0])) | (
            lane >= slots.lows[1]
        )
        states = slots.states
        wide = params.astype(F32)
        turned = pltpu.roll(wide, LANES - slots.reads[0], 1)
        first, second = lane < states, (lane >= states) & (lane < 2 * states)
        self.inputs = [jnp.where(mask, wide, 0.0).astype(BF16) for mask in (first, second)]
        self.reads = [jnp.where(mask, turned, 0.0).astype(BF16) for mask in (first, second)]

    def factors(self, width, narrows):
        spread = self.tables[1][...]
        pairs = [nn(narrows[at], spread) for at in (0, 1)]
        return [(pair[:, :width], pair[:, width:]) for pair in pairs]

    def forward(self, feats, kept):
        slots, lane = self.slots, self.lane
        width = feats.shape[1]
        narrows, lost, mixed, scores = kept
        for way in (0, 1):
            score = nt(self.reads[way], self.params)
            scores[way] = jnp.where(self.reach[way], score, 0.0).astype(BF16)
        sums = nn(self.tables[0][...], self.params)
        sums = jnp.where(self.up_lane, self.params.astype(F32) - sums, sums)
        sums = sums + pltpu.roll(sums, LANES - (slots.lows[0] - slots.rates[0]), 1)
        rated = (lane >= slots.rates[0]) & (lane < slots.lows[0])
        sums = jnp.where(rated, sums, 0.0)
        for at, narrow in enumerate((jnp.exp(sums), jnp.exp(-sums))):
            narrows[at] = jnp.concatenate(halves_of(narrow), axis=1)
        losses, gains = self.factors(width, narrows)
        wide = feats.astype(F32)
        out = None
        for way in (0, 1):
            held = (wide * losses[way]).astype(BF16)
            lost[way] = held
            mix = nn(scores[way], held)
            mixed[way] = mix
            part = gains[way] * mix
            out = part if out is None else out + part
        return out

    def backward(self, grads, kept):
        slots = self.slots
        width = grads.shape[1]
        narrows, lost, mixed, scores = kept
        losses, gains = self.factors(width, narrows)
        wide = grads.astype(F32)
        gx = heads = read_grads = input_grads = 0.0
        for way in (0, 1):
            gained = (wide * gains[way]).astype(BF16)
            back = tn(scores[way], gained)
            gx = gx + losses[way] * back
            held = lost[way]
            score_grad = jnp.where(self.reach[way], nt(gained, held), 0.0).astype(BF16)
            change = held.astype(F32) * back - gained.astype(F32) * mixed[way]
            places = self.tables[2][2 * way * width : 2 * (way + 1) * width, :]
            heads = heads + nn(jnp.concatenate(halves_of(change), axis=1), places)
            read_grads = read_grads + nn(score_grad, self.inputs[way])
            input_grads = input_grads + tn(score_grad, self.reads[way])
        since, till = (mask.astype(F32).astype(BF16) for mask in self.reach)
        both = jnp.concatenate(halves_of(heads), axis=1)
        down, up = nn(till, both), nn(since, both)
        rates = jnp.where(
            self.up_lane, up[:, :LANES] + up[:, LANES:], down[:, :LANES] + down[:, LANES:]
        )
        smalls = input_grads + pltpu.roll(read_grads, slots.reads[0], 1)
        return gx, jnp.where(self.lane >= slots.rates[0], rates, smalls)


LONGEST_SHORT = 32


def forward_kernel(slots, lines, sizes, recv_ref, part_ref, *refs):
    tables, refs = refs[: len(sizes.shapes)], refs[len(sizes.shapes) :]
    mine_ref, other_ref, *kept = refs
    width, model = part_ref.shape
    tokens = recv_ref.shape[0]
    feats, cots = recv_ref[:, :width], recv_ref[:, width : width + model]
    params = recv_ref[:, width + model :]
    if sizes.short:
        down = ShortLines(params, slots, lines, tables).forward(feats, kept)
    else:
        masks = long_lines(params, slots, lines)
        down = scan_block(feats, None, masks, slots, None, None, True, False)[0]
    total = part_ref[...] + tn(down.astype(BF16), cots)
    even = lax.rem(lax.axis_index("row"), 2) == 0
    half = width // 2
    mine_ref[...] = jnp.where(even, total[:half], total[half:])
    other_ref[...] = jnp.where(even, total[half:], total[:half]).astype(BF16)


def backward_kernel(slots, ranks, lines, chunk, sizes, recv_ref, weight_ref, skip_ref, *refs):
    tables, refs = refs[: len(sizes.shapes)], refs[len(sizes.shapes) :]
    *kept, back_ref, small_ref = refs
    width, model = weight_ref.shape
    tokens = recv_ref.shape[0]
    feats = recv_ref[:, :width]
    params = recv_ref[:, width + model :]
    grads = nt(recv_ref[:, width : width + model], weight_ref[...]).astype(BF16)
    if sizes.short:
        gx, small = ShortLines(params, slots, lines, tables).backward(grads, kept)
    else:
        small_ref[...] = jnp.zeros_like(small_ref)
        masks = long_lines(params, slots, lines)
        span = slice(0, tokens)
        gx = scan_block(feats, grads, masks, slots, small_ref, span, False, True)[1]
        small = jnp.transpose(small_ref[...])
    back_ref[:, :width] = gx.astype(BF16)
    if chunk is not None:
        small = small + jnp.concatenate([skip_ref[...]] * ranks, axis=0)
    back_ref[:, width:] = small.astype(BF16)


def strip(array):
    return [array[:, at : at + LANES] for at in range(0, array.shape[1], LANES)]


class Tiles:
    def __init__(self, rows, model, ranks, group):
        self.unit = unit = 8
        steps = rows // unit
        self.places = [(at * unit, lane) for lane in range(0, model, LANES) for at in range(steps)]
        count = len(self.places)
        per = 2 * count // ranks
        self.split = 2 * count % ranks == 0 and per % 2 == 1 and ranks % 2 == 0 and group > 4
        self.per = per
        self.full = per // 2 if self.split else -(-count // ranks)
        self.starts = [count * rank // ranks for rank in range(ranks + 1)]
        self.moved = unit // 2 if self.split else 0
        self.size = unit * (self.full + self.split)

    def of(self, rank):
        if not self.split:
            return self.places[self.starts[rank] : self.starts[rank + 1]]
        first = self.per * (rank // 2) + (rank % 2) * (self.full + 1)
        return self.places[first : first + self.full]

    def shared(self, rank):
        return self.places[self.per * (rank // 2) + self.full]


def lay_out(out_ref, rank, pieces):
    at = 0
    for piece in pieces:
        out_ref[rank, at : at + piece.shape[0], :] = piece
        at += piece.shape[0]


def merge_kernel(ranks, early, mine_ref, theirs_ref, back_ref, out_ref):
    total = mine_ref[...] + theirs_ref[...].astype(F32)
    group = back_ref.shape[0] // ranks
    tiles = Tiles(*mine_ref.shape, ranks, group)
    unit = tiles.unit
    for rank in range(ranks):
        pieces = strip(back_ref[rank * group : (rank + 1) * group, :])
        blocks = [
            total[row : row + unit, lane : lane + LANES].astype(BF16)
            for row, lane in tiles.of(rank)
        ]
        blocks += [jnp.zeros((unit, LANES), BF16)] * (tiles.full - len(blocks))
        if tiles.split:
            row, lane = tiles.shared(rank)
            half = unit // 2
            row += (rank % 2) * half
            moved = pieces[-1].astype(F32)[group - tiles.moved :]
            blocks.append(
                jnp.concatenate([total[row : row + half, lane : lane + LANES], moved], axis=0)
                .astype(BF16)
            )
        lay_out(out_ref, rank, pieces[:early] + blocks)


def sum_kernel(early, recv_ref, back_ref, out_ref, tiles):
    ranks = out_ref.shape[0]
    group = back_ref.shape[0] // ranks
    unit = tiles.unit
    own = slice(recv_ref.shape[1] - tiles.size, recv_ref.shape[1])
    whole = tiles.full * unit
    for half in (0, 1):
        total = recv_ref[half, own, :].astype(F32)
        for rank in range(half + 2, ranks, 2):
            total = total + recv_ref[rank, own, :].astype(F32)
        for rank in range(half, ranks, 2):
            pieces = strip(back_ref[rank * group : (rank + 1) * group, :])
            small = pieces[-1]
            if tiles.split:
                small = jnp.concatenate(
                    [total[whole : whole + unit // 2], small.astype(F32)[: group - tiles.moved]],
                    axis=0,
                ).astype(BF16)
            lay_out(out_ref, rank, pieces[early:-1] + [total[:whole].astype(BF16), small])


def half_kernel(start, recv_ref, out_ref):
    out_ref[...] = recv_ref[:, start : start + out_ref.shape[1], :]


def widen_half(halves_ref, store, tiles):
    ranks = halves_ref.shape[0]
    unit = tiles.unit
    for rank in range(ranks):
        for step, (row, lane) in enumerate(tiles.of(rank)):
            store(row, lane, halves_ref[rank, step * unit : (step + 1) * unit, :].astype(F32))
    if tiles.split:
        at = tiles.full * unit
        for rank in range(0, ranks, 2):
            pair = [
                halves_ref[rank + side, at : at + unit, :].astype(F32)[: unit // 2]
                for side in (0, 1)
            ]
            store(*tiles.shared(rank), jnp.concatenate(pair, axis=0))


def weight_kernel(tiles, theirs_ref, weight_in, weight_out, wide_ref, done):
    rows, model = wide_ref.shape

    def store(row, lane, block):
        wide_ref[row : row + block.shape[0], lane : lane + LANES] = block

    widen_half(theirs_ref, store, tiles)
    half = lax.rem(lax.axis_index("row") + 1, 2)
    start = pl.multiple_of(half * rows, 8)
    copy = pltpu.make_async_copy(wide_ref, weight_out.at[pl.ds(start, rows), :], done)
    copy.start()
    copy.wait()


def finish_kernel(
    slots, ranks, chunk, early, tiles, early_ref, late_ref, gx_ref, small_ref, held_ref,
    weight_out, feat_out, rate_out, input_out, read_out, *skip_out,
):
    rows = weight_out.shape[0] // 2
    start = pl.multiple_of(lax.rem(lax.axis_index("row"), 2) * rows, 8)

    def store(row, lane, block):
        weight_out[pl.ds(start + row, block.shape[0]), lane : lane + LANES] = block

    widen_half(held_ref, store, tiles)
    tile_rows, columns, width = feat_out.shape
    narrow = columns // ranks
    group = tile_rows * narrow
    lanes = width // LANES

    def part_of(part):
        ref, part = (early_ref, part) if part < early else (late_ref, part - early)
        return ref[:, part * group : (part + 1) * group, :].astype(F32)

    def row_of(array, row):
        return jnp.concatenate(
            [array[rank, row * narrow : (row + 1) * narrow] for rank in range(ranks)], axis=0
        )

    for part in range(lanes):
        lane = slice(part * LANES, (part + 1) * LANES)
        back = part_of(part)
        for row in range(tile_rows):
            span = slice(row * columns, (row + 1) * columns)
            feat_out[row, :, lane] = (gx_ref[span, lane] + row_of(back, row)).astype(BF16)
    back = late_ref[:, late_ref.shape[1] - group :, :].astype(F32)
    if tiles.split:
        tail = early_ref[:, early_ref.shape[1] - tiles.unit :, :].astype(F32)
        back = jnp.concatenate([back[:, tiles.moved :], tail[:, tiles.unit - tiles.moved :]], axis=1)
    for row in range(tile_rows):
        span = slice(row * columns, (row + 1) * columns)
        held = jnp.transpose(row_of(back, row))
        for way in (0, 1):
            at = slots.inputs[way]
            input_out[way, :, row, :] = small_ref[at : at + slots.states, span]
            input_out[2 + way, :, row, :] = held[at : at + slots.states]
            at = slots.reads[way]
            read_out[way, :, row, :] = small_ref[at : at + slots.states, span]
            read_out[2 + way, :, row, :] = held[at : at + slots.states]
            at = slots.rates[way]
            rate_out[way, :, row, :] = small_ref[at : at + slots.heads, span]
            rate_out[2 + way, :, row, :] = held[at : at + slots.heads]
    if chunk is not None:
        piece = width // chunk
        gathered = jnp.sum(back, axis=0)
        places = skip_places(slots, width, piece)
        places = places[:width] + places[width:]
        high, low = halves_of(gathered)
        spread = nt(high, places) + nt(low, places)
        lane_of = iota((chunk, width), 1)
        start = iota((chunk, width), 0) * piece
        owned = (lane_of >= start) & (lane_of < start + piece)
        skip_out[0][...] = jnp.sum(jnp.where(owned, spread, 0.0), axis=0)


def call(
    kernel, name, out_shape, operands, scratch=(), flops=0, moved=0, grant=VMEM_GRANT,
    whole=(), aliases=None,
):
    def spec(side, at):
        return pl.BlockSpec(memory_space=pl.ANY if (side, at) in whole else pltpu.VMEM)

    many = isinstance(out_shape, tuple)
    outs = tuple(spec("out", at) for at in range(len(out_shape) if many else 1))
    return pl.pallas_call(
        kernel,
        name=name,
        out_shape=out_shape,
        in_specs=[spec("in", at) for at in range(len(operands))],
        out_specs=outs if many else outs[0],
        scratch_shapes=list(scratch),
        input_output_aliases=aliases or {},
        compiler_params=pltpu.CompilerParams(vmem_limit_bytes=grant),
        cost_estimate=pl.CostEstimate(flops=flops, bytes_accessed=moved, transcendentals=0),
    )(*operands)


def local(ranks, features, decay_rate, input_proj, read_proj, skip_gain, out_weight, out_cotangent):
    tile_rows, columns, width = features.shape
    model = out_cotangent.shape[2]
    heads, states = decay_rate.shape[1], input_proj.shape[1]
    slots = Slots(heads, states)
    tokens = tile_rows * columns
    chunk = tokens // ranks
    room = chunk * (LANES - slots.used)
    if chunk % 8 or width % chunk or 2 * width > room:
        chunk = None
    shape = jax.ShapeDtypeStruct

    def exchange(array):
        return lax.all_to_all(array, "row", split_axis=0, concat_axis=0, tiled=True)

    packed = call(
        functools.partial(pack_kernel, slots, ranks), "pack",
        shape((tokens, width + model + LANES), BF16),
        (features, out_cotangent, decay_rate, input_proj, read_proj),
        [pltpu.VMEM((LANES, tokens), F32)],
        flops=2 * tokens * tokens * (width + model), moved=4 * tokens * (width + model), grant=None,
    )
    received = exchange(packed)
    skip_shape = (1, width) if chunk is None else (chunk, LANES)
    lines = columns // ranks
    tables = Tables(slots, lines, tokens, width)
    gx_rows, small_rows, partial, skip_part, *table = call(
        functools.partial(rows_kernel, slots, chunk, tables), "rows",
        (
            shape((tokens, width), F32),
            shape((LANES, tokens), F32),
            shape((width, model), F32),
            shape(skip_shape, F32),
            *(shape(sizes, BF16) for sizes in tables.shapes),
        ),
        (
            features, out_cotangent, out_weight, skip_gain.reshape(1, width),
            decay_rate, input_proj, read_proj,
        ),
        [pltpu.VMEM((LANES, columns), F32)],
        flops=2 * tokens * width * (2 * model + 3 * columns), moved=8 * tokens * width,
    )
    half = width // 2
    partners = [(rank, rank ^ 1) for rank in range(ranks)]
    mine, other, *kept = call(
        functools.partial(forward_kernel, slots, lines, tables), "forward",
        (
            shape((half, model), F32),
            shape((half, model), BF16),
            *(shape(*leaf) for leaf in tables.kept),
        ),
        (received, partial, *table),
        flops=2 * tokens * width * (2 * model + columns), moved=8 * tokens * width,
    )
    theirs = lax.ppermute(other, "row", partners)
    back = call(
        functools.partial(backward_kernel, slots, ranks, lines, chunk, tables), "backward",
        shape((tokens, width + LANES), BF16), (received, out_weight, skip_part, *table, *kept),
        [pltpu.VMEM((LANES, tokens), F32)],
        flops=2 * tokens * width * (2 * model + 3 * columns), moved=8 * tokens * width,
    )
    group = tokens // ranks
    tiles = Tiles(half, model, ranks, group)
    strips = width // LANES + 1
    early = strips // 4
    merged = call(
        functools.partial(merge_kernel, ranks, early), "merge",
        shape((ranks, early * group + tiles.size, LANES), BF16), (mine, theirs, back),
        flops=width * model, moved=2 * width * model,
    )
    returned = exchange(merged)
    whole = tiles.full * tiles.unit
    late_rows = (strips - early) * group + whole
    summed = call(
        functools.partial(sum_kernel, early, tiles=tiles), "sum",
        shape((ranks, late_rows, LANES), BF16), (returned, back),
        flops=width * model, moved=2 * width * model,
    )
    last = exchange(summed)
    held = call(
        functools.partial(half_kernel, (strips - early - 1) * group), "half",
        shape((ranks, tiles.size, LANES), BF16), (last,),
        flops=width * model, moved=2 * width * model,
    )
    swapped = lax.ppermute(held, "row", partners)
    outs = [
        shape((width, model), F32),
        shape(features.shape, BF16),
        shape(decay_rate.shape, F32),
        shape(input_proj.shape, F32),
        shape(read_proj.shape, F32),
    ]
    if chunk is not None:
        outs.append(shape((width,), F32))
    done = call(
        functools.partial(finish_kernel, slots, ranks, chunk, early, tiles), "finish",
        tuple(outs), (returned, last, gx_rows, small_rows, held),
        flops=2 * tokens * tokens * width, moved=8 * tokens * width,
    )
    grad_weight = call(
        functools.partial(weight_kernel, tiles), "weight", shape((width, model), F32),
        (swapped, done[0]),
        [pltpu.VMEM((half, model), F32), pltpu.SemaphoreType.DMA(())],
        flops=width * model, moved=6 * width * model,
        whole=[("in", 1), ("out", 0)], aliases={1: 0},
    )
    if chunk is None:
        grad_skip = lax.psum(skip_part, "row").reshape(width)
    else:
        grad_skip = done[5]
    return (*done[1:5], grad_skip, grad_weight)


def solution(mesh):
    in_specs = (
        P(("grp", "row"), None, None),
        P(None, None, ("grp", "row"), None),
        P(None, None, ("grp", "row"), None),
        P(None, None, ("grp", "row"), None),
        P(),
        P(),
        P(("grp", "row"), None, None),
    )
    out_specs = (
        P(("grp", "row"), None, None),
        P(None, None, ("grp", "row"), None),
        P(None, None, ("grp", "row"), None),
        P(None, None, ("grp", "row"), None),
        P("grp"),
        P("grp", None),
    )
    body = functools.partial(local, mesh.shape["row"])
    return jax.shard_map(body, mesh=mesh, in_specs=in_specs, out_specs=out_specs, check_vma=False)
```
